512 devices in a mesh: ctx: 64 (over z, y), head: 8 (over x, core).
Axes of the slice: x: 4, y: 4, z: 16, core: 2. Of those that a mesh axis runs over, the one named last changes fastest.
Arguments:
- query: bfloat16 [65536, 1024], P(('ctx', 'head')), may hold values from -40 to 40
- key_in: bfloat16 [65536, 1024], P(('ctx', 'head')), may hold values from -9 to 9
- value_in: bfloat16 [65536, 1024], P(('ctx', 'head')), may hold values from -6 to 6
- grad_out: bfloat16 [65536, 1024], P(('ctx', 'head')), may hold values from -6 to 6
- random_blocks: int32 [1024, 8, 3], P('ctx', 'head'), may hold values from 0 to 1023, as said below
- universal_segment_indices: int32 [2], replicated, may hold values from 0 to 1023, as said below
Outputs:
- head_results: bfloat16 [65536, 1024], P('ctx', 'head')
- asker_derivative: bfloat16 [65536, 1024], P('ctx', 'head')
- grad_key: bfloat16 [65536, 1024], P('ctx', 'head')
- grad_value: bfloat16 [65536, 1024], P('ctx', 'head')
The draws below stay inside these ranges and needn't reach their ends.
Inputs may be any that keep to these rules, and one draw needn't show every extreme that they name: `random_blocks`: within one device's share of the lists (16 query blocks, 1 head) at most 2 entries name blocks of one index c of ctx (blocks c * 16 to c * 16 + 15), and in every share some index gets exactly 2. `universal_segment_indices`: the global blocks are different, and one of them is the last block 1023.
All inputs are finite; a program needn't handle non-finite values.
Results may differ from the reference program's by a relative error of at most 0.0075.
Values may be sent and summed in bfloat16 or wider, within the bound.
No kernel may reach another device: no remote copies, remote signals or barrier semaphores. Data moves between devices by JAX's collectives and lax.ppermute only.
A program may use at most 128 MiB of HBM per device.

```python
import functools
import jax
import jax.numpy as jnp
from jax import lax

HEADS = 8
FEATURE_LENGTH = 128
SPAN_TOKENS = 64
RANDOM = 3
WORLDWIDE_COUNT = 2
SEQ = 65536
NB = 1024
BLK_DEV = 16
HEAD_DEV = 1
CAP = 2


def paired_fields(key):
    width = HEADS * FEATURE_LENGTH
    key_field = 2.5 * jnp.clip(jax.random.normal(jax.random.fold_in(key, 21), (SEQ, width), jnp.float32), -3.6, 3.6)
    query_field = jnp.clip(jax.random.normal(jax.random.fold_in(key, 22), (SEQ, width), jnp.float32), -4.0, 4.0)
    return (query_field, key_field)


def draw_query(key, part):
    return paired_fields(key)[0].astype(jnp.bfloat16)


def draw_key_in(key, part):
    return paired_fields(key)[1].astype(jnp.bfloat16)


def draw_random_blocks(key, part):
    ctx_count = NB // BLK_DEV
    group_count = HEADS // HEAD_DEV
    per_device = BLK_DEV * HEAD_DEV * RANDOM
    pool_size = ctx_count * CAP

    def one_device(device_key):
        levels = jax.random.randint(jax.random.fold_in(device_key, 1), (ctx_count,), 0, 3)
        forced = jax.random.randint(jax.random.fold_in(device_key, 2), (), 0, ctx_count)
        levels = jnp.where(jnp.arange(ctx_count, dtype=jnp.int32) == forced, 3, levels)
        noise = jax.random.randint(jax.random.fold_in(device_key, 3), (pool_size,), 0, 1024)
        slot_ids = jnp.arange(pool_size, dtype=jnp.int32)
        owner_of = slot_ids // CAP
        ranking = (levels[owner_of] * 1024 + noise) * pool_size + slot_ids
        unused, picked = lax.top_k(ranking, per_device)
        owners = jax.random.permutation(jax.random.fold_in(device_key, 4), picked // CAP)
        local_ids = jax.random.randint(jax.random.fold_in(device_key, 5), (per_device,), 0, BLK_DEV)
        return (owners * BLK_DEV + local_ids).astype(jnp.int32).reshape(BLK_DEV, HEAD_DEV, RANDOM)
    device_keys = jax.random.split(key, ctx_count * group_count)
    lists = jax.vmap(one_device)(device_keys).reshape(ctx_count, group_count, BLK_DEV, HEAD_DEV, RANDOM)
    return lists.transpose(0, 2, 1, 3, 4).reshape(NB, HEADS, RANDOM)


def draw_universal_segment_indices(key, part):
    other_id = jax.random.randint(jax.random.fold_in(key, 31), (), 0, NB - 1)
    flipped = jax.random.randint(jax.random.fold_in(key, 32), (), 0, 2)
    last_id = jnp.full((), NB - 1, jnp.int32)
    first = jnp.where(flipped == 0, other_id, last_id)
    second = jnp.where(flipped == 0, last_id, other_id)
    return jnp.stack([first, second]).astype(jnp.int32)


def shard_levels(rng, extent, shards, smallest, top_value):
    def one(position, blocks):
        heights = jax.random.uniform(jax.random.fold_in(jax.random.fold_in(rng, 6), position), (blocks,), jnp.float32, smallest / len(shards), top_value / len(shards))
        return jnp.repeat(jnp.exp(heights), extent[position] // blocks).reshape((-1,) + (1,) * (len(extent) - position - 1))

    factor_of = one(*shards[0])
    for cut in shards[1:]:
        factor_of = factor_of * one(*cut)
    return factor_of


def normal_values(rng, dims, scale, limit, pieces=(), kind=jnp.bfloat16):
    entries = jax.random.normal(rng, dims, jnp.float32) * scale
    if len(pieces) > 0:
        entries = shard_levels(rng, dims, pieces, -0.22, 0.18) * entries
    return jnp.clip(entries, min=-limit, max=limit).astype(kind)


def setup_inputs(seed: int = 0) -> dict:
    arg_keys = jax.random.split(jax.random.key(seed), 7)
    return {
        "query": draw_query(jax.random.fold_in(arg_keys[6], 71), 0),
        "key_in": draw_key_in(jax.random.fold_in(arg_keys[6], 71), 0),
        "value_in": normal_values(arg_keys[2], (SEQ, HEADS * FEATURE_LENGTH), 1.0, 6.0, ((0, 512),)),
        "grad_out": normal_values(arg_keys[3], (SEQ, HEADS * FEATURE_LENGTH), 1.0, 6.0, ((0, 512),)),
        "random_blocks": draw_random_blocks(jax.random.fold_in(arg_keys[6], 71), 0),
        "universal_segment_indices": draw_universal_segment_indices(jax.random.fold_in(arg_keys[6], 71), 0),
    }


def cast_down_and_back(values):
    return lax.optimization_barrier(values.astype(jnp.bfloat16)).astype(jnp.float32)


def list_masks(listed, block_total):
    inside = (listed >= 0) & (listed < block_total)
    kept = []
    for slot_pos in range(listed.shape[-1]):
        seen = jnp.zeros(listed.shape[:-1], dtype=jnp.bool_)
        for prior_pos in range(slot_pos):
            seen = seen | (inside[..., prior_pos] & (listed[..., prior_pos] == listed[..., slot_pos]))
        kept.append(inside[..., slot_pos] & jnp.logical_not(seen))
    return jnp.stack(kept, -1)


def one_head(inputs, universal_segment_indices):
    query_h, key_h, value_h, dout_h, listed, kept = inputs
    inverse_root_dimension = FEATURE_LENGTH ** -0.5
    q_blocks = query_h.reshape(NB, SPAN_TOKENS, FEATURE_LENGTH)
    k_blocks = key_h.reshape(NB, SPAN_TOKENS, FEATURE_LENGTH)
    v_blocks = value_h.reshape(NB, SPAN_TOKENS, FEATURE_LENGTH)
    dout_blocks = dout_h.reshape(NB, SPAN_TOKENS, FEATURE_LENGTH)
    safe_ids = jnp.clip(listed, 0, NB - 1).astype(jnp.int32)
    collected_lookup_segments = k_blocks[safe_ids].astype(jnp.float32)
    collected_content_segments = v_blocks[safe_ids].astype(jnp.float32)
    asker_float_copy = q_blocks.astype(jnp.float32)
    raw_affinities = jnp.einsum('zeb,zpab->zepa', asker_float_copy, collected_lookup_segments) * inverse_root_dimension
    live = kept[:, None, :, None]
    row_max = jnp.max(jnp.where(live, raw_affinities, -jnp.inf), axis=(2, 3), keepdims=True)
    normalized_affinities = jnp.where(live, jnp.exp(raw_affinities - row_max), 0.0)
    normalizer_totals = jnp.sum(normalized_affinities, axis=(2, 3))
    sparse_mixture = (jnp.einsum('dknf,dnft->dkt', cast_down_and_back(normalized_affinities), collected_content_segments) / normalizer_totals[..., None]).astype(jnp.bfloat16)

    global_q = q_blocks[universal_segment_indices].reshape(WORLDWIDE_COUNT * SPAN_TOKENS, FEATURE_LENGTH)
    global_scores = jnp.dot(global_q, key_h.T, preferred_element_type=jnp.float32) * inverse_root_dimension
    global_max = jnp.max(global_scores, axis=1, keepdims=True)
    global_weights = jnp.exp(global_scores - global_max)
    global_total = jnp.sum(global_weights, axis=1, keepdims=True)
    universal_mixture = (jnp.dot(global_weights.astype(jnp.bfloat16), value_h, preferred_element_type=jnp.float32) / global_total).astype(jnp.bfloat16)
    head_results = sparse_mixture.at[universal_segment_indices].set(universal_mixture.reshape(WORLDWIDE_COUNT, SPAN_TOKENS, FEATURE_LENGTH))

    is_global = jnp.zeros((NB,), dtype=jnp.bool_).at[universal_segment_indices].set(True)
    filtered_upstream = jnp.where(is_global[:, None, None], jnp.zeros((), jnp.bfloat16), dout_blocks)
    upstream_float_copy = filtered_upstream.astype(jnp.float32)
    rowwise_correction = jnp.sum(upstream_float_copy * sparse_mixture.astype(jnp.float32), axis=-1)
    probabilities = normalized_affinities / normalizer_totals[:, :, None, None]
    affinity_derivative = jnp.einsum('zeb,zpab->zepa', upstream_float_copy, collected_content_segments)
    raw_affinity_derivative = cast_down_and_back(probabilities * (affinity_derivative - rowwise_correction[:, :, None, None]))
    sparse_asker_derivative = jnp.einsum('dknf,dnft->dkt', raw_affinity_derivative, collected_lookup_segments) * inverse_root_dimension
    key_gradient_parts = jnp.einsum('hmtu,hme->htue', raw_affinity_derivative, asker_float_copy) * inverse_root_dimension
    value_gradient_parts = jnp.einsum('hmtu,hme->htue', cast_down_and_back(probabilities), upstream_float_copy)
    key_gradient_parts = key_gradient_parts.at[:, 3:3 + RANDOM].set(cast_down_and_back(key_gradient_parts[:, 3:3 + RANDOM]))
    value_gradient_parts = value_gradient_parts.at[:, 3:3 + RANDOM].set(cast_down_and_back(value_gradient_parts[:, 3:3 + RANDOM]))
    grad_key = jnp.zeros((NB, SPAN_TOKENS, FEATURE_LENGTH), jnp.float32).at[safe_ids].add(key_gradient_parts)
    grad_value = jnp.zeros((NB, SPAN_TOKENS, FEATURE_LENGTH), jnp.float32).at[safe_ids].add(value_gradient_parts)

    global_dout = dout_blocks[universal_segment_indices].reshape(WORLDWIDE_COUNT * SPAN_TOKENS, FEATURE_LENGTH)
    global_delta = jnp.sum(global_dout.astype(jnp.float32) * universal_mixture.astype(jnp.float32), axis=-1, keepdims=True)
    global_prob = global_weights / global_total
    global_dprob = jnp.dot(global_dout, value_h.T, preferred_element_type=jnp.float32)
    global_dscore = (global_prob * (global_dprob - global_delta)).astype(jnp.bfloat16)
    grad_key = grad_key.reshape(SEQ, FEATURE_LENGTH) + jnp.dot(global_dscore.T, global_q, preferred_element_type=jnp.float32) * inverse_root_dimension
    grad_value = grad_value.reshape(SEQ, FEATURE_LENGTH) + jnp.dot(global_prob.astype(jnp.bfloat16).T, global_dout, preferred_element_type=jnp.float32)
    universal_asker_derivative = jnp.dot(global_dscore, key_h, preferred_element_type=jnp.float32) * inverse_root_dimension
    asker_derivative = sparse_asker_derivative.at[universal_segment_indices].set(universal_asker_derivative.reshape(WORLDWIDE_COUNT, SPAN_TOKENS, FEATURE_LENGTH))
    return (head_results.reshape(SEQ, FEATURE_LENGTH), asker_derivative.reshape(SEQ, FEATURE_LENGTH).astype(jnp.bfloat16),
            grad_key.astype(jnp.bfloat16), grad_value.astype(jnp.bfloat16))


def reference(query, key_in, value_in, grad_out, random_blocks, universal_segment_indices):
    def split_heads(matrix):
        return matrix.reshape(SEQ, HEADS, FEATURE_LENGTH).transpose(1, 0, 2)

    def join_heads(matrix):
        return matrix.transpose(1, 0, 2).reshape(SEQ, HEADS * FEATURE_LENGTH)

    block_ids = jnp.arange(NB, dtype=jnp.int32)
    window_ids = jnp.stack([block_ids - 1, block_ids, block_ids + 1], 1)
    window_ids = jnp.broadcast_to(window_ids[:, None, :], (NB, HEADS, 3))
    global_cols = jnp.broadcast_to(universal_segment_indices[None, None, :], (NB, HEADS, WORLDWIDE_COUNT))
    listed = jnp.concatenate([window_ids, random_blocks, global_cols], 2).astype(jnp.int32)
    kept = list_masks(listed, NB)
    results = lax.map(functools.partial(one_head, universal_segment_indices=universal_segment_indices),
                      (split_heads(query), split_heads(key_in), split_heads(value_in), split_heads(grad_out),
                       listed.transpose(1, 0, 2), kept.transpose(1, 0, 2)))
    return (join_heads(results[0]), join_heads(results[1]), join_heads(results[2]), join_heads(results[3]))
```

```python
import functools

import jax
import jax.numpy as jnp
from jax import lax
from jax.experimental import pallas as pl
from jax.experimental.pallas import tpu as pltpu
from jax.sharding import Mesh
from jax.sharding import PartitionSpec as P

FEATURE_LENGTH = 128
SPAN_TOKENS = 64
RANDOM = 3
WORLDWIDE_COUNT = 2
Z_AXIS = "ctx_0"
Y_AXIS = "ctx_1"
CTX = (Z_AXIS, Y_AXIS)
CTX_HEAD = (Z_AXIS, Y_AXIS, "head")
NEG = -1e30
SCALE = FEATURE_LENGTH ** (-0.5)
UNROLL = 4
SLOTS = 1 + RANDOM
D = FEATURE_LENGTH
S = SPAN_TOKENS
G = WORLDWIDE_COUNT * SPAN_TOKENS
VMEM = pl.BlockSpec(memory_space=pltpu.VMEM)
SMEM = pl.BlockSpec(memory_space=pltpu.SMEM)
PARAMS = pltpu.CompilerParams(vmem_limit_bytes=56 * 2**20)


def dot_nt(a, b):
    return lax.dot_general(a, b, (((1,), (1,)), ((), ())), preferred_element_type=jnp.float32)


def dot_nn(a, b):
    return lax.dot_general(a, b, (((1,), (0,)), ((), ())), preferred_element_type=jnp.float32)


def dot_tn(a, b):
    return lax.dot_general(a, b, (((0,), (0,)), ((), ())), preferred_element_type=jnp.float32)


def list_masks(listed, block_total):
    inside = (listed >= 0) & (listed < block_total)
    kept = []
    for slot_pos in range(listed.shape[-1]):
        seen = jnp.zeros(listed.shape[:-1], dtype=jnp.bool_)
        for prior_pos in range(slot_pos):
            seen = seen | inside[..., prior_pos] & (listed[..., prior_pos] == listed[..., slot_pos])
        kept.append(inside[..., slot_pos] & jnp.logical_not(seen))
    return jnp.stack(kept, -1)


def exchange(array, axes):
    return lax.all_to_all(array, axes, split_axis=0, concat_axis=0, tiled=True)


def to_all(array, axes):
    count = lax.axis_size(axes)
    return exchange(jnp.broadcast_to(array[None], (count,) + array.shape), axes)


def by_head(first, second):
    rows = first.shape[0]
    heads = first.shape[1] // D
    both = jnp.concatenate([first.reshape(rows, heads, D), second.reshape(rows, heads, D)], 2)
    return exchange(both.transpose(1, 0, 2), "head").reshape(heads * rows, 2 * D)


def merge(parts):
    top = functools.reduce(jnp.maximum, [part[0] for part in parts])
    factors = [jnp.exp(part[0] - top) for part in parts]
    total = sum(part[1] * factor for part, factor in zip(parts, factors))
    slope = sum(part[2] * factor for part, factor in zip(parts, factors))
    return top, total, slope


def column_stats(scores, slopes):
    top = jnp.max(scores, axis=0, keepdims=True)
    weights = jnp.exp(scores - top)
    return (
        top,
        jnp.sum(weights, axis=0, keepdims=True),
        jnp.sum(weights * slopes, axis=0, keepdims=True),
    )


def own_scores(i, blocks, qd_ref, kv_ref, shared_ref, bias_ref):
    low = max(i - 1, 0) * S
    high = min(i + 2, blocks) * S
    q = qd_ref[i * S : (i + 1) * S, :D]
    dout = qd_ref[i * S : (i + 1) * S, D:]
    scores = dot_nt(kv_ref[low:high, :D], q) * SCALE
    slopes = dot_nt(kv_ref[low:high, D:], dout)
    global_scores = dot_nt(shared_ref[:, 2 * D : 3 * D], q) * SCALE
    global_scores = jnp.concatenate(
        [
            global_scores[g * S : (g + 1) * S] + bias_ref[i * WORLDWIDE_COUNT + g]
            for g in range(WORLDWIDE_COUNT)
        ],
        0,
    )
    global_slopes = dot_nt(shared_ref[:, 3 * D :], dout)
    return low, high, q, dout, scores, slopes, global_scores, global_slopes


def own_stats_kernel(bias_ref, qd_ref, kv_ref, shared_ref, own_ref, rows_ref):
    tokens = qd_ref.shape[0]
    blocks = tokens // S
    for i in range(blocks):
        _, _, _, _, scores, slopes, global_scores, global_slopes = own_scores(
            i, blocks, qd_ref, kv_ref, shared_ref, bias_ref
        )
        top, total, slope = merge(
            [column_stats(scores, slopes), column_stats(global_scores, global_slopes)]
        )
        own_ref[0, i : i + 1, :] = top
        own_ref[1, i : i + 1, :] = total
        own_ref[2, i : i + 1, :] = slope
    parts = []
    for low in range(0, tokens, G):
        scores = dot_nt(kv_ref[low : low + G, :D], shared_ref[:, :D]) * SCALE
        slopes = dot_nt(kv_ref[low : low + G, D:], shared_ref[:, D : 2 * D])
        parts.append(column_stats(scores, slopes))
    top, total, slope = merge(parts)
    rows_ref[0:1, :] = top
    rows_ref[1:2, :] = total
    rows_ref[2:3, :] = slope


def edge_stats_kernel(
    meta_ref, slot_ref, item_ref, cell_ref, qd_ref, kv_ref, own_ref, out_ref, top_ref, total_ref, slope_ref
):
    group = qd_ref.shape[0] // S
    blocks = own_ref.shape[1]
    top_ref[...] = jnp.full(top_ref.shape, NEG, jnp.float32)
    total_ref[...] = jnp.zeros(total_ref.shape, jnp.float32)
    slope_ref[...] = jnp.zeros(slope_ref.shape, jnp.float32)

    def step(t, carry):
        found = []
        for u in range(UNROLL):
            pos = t * UNROLL + u
            cell = pl.multiple_of(cell_ref[pos] * S, S)
            item = pl.multiple_of(item_ref[pos] * S, S)
            scores = dot_nt(kv_ref[pl.ds(cell, S), :D], qd_ref[pl.ds(item, S), :D]) * SCALE
            slopes = dot_nt(kv_ref[pl.ds(cell, S), D:], qd_ref[pl.ds(item, S), D:])
            found.append((slot_ref[pos], column_stats(scores, slopes)))
        for slot, (top, total, slope) in found:
            top_ref[pl.ds(slot, 1), :] = top
            total_ref[pl.ds(slot, 1), :] = total
            slope_ref[pl.ds(slot, 1), :] = slope
        return carry

    lax.fori_loop(0, meta_ref[0], step, 0)
    mine = pl.multiple_of(SLOTS * group + meta_ref[1] * blocks, 8)
    top_ref[pl.ds(mine, blocks), :] = own_ref[0]
    total_ref[pl.ds(mine, blocks), :] = own_ref[1]
    slope_ref[pl.ds(mine, blocks), :] = own_ref[2]
    top, total, slope = merge(
        [
            (
                top_ref[s * group : (s + 1) * group, :],
                total_ref[s * group : (s + 1) * group, :],
                slope_ref[s * group : (s + 1) * group, :],
            )
            for s in range(SLOTS + 1)
        ]
    )
    out_ref[0] = top
    out_ref[1] = total
    out_ref[2] = slope


def edge_grads_kernel(
    meta_ref, slot_ref, item_ref, cell_ref, qd_ref, kv_ref, parts_ref, table_ref, partial_ref, final_ref
):
    group = qd_ref.shape[0] // S
    lanes = parts_ref.shape[0]
    top, total, slope = merge(
        [(parts_ref[lane, 0], parts_ref[lane, 1], parts_ref[lane, 2]) for lane in range(lanes)]
    )
    inverse = 1.0 / total
    final_ref[0] = top
    final_ref[1] = inverse
    final_ref[2] = slope * inverse
    table_ref[...] = jnp.zeros(table_ref.shape, jnp.bfloat16)
    partial_ref[...] = jnp.zeros(partial_ref.shape, jnp.float32)

    def step(t, carry):
        found = []
        for u in range(UNROLL):
            pos = t * UNROLL + u
            live = slot_ref[pos] < SLOTS * group
            item_pos = item_ref[pos]
            cell = pl.multiple_of(cell_ref[pos] * S, S)
            item = pl.multiple_of(item_pos * S, S)
            key = kv_ref[pl.ds(cell, S), :D]
            value = kv_ref[pl.ds(cell, S), D:]
            q = qd_ref[pl.ds(item, S), :D]
            dout = qd_ref[pl.ds(item, S), D:]
            scores = dot_nt(key, q) * SCALE
            slopes = dot_nt(value, dout)
            prob = jnp.exp(scores - final_ref[0, pl.ds(item_pos, 1), :])
            prob = prob * final_ref[1, pl.ds(item_pos, 1), :]
            prob = jnp.where(live, prob, 0.0)
            dscore = prob * ((slopes - final_ref[2, pl.ds(item_pos, 1), :]) * SCALE)
            prob = prob.astype(jnp.bfloat16)
            dscore = dscore.astype(jnp.bfloat16)
            found.append(
                (
                    cell,
                    item,
                    dot_nn(dscore, q),
                    dot_nn(prob, dout),
                    dot_tn(prob, value),
                    dot_tn(dscore, key),
                )
            )
        for cell, item, dkey, dvalue, mixed, dq in found:
            at = pl.ds(cell, S)
            table_ref[at, :D] = (table_ref[at, :D].astype(jnp.float32) + dkey).astype(jnp.bfloat16)
            table_ref[at, D:] = (table_ref[at, D:].astype(jnp.float32) + dvalue).astype(jnp.bfloat16)
            at = pl.ds(item, S)
            partial_ref[at, :D] += mixed
            partial_ref[at, D:] += dq
        return carry

    lax.fori_loop(0, meta_ref[0], step, 0)


def own_grads_kernel(
    meta_ref, bias_ref, flag_ref, qd_ref, kv_ref, shared_ref, final_ref, rows_ref, pairs_ref, mixed_ref, shared_grad_ref
):
    tokens = qd_ref.shape[0]
    blocks = tokens // S
    first = meta_ref[1] * blocks
    rows = rows_ref[...]
    row_top = jnp.max(rows[:, 0:1, :], axis=0)
    factors = jnp.exp(rows[:, 0:1, :] - row_top[None])
    sums = jnp.sum(rows * factors, axis=0)
    row_inverse = 1.0 / sums[1:2]
    row_slope = sums[2:3] * row_inverse
    q = shared_ref[:, :D]
    dout = shared_ref[:, D : 2 * D]
    mixed = jnp.zeros((G, D), jnp.float32)
    dq = jnp.zeros((G, D), jnp.float32)
    for low in range(0, tokens, G):
        key = kv_ref[low : low + G, :D]
        value = kv_ref[low : low + G, D:]
        scores = dot_nt(key, q) * SCALE
        slopes = dot_nt(value, dout)
        prob = jnp.exp(scores - row_top) * row_inverse
        dscore = (prob * ((slopes - row_slope) * SCALE)).astype(jnp.bfloat16)
        prob = prob.astype(jnp.bfloat16)
        pairs_ref[low : low + G, :D] = dot_nn(dscore, q)
        pairs_ref[low : low + G, D:] = dot_nn(prob, dout)
        mixed = mixed + dot_tn(prob, value)
        dq = dq + dot_tn(dscore, key)
    shared_grad_ref[G:, :D] = mixed
    shared_grad_ref[G:, D:] = dq
    global_dkey = jnp.zeros((G, D), jnp.float32)
    global_dvalue = jnp.zeros((G, D), jnp.float32)
    for i in range(blocks):
        low, high, q, dout, scores, slopes, global_scores, global_slopes = own_scores(
            i, blocks, qd_ref, kv_ref, shared_ref, bias_ref
        )
        top = final_ref[0, pl.ds(first + i, 1), :]
        inverse = final_ref[1, pl.ds(first + i, 1), :] * flag_ref[i]
        slope = final_ref[2, pl.ds(first + i, 1), :]

        def both(scores, slopes):
            prob = jnp.exp(scores - top) * inverse
            dscore = (prob * ((slopes - slope) * SCALE)).astype(jnp.bfloat16)
            return prob.astype(jnp.bfloat16), dscore

        prob, dscore = both(scores, slopes)
        global_prob, global_dscore = both(global_scores, global_slopes)
        pairs_ref[low:high, :D] += dot_nn(dscore, q)
        pairs_ref[low:high, D:] += dot_nn(prob, dout)
        global_dkey = global_dkey + dot_nn(global_dscore, q)
        global_dvalue = global_dvalue + dot_nn(global_prob, dout)
        mixed_ref[i * S : (i + 1) * S, :D] = dot_tn(prob, kv_ref[low:high, D:]) + dot_tn(
            global_prob, shared_ref[:, 3 * D :]
        )
        mixed_ref[i * S : (i + 1) * S, D:] = dot_tn(dscore, kv_ref[low:high, :D]) + dot_tn(
            global_dscore, shared_ref[:, 2 * D : 3 * D]
        )
    shared_grad_ref[:G, :D] = global_dkey
    shared_grad_ref[:G, D:] = global_dvalue


def body(query, key_in, value_in, grad_out, random_blocks, universal_segment_indices):
    f32 = jnp.float32
    z_count = lax.axis_size(Z_AXIS)
    y_count = lax.axis_size(Y_AXIS)
    ctx_count = z_count * y_count
    z_place = lax.axis_index(Z_AXIS)
    y_place = lax.axis_index(Y_AXIS)
    ctx_place = z_place * y_count + y_place

    kv = by_head(key_in, value_in)
    query, grad_out, random_blocks, kv = lax.optimization_barrier(
        (query, grad_out, random_blocks, kv)
    )
    kv_all = lax.all_gather(kv, Z_AXIS, axis=0, tiled=True)
    qd = by_head(query, grad_out)
    tokens = qd.shape[0]
    block_count = tokens // S
    group = block_count * y_count
    block_total = ctx_count * block_count
    cells = z_count * block_count

    owners = universal_segment_indices // block_count
    starts = universal_segment_indices % block_count * S
    pieces = []
    for g in range(WORLDWIDE_COUNT):
        pieces.append(
            jnp.concatenate(
                [lax.dynamic_slice_in_dim(part, starts[g], S, 0) for part in (qd, kv)], 1
            )
        )
    chunk = G // ctx_count
    sent = jnp.concatenate(pieces, 0).reshape(ctx_count, chunk, 4 * D)
    arrived = exchange(sent, CTX)
    owner = owners[(ctx_place * chunk) // S]
    picked = lax.dynamic_slice_in_dim(arrived, owner, 1, 0)[0]
    shared = to_all(picked, CTX).reshape(G, 4 * D)

    qd_group = to_all(qd, Y_AXIS).reshape(group * S, 2 * D)
    random_group = to_all(random_blocks[:, 0, :], Y_AXIS).reshape(group, RANDOM)

    ids = z_place * group + jnp.arange(group, dtype=jnp.int32)
    local = jnp.arange(group, dtype=jnp.int32) % block_count
    globals_ = jnp.broadcast_to(universal_segment_indices[None], (group, WORLDWIDE_COUNT))
    listed = jnp.concatenate(
        [jnp.stack([ids - 1, ids, ids + 1], 1), random_group, globals_], 1
    )
    kept = list_masks(listed, block_total)
    is_global = jnp.any(ids[:, None] == universal_segment_indices[None], 1)
    border = jnp.where(local == 0, ids - 1, jnp.where(local == block_count - 1, ids + 1, -1))
    named = jnp.concatenate([border[:, None], random_group], 1)
    valid = jnp.concatenate(
        [((border >= 0) & (border < block_total))[:, None], kept[:, 3 : 3 + RANDOM]], 1
    )
    lane = named // block_count % y_count
    valid = valid & jnp.logical_not(is_global)[:, None] & (lane == y_place)
    cell = named // group * block_count + named % block_count
    valid = valid.T.reshape(-1)
    cell = cell.T.reshape(-1)
    entries = SLOTS * group
    order = jnp.arange(entries, dtype=jnp.int32)
    rank = jnp.cumsum(valid.astype(jnp.int32)) - 1
    edge_count = rank[-1] + 1
    hit = (rank[None, :] == order[:, None]) & valid[None, :]
    slot_list = jnp.sum(jnp.where(hit, order[None, :], 0), 1)
    cell_list = jnp.sum(jnp.where(hit, cell[None, :], 0), 1)
    slot_list = jnp.where(order < edge_count, slot_list, entries + group)
    item_list = jnp.where(order < edge_count, slot_list % group, 0)
    meta = jnp.stack([(edge_count + UNROLL - 1) // UNROLL, y_place]).astype(jnp.int32)
    lists = (meta, slot_list, item_list, cell_list)

    own_first = y_place * block_count
    own_kept = lax.dynamic_slice_in_dim(kept, own_first, block_count, 0)
    bias = jnp.where(own_kept[:, 3 + RANDOM :], 0.0, NEG).astype(f32).reshape(-1)
    own_ids = ctx_place * block_count + jnp.arange(block_count, dtype=jnp.int32)
    hits = own_ids[:, None] == universal_segment_indices[None]
    flags = jnp.where(jnp.any(hits, 1), 0.0, 1.0).astype(f32)

    own, rows = pl.pallas_call(
        own_stats_kernel,
        out_shape=(
            jax.ShapeDtypeStruct((3, block_count, S), f32),
            jax.ShapeDtypeStruct((3, G), f32),
        ),
        in_specs=[SMEM, VMEM, VMEM, VMEM],
        out_specs=(VMEM, VMEM),
        compiler_params=PARAMS,
        name="own_stats",
    )(bias, qd, kv, shared)
    rows_all = to_all(rows, CTX)

    stat_rows = (SLOTS + 1) * group + 8
    stats = pl.pallas_call(
        edge_stats_kernel,
        out_shape=jax.ShapeDtypeStruct((3, group, S), f32),
        in_specs=[SMEM] * 4 + [VMEM] * 3,
        out_specs=VMEM,
        scratch_shapes=[pltpu.VMEM((stat_rows, S), f32)] * 3,
        compiler_params=PARAMS,
        name="edge_stats",
    )(*lists, qd_group, kv_all, own)
    parts = to_all(stats, Y_AXIS)

    table, partial, final = pl.pallas_call(
        edge_grads_kernel,
        out_shape=(
            jax.ShapeDtypeStruct((cells * S, 2 * D), jnp.bfloat16),
            jax.ShapeDtypeStruct((group * S, 2 * D), f32),
            jax.ShapeDtypeStruct((3, group, S), f32),
        ),
        in_specs=[SMEM] * 4 + [VMEM] * 3,
        out_specs=(VMEM, VMEM, VMEM),
        compiler_params=PARAMS,
        name="edge_grads",
    )(*lists, qd_group, kv_all, parts)
    returned = lax.psum_scatter(table, Z_AXIS, scatter_dimension=0, tiled=True)

    pairs, mixed, shared_grads = pl.pallas_call(
        own_grads_kernel,
        out_shape=(
            jax.ShapeDtypeStruct((tokens, 2 * D), f32),
            jax.ShapeDtypeStruct((tokens, 2 * D), f32),
            jax.ShapeDtypeStruct((2 * G, 2 * D), f32),
        ),
        in_specs=[SMEM] * 3 + [VMEM] * 5,
        out_specs=(VMEM, VMEM, VMEM),
        compiler_params=PARAMS,
        name="own_grads",
    )(meta, bias, flags, qd, kv, shared, final, rows_all)

    spread = exchange(
        shared_grads.astype(jnp.bfloat16).reshape(ctx_count, 2 * G // ctx_count, 2 * D), CTX
    )
    summed = jnp.sum(spread.astype(f32), 0).astype(jnp.bfloat16)
    shared_sums = to_all(summed, CTX).reshape(2, WORLDWIDE_COUNT, 1, S, 2 * D).astype(f32)

    halves = exchange(
        partial.astype(jnp.bfloat16).reshape(y_count, tokens, 2 * D), Y_AXIS
    ).astype(f32)
    mixed = (jnp.sum(halves, 0) + mixed).reshape(block_count, S, 2 * D)
    pairs = (returned.astype(f32) + pairs).reshape(block_count, S, 2 * D)
    for g in range(WORLDWIDE_COUNT):
        mask = hits[:, g][:, None, None]
        mixed = jnp.where(mask, shared_sums[1, g], mixed)
        pairs = pairs + jnp.where(mask, shared_sums[0, g], 0.0)
    mixed = mixed.reshape(tokens, 2 * D).astype(jnp.bfloat16)
    pairs = pairs.reshape(tokens, 2 * D).astype(jnp.bfloat16)
    return mixed[:, :D], mixed[:, D:], pairs[:, :D], pairs[:, D:]


def solution(mesh):
    torus = Mesh(mesh.devices.reshape(16, 4, mesh.shape["head"]), ("ctx_0", "ctx_1", "head"))
    return on_torus(torus)


def on_torus(torus):
    placed = (
        P(CTX_HEAD, None),
        P(CTX_HEAD, None),
        P(CTX_HEAD, None),
        P(CTX_HEAD, None),
        P(CTX, "head", None),
        P(),
    )
    return jax.shard_map(
        body,
        mesh=torus,
        in_specs=placed,
        out_specs=(P(CTX, "head"), P(CTX, "head"), P(CTX, "head"), P(CTX, "head")),
        check_vma=False,
    )
```

```python
import functools

import jax
import jax.numpy as jnp
from jax import lax
from jax.experimental import pallas as pl
from jax.experimental.pallas import tpu as pltpu
from jax.sharding import Mesh
from jax.sharding import PartitionSpec as P

FEATURE_LENGTH = 128
SPAN_TOKENS = 64
RANDOM = 3
WORLDWIDE_COUNT = 2
Z_AXIS = "ctx_0"
Y_AXIS = "ctx_1"
CTX = (Z_AXIS, Y_AXIS)
CTX_HEAD = (Z_AXIS, Y_AXIS, "head")
NEG = -1e30
SCALE = FEATURE_LENGTH ** (-0.5)
UNROLL = 4
SLOTS = 1 + RANDOM
D = FEATURE_LENGTH
S = SPAN_TOKENS
G = WORLDWIDE_COUNT * SPAN_TOKENS
VMEM = pl.BlockSpec(memory_space=pltpu.VMEM)
SMEM = pl.BlockSpec(memory_space=pltpu.SMEM)
PARAMS = pltpu.CompilerParams(vmem_limit_bytes=56 * 2**20)


def dot_nt(a, b):
    return lax.dot_general(a, b, (((1,), (1,)), ((), ())), preferred_element_type=jnp.float32)


def dot_nn(a, b):
    return lax.dot_general(a, b, (((1,), (0,)), ((), ())), preferred_element_type=jnp.float32)


def dot_tn(a, b):
    return lax.dot_general(a, b, (((0,), (0,)), ((), ())), preferred_element_type=jnp.float32)


def list_masks(listed, block_total):
    inside = (listed >= 0) & (listed < block_total)
    kept = []
    for slot_pos in range(listed.shape[-1]):
        seen = jnp.zeros(listed.shape[:-1], dtype=jnp.bool_)
        for prior_pos in range(slot_pos):
            seen = seen | inside[..., prior_pos] & (listed[..., prior_pos] == listed[..., slot_pos])
        kept.append(inside[..., slot_pos] & jnp.logical_not(seen))
    return jnp.stack(kept, -1)


def exchange(array, axes):
    return lax.all_to_all(array, axes, split_axis=0, concat_axis=0, tiled=True)


def to_all(array, axes):
    count = lax.axis_size(axes)
    return exchange(jnp.broadcast_to(array[None], (count,) + array.shape), axes)


def by_head(first, second):
    rows = first.shape[0]
    heads = first.shape[1] // D
    both = jnp.concatenate([first.reshape(rows, heads, D), second.reshape(rows, heads, D)], 2)
    return exchange(both.transpose(1, 0, 2), "head").reshape(heads * rows, 2 * D)


def merge(parts):
    top = functools.reduce(jnp.maximum, [part[0] for part in parts])
    factors = [jnp.exp(part[0] - top) for part in parts]
    total = sum(part[1] * factor for part, factor in zip(parts, factors))
    slope = sum(part[2] * factor for part, factor in zip(parts, factors))
    return top, total, slope


def column_stats(scores, slopes):
    top = jnp.max(scores, axis=0, keepdims=True)
    weights = jnp.exp(scores - top)
    return (
        top,
        jnp.sum(weights, axis=0, keepdims=True),
        jnp.sum(weights * slopes, axis=0, keepdims=True),
    )


def own_scores(i, blocks, qd_ref, kv_ref, shared_ref, bias_ref):
    low = max(i - 1, 0) * S
    high = min(i + 2, blocks) * S
    q = qd_ref[i * S : (i + 1) * S, :D]
    dout = qd_ref[i * S : (i + 1) * S, D:]
    scores = dot_nt(kv_ref[low:high, :D], q) * SCALE
    slopes = dot_nt(kv_ref[low:high, D:], dout)
    global_scores = dot_nt(shared_ref[:, 2 * D : 3 * D], q) * SCALE
    global_scores = jnp.concatenate(
        [
            global_scores[g * S : (g + 1) * S] + bias_ref[i * WORLDWIDE_COUNT + g]
            for g in range(WORLDWIDE_COUNT)
        ],
        0,
    )
    global_slopes = dot_nt(shared_ref[:, 3 * D :], dout)
    return low, high, q, dout, scores, slopes, global_scores, global_slopes


def own_stats_kernel(bias_ref, qd_ref, kv_ref, shared_ref, own_ref, rows_ref):
    tokens = qd_ref.shape[0]
    blocks = tokens // S
    for i in range(blocks):
        _, _, _, _, scores, slopes, global_scores, global_slopes = own_scores(
            i, blocks, qd_ref, kv_ref, shared_ref, bias_ref
        )
        top, total, slope = merge(
            [column_stats(scores, slopes), column_stats(global_scores, global_slopes)]
        )
        own_ref[0, i : i + 1, :] = top
        own_ref[1, i : i + 1, :] = total
        own_ref[2, i : i + 1, :] = slope
    parts = []
    for low in range(0, tokens, G):
        scores = dot_nt(kv_ref[low : low + G, :D], shared_ref[:, :D]) * SCALE
        slopes = dot_nt(kv_ref[low : low + G, D:], shared_ref[:, D : 2 * D])
        parts.append(column_stats(scores, slopes))
    top, total, slope = merge(parts)
    rows_ref[0:1, :] = top
    rows_ref[1:2, :] = total
    rows_ref[2:3, :] = slope


def edge_stats_kernel(
    meta_ref, slot_ref, item_ref, cell_ref, qd_ref, kv_ref, own_ref, out_ref, top_ref, total_ref, slope_ref
):
    group = qd_ref.shape[0] // S
    blocks = own_ref.shape[1]
    top_ref[...] = jnp.full(top_ref.shape, NEG, jnp.float32)
    total_ref[...] = jnp.zeros(total_ref.shape, jnp.float32)
    slope_ref[...] = jnp.zeros(slope_ref.shape, jnp.float32)

    def step(t, carry):
        found = []
        for u in range(UNROLL):
            pos = t * UNROLL + u
            cell = pl.multiple_of(cell_ref[pos] * S, S)
            item = pl.multiple_of(item_ref[pos] * S, S)
            scores = dot_nt(kv_ref[pl.ds(cell, S), :D], qd_ref[pl.ds(item, S), :D]) * SCALE
            slopes = dot_nt(kv_ref[pl.ds(cell, S), D:], qd_ref[pl.ds(item, S), D:])
            found.append((slot_ref[pos], column_stats(scores, slopes)))
        for slot, (top, total, slope) in found:
            top_ref[pl.ds(slot, 1), :] = top
            total_ref[pl.ds(slot, 1), :] = total
            slope_ref[pl.ds(slot, 1), :] = slope
        return carry

    lax.fori_loop(0, meta_ref[0], step, 0)
    mine = pl.multiple_of(SLOTS * group + meta_ref[1] * blocks, 8)
    top_ref[pl.ds(mine, blocks), :] = own_ref[0]
    total_ref[pl.ds(mine, blocks), :] = own_ref[1]
    slope_ref[pl.ds(mine, blocks), :] = own_ref[2]
    top, total, slope = merge(
        [
            (
                top_ref[s * group : (s + 1) * group, :],
                total_ref[s * group : (s + 1) * group, :],
                slope_ref[s * group : (s + 1) * group, :],
            )
            for s in range(SLOTS + 1)
        ]
    )
    first = jnp.concatenate([top, total], 1)
    second = jnp.concatenate([slope, slope], 1)
    for lane in range(out_ref.shape[0]):
        out_ref[lane, :group, :] = first
        out_ref[lane, group:, :] = second


def edge_grads_kernel(
    meta_ref, slot_ref, item_ref, cell_ref, qd_ref, kv_ref, parts_ref, table_ref, final_ref, mixed_ref, *rest
):
    sent_refs = rest[:-1]
    partial_ref = rest[-1]
    group = qd_ref.shape[0] // S
    tokens = mixed_ref.shape[0]
    lanes = parts_ref.shape[0]
    top, total, slope = merge(
        [
            (
                parts_ref[lane, :group, :S],
                parts_ref[lane, :group, S:],
                parts_ref[lane, group:, :S],
            )
            for lane in range(lanes)
        ]
    )
    inverse = 1.0 / total
    final_ref[0] = top
    final_ref[1] = inverse
    final_ref[2] = slope * inverse
    table_ref[...] = jnp.zeros(table_ref.shape, jnp.bfloat16)
    partial_ref[...] = jnp.zeros(partial_ref.shape, jnp.float32)

    def step(t, carry):
        found = []
        for u in range(UNROLL):
            pos = t * UNROLL + u
            slot = slot_ref[pos]
            live = slot < SLOTS * group
            item_pos = lax.rem(slot, group)
            cell = pl.multiple_of(cell_ref[pos] * S, S)
            item = pl.multiple_of(item_ref[pos] * S, S)
            key = kv_ref[pl.ds(cell, S), :D]
            value = kv_ref[pl.ds(cell, S), D:]
            q = qd_ref[pl.ds(item, S), :D]
            dout = qd_ref[pl.ds(item, S), D:]
            scores = dot_nt(key, q) * SCALE
            slopes = dot_nt(value, dout)
            prob = jnp.exp(scores - final_ref[0, pl.ds(item_pos, 1), :])
            prob = prob * final_ref[1, pl.ds(item_pos, 1), :]
            prob = jnp.where(live, prob, 0.0)
            dscore = prob * ((slopes - final_ref[2, pl.ds(item_pos, 1), :]) * SCALE)
            prob = prob.astype(jnp.bfloat16)
            dscore = dscore.astype(jnp.bfloat16)
            found.append(
                (
                    cell,
                    item,
                    dot_nn(dscore, q),
                    dot_nn(prob, dout),
                    dot_tn(prob, value),
                    dot_tn(dscore, key),
                )
            )
        for cell, item, dkey, dvalue, mixed, dq in found:
            at = pl.ds(cell, S)
            table_ref[at, :D] = (table_ref[at, :D].astype(jnp.float32) + dkey).astype(jnp.bfloat16)
            table_ref[at, D:] = (table_ref[at, D:].astype(jnp.float32) + dvalue).astype(jnp.bfloat16)
            at = pl.ds(item, S)
            partial_ref[at, :D] += mixed
            partial_ref[at, D:] += dq
        return carry

    lax.fori_loop(0, meta_ref[0], step, 0)
    mixed_ref[...] = partial_ref[:tokens, :]
    for shift, sent_ref in enumerate(sent_refs):
        low = (shift + 1) * tokens
        sent_ref[...] = partial_ref[low : low + tokens, :].astype(jnp.bfloat16)


def own_grads_kernel(
    meta_ref,
    bias_ref,
    flag_ref,
    qd_ref,
    kv_ref,
    shared_ref,
    final_ref,
    rows_ref,
    edge_ref,
    pairs_ref,
    mixed_ref,
    shared_grad_ref,
):
    tokens = qd_ref.shape[0]
    blocks = tokens // S
    first = meta_ref[1] * blocks
    rows = rows_ref[...]
    row_top = jnp.max(rows[:, 0:1, :], axis=0)
    factors = jnp.exp(rows[:, 0:1, :] - row_top[None])
    sums = jnp.sum(rows * factors, axis=0)
    row_inverse = 1.0 / sums[1:2]
    row_slope = sums[2:3] * row_inverse
    q = shared_ref[:, :D]
    dout = shared_ref[:, D : 2 * D]
    mixed = jnp.zeros((G, D), jnp.float32)
    dq = jnp.zeros((G, D), jnp.float32)
    for low in range(0, tokens, G):
        key = kv_ref[low : low + G, :D]
        value = kv_ref[low : low + G, D:]
        scores = dot_nt(key, q) * SCALE
        slopes = dot_nt(value, dout)
        prob = jnp.exp(scores - row_top) * row_inverse
        dscore = (prob * ((slopes - row_slope) * SCALE)).astype(jnp.bfloat16)
        prob = prob.astype(jnp.bfloat16)
        pairs_ref[low : low + G, :D] = dot_nn(dscore, q)
        pairs_ref[low : low + G, D:] = dot_nn(prob, dout)
        mixed = mixed + dot_tn(prob, value)
        dq = dq + dot_tn(dscore, key)
    shared_grad_ref[G:, :D] = mixed
    shared_grad_ref[G:, D:] = dq
    global_dkey = jnp.zeros((G, D), jnp.float32)
    global_dvalue = jnp.zeros((G, D), jnp.float32)
    for i in range(blocks):
        low, high, q, dout, scores, slopes, global_scores, global_slopes = own_scores(
            i, blocks, qd_ref, kv_ref, shared_ref, bias_ref
        )
        top = final_ref[0, pl.ds(first + i, 1), :]
        inverse = final_ref[1, pl.ds(first + i, 1), :] * flag_ref[i]
        slope = final_ref[2, pl.ds(first + i, 1), :]

        def both(scores, slopes):
            prob = jnp.exp(scores - top) * inverse
            dscore = (prob * ((slopes - slope) * SCALE)).astype(jnp.bfloat16)
            return prob.astype(jnp.bfloat16), dscore

        prob, dscore = both(scores, slopes)
        global_prob, global_dscore = both(global_scores, global_slopes)
        pairs_ref[low:high, :D] += dot_nn(dscore, q)
        pairs_ref[low:high, D:] += dot_nn(prob, dout)
        global_dkey = global_dkey + dot_nn(global_dscore, q)
        global_dvalue = global_dvalue + dot_nn(global_prob, dout)
        at = slice(i * S, (i + 1) * S)
        mixed_ref[at, :D] = (
            edge_ref[at, :D]
            + dot_tn(prob, kv_ref[low:high, D:])
            + dot_tn(global_prob, shared_ref[:, 3 * D :])
        )
        mixed_ref[at, D:] = (
            edge_ref[at, D:]
            + dot_tn(dscore, kv_ref[low:high, :D])
            + dot_tn(global_dscore, shared_ref[:, 2 * D : 3 * D])
        )
    shared_grad_ref[:G, :D] = global_dkey
    shared_grad_ref[:G, D:] = global_dvalue


def body(query, key_in, value_in, grad_out, random_blocks, universal_segment_indices):
    f32 = jnp.float32
    z_count = lax.axis_size(Z_AXIS)
    y_count = lax.axis_size(Y_AXIS)
    ctx_count = z_count * y_count
    z_place = lax.axis_index(Z_AXIS)
    y_place = lax.axis_index(Y_AXIS)
    ctx_place = z_place * y_count + y_place

    kv = by_head(key_in, value_in)
    query, grad_out, random_blocks, kv = lax.optimization_barrier(
        (query, grad_out, random_blocks, kv)
    )
    kv_all = lax.all_gather(kv, Z_AXIS, axis=0, tiled=True)
    qd = by_head(query, grad_out)
    tokens = qd.shape[0]
    block_count = tokens // S
    group = block_count * y_count
    block_total = ctx_count * block_count
    cells = z_count * block_count

    owners = universal_segment_indices // block_count
    starts = universal_segment_indices % block_count * S
    pieces = []
    for g in range(WORLDWIDE_COUNT):
        pieces.append(
            jnp.concatenate(
                [lax.dynamic_slice_in_dim(part, starts[g], S, 0) for part in (qd, kv)], 1
            )
        )
    part = G // y_count
    owner = owners[(y_place * part) // S]
    sent = jnp.concatenate(pieces, 0).reshape(y_count, part, 4 * D)
    picked = lax.dynamic_index_in_dim(exchange(sent, Y_AXIS), owner % y_count, 0, False)
    sent = picked.reshape(z_count, part // z_count, 4 * D)
    picked = lax.dynamic_index_in_dim(exchange(sent, Z_AXIS), owner // y_count, 0, False)
    shared = to_all(picked, Z_AXIS).reshape(part, 4 * D)
    shared = to_all(shared, Y_AXIS).reshape(G, 4 * D)

    shifts = range(1, y_count)
    forward = [[(i, (i + shift) % y_count) for i in range(y_count)] for shift in shifts]
    backward = [[(i, (i - shift) % y_count) for i in range(y_count)] for shift in shifts]
    qd_group = jnp.concatenate([qd] + [lax.ppermute(qd, Y_AXIS, pairs) for pairs in forward], 0)
    random_group = to_all(random_blocks[:, 0, :], Y_AXIS).reshape(group, RANDOM)

    ids = z_place * group + jnp.arange(group, dtype=jnp.int32)
    local = jnp.arange(group, dtype=jnp.int32) % block_count
    globals_ = jnp.broadcast_to(universal_segment_indices[None], (group, WORLDWIDE_COUNT))
    listed = jnp.concatenate(
        [jnp.stack([ids - 1, ids, ids + 1], 1), random_group, globals_], 1
    )
    kept = list_masks(listed, block_total)
    is_global = jnp.any(ids[:, None] == universal_segment_indices[None], 1)
    border = jnp.where(local == 0, ids - 1, jnp.where(local == block_count - 1, ids + 1, -1))
    named = jnp.concatenate([border[:, None], random_group], 1)
    valid = jnp.concatenate(
        [((border >= 0) & (border < block_total))[:, None], kept[:, 3 : 3 + RANDOM]], 1
    )
    lane = named // block_count % y_count
    valid = valid & jnp.logical_not(is_global)[:, None] & (lane == y_place)
    cell = named // group * block_count + named % block_count
    valid = valid.T.reshape(-1)
    cell = cell.T.reshape(-1)
    entries = SLOTS * group
    order = jnp.arange(entries, dtype=jnp.int32)
    rank = jnp.cumsum(valid.astype(jnp.int32)) - 1
    edge_count = rank[-1] + 1
    hit = (rank[None, :] == order[:, None]) & valid[None, :]
    slot_list = jnp.sum(jnp.where(hit, order[None, :], 0), 1)
    cell_list = jnp.sum(jnp.where(hit, cell[None, :], 0), 1)
    slot_list = jnp.where(order < edge_count, slot_list, entries + group)
    item_list = slot_list % group
    item_list = (y_place - item_list // block_count) % y_count * block_count + item_list % block_count
    meta = jnp.stack([(edge_count + UNROLL - 1) // UNROLL, y_place]).astype(jnp.int32)
    lists = (meta, slot_list, item_list, cell_list)

    own_first = y_place * block_count
    own_kept = lax.dynamic_slice_in_dim(kept, own_first, block_count, 0)
    bias = jnp.where(own_kept[:, 3 + RANDOM :], 0.0, NEG).astype(f32).reshape(-1)
    own_ids = ctx_place * block_count + jnp.arange(block_count, dtype=jnp.int32)
    hits = own_ids[:, None] == universal_segment_indices[None]
    flags = jnp.where(jnp.any(hits, 1), 0.0, 1.0).astype(f32)

    own, rows = pl.pallas_call(
        own_stats_kernel,
        out_shape=(
            jax.ShapeDtypeStruct((3, block_count, S), f32),
            jax.ShapeDtypeStruct((3, G), f32),
        ),
        in_specs=[SMEM, VMEM, VMEM, VMEM],
        out_specs=(VMEM, VMEM),
        compiler_params=PARAMS,
        name="own_stats",
    )(bias, qd, kv, shared)
    rows_all = to_all(rows, Z_AXIS)
    own, rows_all = lax.optimization_barrier((own, rows_all))

    stat_rows = (SLOTS + 1) * group + 8
    stats = pl.pallas_call(
        edge_stats_kernel,
        out_shape=jax.ShapeDtypeStruct((y_count, 2 * group, 2 * S), f32),
        in_specs=[SMEM] * 4 + [VMEM] * 3,
        out_specs=VMEM,
        scratch_shapes=[pltpu.VMEM((stat_rows, S), f32)] * 3,
        compiler_params=PARAMS,
        name="edge_stats",
    )(*lists, qd_group, kv_all, own)
    parts = exchange(stats, Y_AXIS)

    table, final, edge_mixed, *halves = pl.pallas_call(
        edge_grads_kernel,
        out_shape=(
            jax.ShapeDtypeStruct((cells * S, 2 * D), jnp.bfloat16),
            jax.ShapeDtypeStruct((3, group, S), f32),
            jax.ShapeDtypeStruct((tokens, 2 * D), f32),
        )
        + (jax.ShapeDtypeStruct((tokens, 2 * D), jnp.bfloat16),) * (y_count - 1),
        in_specs=[SMEM] * 4 + [VMEM] * 3,
        out_specs=(VMEM,) * (y_count + 2),
        scratch_shapes=[pltpu.VMEM((group * S, 2 * D), f32)],
        compiler_params=PARAMS,
        name="edge_grads",
    )(*lists, qd_group, kv_all, parts)
    returned = lax.psum_scatter(table, Z_AXIS, scatter_dimension=0, tiled=True)
    halves = [lax.ppermute(half, Y_AXIS, pairs) for half, pairs in zip(halves, backward)]
    rows_all = to_all(rows_all, Y_AXIS).reshape(ctx_count, 3, G)

    pairs, mixed, shared_grads = pl.pallas_call(
        own_grads_kernel,
        out_shape=(
            jax.ShapeDtypeStruct((tokens, 2 * D), f32),
            jax.ShapeDtypeStruct((tokens, 2 * D), f32),
            jax.ShapeDtypeStruct((2 * G, 2 * D), f32),
        ),
        in_specs=[SMEM] * 3 + [VMEM] * 6,
        out_specs=(VMEM, VMEM, VMEM),
        compiler_params=PARAMS,
        name="own_grads",
    )(meta, bias, flags, qd, kv, shared, final, rows_all, edge_mixed)

    summed = shared_grads.astype(jnp.bfloat16)
    for axis in (Y_AXIS, Z_AXIS):
        count = lax.axis_size(axis)
        summed = exchange(summed.reshape(count, -1, 2 * D), axis)
        summed = jnp.sum(summed.astype(f32), 0).astype(jnp.bfloat16)
    for axis in (Z_AXIS, Y_AXIS):
        summed = to_all(summed, axis).reshape(-1, 2 * D)
    shared_sums = summed.reshape(2, WORLDWIDE_COUNT, 1, S, 2 * D).astype(f32)

    mixed = sum([half.astype(f32) for half in halves], mixed).reshape(block_count, S, 2 * D)
    pairs = (returned.astype(f32) + pairs).reshape(block_count, S, 2 * D)
    for g in range(WORLDWIDE_COUNT):
        mask = hits[:, g][:, None, None]
        mixed = jnp.where(mask, shared_sums[1, g], mixed)
        pairs = pairs + jnp.where(mask, shared_sums[0, g], 0.0)
    mixed = mixed.reshape(tokens, 2 * D).astype(jnp.bfloat16)
    pairs = pairs.reshape(tokens, 2 * D).astype(jnp.bfloat16)
    return mixed[:, :D], mixed[:, D:], pairs[:, :D], pairs[:, D:]


def solution(mesh):
    torus = Mesh(mesh.devices.reshape(16, 4, mesh.shape["head"]), ("ctx_0", "ctx_1", "head"))
    return on_torus(torus)


def on_torus(torus):
    placed = (
        P(CTX_HEAD, None),
        P(CTX_HEAD, None),
        P(CTX_HEAD, None),
        P(CTX_HEAD, None),
        P(CTX, "head", None),
        P(),
    )
    return jax.shard_map(
        body,
        mesh=torus,
        in_specs=placed,
        out_specs=(P(CTX, "head"), P(CTX, "head"), P(CTX, "head"), P(CTX, "head")),
        check_vma=False,
    )
```

```python
import functools

import jax
import jax.numpy as jnp
from jax import lax
from jax.experimental import pallas as pl
from jax.experimental.pallas import tpu as pltpu
from jax.sharding import Mesh
from jax.sharding import PartitionSpec as P

FEATURE_LENGTH = 128
SPAN_TOKENS = 64
RANDOM = 3
WORLDWIDE_COUNT = 2
Z_AXIS = "ctx_0"
Y_AXIS = "ctx_1"
CTX = (Z_AXIS, Y_AXIS)
CTX_HEAD = (Z_AXIS, Y_AXIS, "head")
NEG = -1e30
SCALE = FEATURE_LENGTH ** (-0.5)
UNROLL = 4
DEPTH = 8
STAGES = 16
SLOTS = 1 + RANDOM
D = FEATURE_LENGTH
S = SPAN_TOKENS
G = WORLDWIDE_COUNT * SPAN_TOKENS
VMEM = pl.BlockSpec(memory_space=pltpu.VMEM)
SMEM = pl.BlockSpec(memory_space=pltpu.SMEM)
ANY = pl.BlockSpec(memory_space=pl.ANY)
PARAMS = pltpu.CompilerParams(vmem_limit_bytes=56 * 2**20)


def dot_nt(a, b):
    return lax.dot_general(a, b, (((1,), (1,)), ((), ())), preferred_element_type=jnp.float32)


def dot_nn(a, b):
    return lax.dot_general(a, b, (((1,), (0,)), ((), ())), preferred_element_type=jnp.float32)


def dot_tn(a, b):
    return lax.dot_general(a, b, (((0,), (0,)), ((), ())), preferred_element_type=jnp.float32)


def list_masks(listed, block_total):
    inside = (listed >= 0) & (listed < block_total)
    kept = []
    for slot_pos in range(listed.shape[-1]):
        seen = jnp.zeros(listed.shape[:-1], dtype=jnp.bool_)
        for prior_pos in range(slot_pos):
            seen = seen | inside[..., prior_pos] & (listed[..., prior_pos] == listed[..., slot_pos])
        kept.append(inside[..., slot_pos] & jnp.logical_not(seen))
    return jnp.stack(kept, -1)


def exchange(array, axes):
    return lax.all_to_all(array, axes, split_axis=0, concat_axis=0, tiled=True)


def to_all(array, axes):
    count = lax.axis_size(axes)
    return exchange(jnp.broadcast_to(array[None], (count,) + array.shape), axes)


def by_head(first, second):
    rows = first.shape[0]
    heads = first.shape[1] // D
    both = jnp.concatenate([first.reshape(rows, heads, D), second.reshape(rows, heads, D)], 2)
    return exchange(both.transpose(1, 0, 2), "head").reshape(heads * rows, 2 * D)


def merge(parts):
    top = functools.reduce(jnp.maximum, [part[0] for part in parts])
    factors = [jnp.exp(part[0] - top) for part in parts]
    total = sum(part[1] * factor for part, factor in zip(parts, factors))
    slope = sum(part[2] * factor for part, factor in zip(parts, factors))
    return top, total, slope


def column_stats(scores, slopes):
    top = jnp.max(scores, axis=0, keepdims=True)
    weights = jnp.exp(scores - top)
    return (
        top,
        jnp.sum(weights, axis=0, keepdims=True),
        jnp.sum(weights * slopes, axis=0, keepdims=True),
    )


def own_scores(i, blocks, qd_ref, kv_ref, shared_ref, bias_ref):
    low = max(i - 1, 0) * S
    high = min(i + 2, blocks) * S
    q = qd_ref[i * S : (i + 1) * S, :D]
    dout = qd_ref[i * S : (i + 1) * S, D:]
    scores = dot_nt(kv_ref[low:high, :D], q) * SCALE
    slopes = dot_nt(kv_ref[low:high, D:], dout)
    global_scores = dot_nt(shared_ref[:, 2 * D : 3 * D], q) * SCALE
    global_scores = jnp.concatenate(
        [
            global_scores[g * S : (g + 1) * S] + bias_ref[i * WORLDWIDE_COUNT + g]
            for g in range(WORLDWIDE_COUNT)
        ],
        0,
    )
    global_slopes = dot_nt(shared_ref[:, 3 * D :], dout)
    return low, high, q, dout, scores, slopes, global_scores, global_slopes


def own_stats_kernel(bias_ref, qd_ref, kv_ref, shared_ref, own_ref, rows_ref):
    tokens = qd_ref.shape[0]
    blocks = tokens // S
    for i in range(blocks):
        _, _, _, _, scores, slopes, global_scores, global_slopes = own_scores(
            i, blocks, qd_ref, kv_ref, shared_ref, bias_ref
        )
        top, total, slope = merge(
            [column_stats(scores, slopes), column_stats(global_scores, global_slopes)]
        )
        own_ref[0, i : i + 1, :] = top
        own_ref[1, i : i + 1, :] = total
        own_ref[2, i : i + 1, :] = slope
    parts = []
    for low in range(0, tokens, G):
        scores = dot_nt(kv_ref[low : low + G, :D], shared_ref[:, :D]) * SCALE
        slopes = dot_nt(kv_ref[low : low + G, D:], shared_ref[:, D : 2 * D])
        parts.append(column_stats(scores, slopes))
    top, total, slope = merge(parts)
    rows_ref[0:1, :] = top
    rows_ref[1:2, :] = total
    rows_ref[2:3, :] = slope


def cell_fetcher(meta_ref, cell_ref, kv_ref, fetch_ref, fetch_sems):
    def copies(t):
        found = []
        for u in range(UNROLL):
            buffer = lax.rem(t, DEPTH) * UNROLL + u
            cell = pl.multiple_of(cell_ref[t * UNROLL + u] * S, S)
            found.append(
                pltpu.make_async_copy(
                    kv_ref.at[pl.ds(cell, S), :], fetch_ref.at[buffer], fetch_sems.at[buffer]
                )
            )
        return found

    def start(t):
        @pl.when(t < meta_ref[0])
        def _():
            for copy in copies(t):
                copy.start()

    def wait(t):
        for copy in copies(t):
            copy.wait()

    return start, wait


def diagonal(qd):
    zeros = jnp.zeros((S, D), jnp.bfloat16)
    return jnp.concatenate(
        [jnp.concatenate([qd[:, :D], zeros], 1), jnp.concatenate([zeros, qd[:, D:]], 1)], 0
    )


def lane_scale():
    return jnp.where(lax.broadcasted_iota(jnp.int32, (1, 2 * S), 1) < S, SCALE, 1.0)


def edge_stats_kernel(
    meta_ref,
    slot_ref,
    item_ref,
    cell_ref,
    qd_ref,
    kv_ref,
    own_ref,
    out_ref,
    table_ref,
    top_ref,
    total_ref,
    slope_ref,
    zero_ref,
    fetch_ref,
    fetch_sems,
    zero_sems,
):
    group = qd_ref.shape[0] // S
    blocks = own_ref.shape[1]
    start, wait = cell_fetcher(meta_ref, cell_ref, kv_ref, fetch_ref, fetch_sems)
    for t in range(DEPTH):
        start(t)
    rows = zero_ref.shape[0]
    zero_ref[...] = jnp.zeros(zero_ref.shape, jnp.bfloat16)
    clears = [
        pltpu.make_async_copy(zero_ref, table_ref.at[pl.ds(i * rows, rows), :], zero_sems.at[i])
        for i in range(table_ref.shape[0] // rows)
    ]
    for clear in clears:
        clear.start()
    top_ref[...] = jnp.full(top_ref.shape, NEG, jnp.float32)
    total_ref[...] = jnp.zeros(total_ref.shape, jnp.float32)
    slope_ref[...] = jnp.zeros(slope_ref.shape, jnp.float32)
    factor = lane_scale()

    def step(t, carry):
        wait(t)
        found = []
        for u in range(UNROLL):
            pos = t * UNROLL + u
            item = pl.multiple_of(item_ref[pos] * S, S)
            pairs = fetch_ref[lax.rem(t, DEPTH) * UNROLL + u]
            both = dot_nt(pairs, diagonal(qd_ref[pl.ds(item, S), :])) * factor
            top = jnp.max(both, axis=0, keepdims=True)
            weights = jnp.exp(both - top)
            total = jnp.sum(weights, axis=0, keepdims=True)
            slope = jnp.sum(weights * pltpu.roll(both, S, 1), axis=0, keepdims=True)
            found.append((slot_ref[pos], top, total, slope))
        for slot, top, total, slope in found:
            top_ref[pl.ds(slot, 1), :] = top
            total_ref[pl.ds(slot, 1), :] = total
            slope_ref[pl.ds(slot, 1), :] = slope
        start(t + DEPTH)
        return carry

    lax.fori_loop(0, meta_ref[0], step, 0)
    mine = pl.multiple_of(SLOTS * group + meta_ref[1] * blocks, 8)
    top_ref[pl.ds(mine, blocks), :S] = own_ref[0]
    total_ref[pl.ds(mine, blocks), :S] = own_ref[1]
    slope_ref[pl.ds(mine, blocks), :S] = own_ref[2]
    top, total, slope = merge(
        [
            (
                top_ref[s * group : (s + 1) * group, :S],
                total_ref[s * group : (s + 1) * group, :S],
                slope_ref[s * group : (s + 1) * group, :S],
            )
            for s in range(SLOTS + 1)
        ]
    )
    first = jnp.concatenate([top, total], 1)
    second = jnp.concatenate([slope, slope], 1)
    for lane in range(out_ref.shape[0]):
        out_ref[lane, :group, :] = first
        out_ref[lane, group:, :] = second
    for clear in clears:
        clear.wait()


def edge_grads_kernel(
    meta_ref,
    slot_ref,
    item_ref,
    cell_ref,
    order_ref,
    last_ref,
    qd_ref,
    kv_ref,
    parts_ref,
    cleared_ref,
    table_ref,
    final_ref,
    mixed_ref,
    *rest,
):
    sent_refs = rest[:-6]
    partial_ref, sum_ref, stage_ref, fetch_ref, fetch_sems, stage_sems = rest[-6:]
    group = qd_ref.shape[0] // S
    tokens = mixed_ref.shape[0]
    lanes = parts_ref.shape[0]
    start, wait = cell_fetcher(meta_ref, cell_ref, kv_ref, fetch_ref, fetch_sems)
    for t in range(DEPTH):
        start(t)
    top, total, slope = merge(
        [
            (
                parts_ref[lane, :group, :],
                pltpu.roll(parts_ref[lane, :group, :], S, 1),
                parts_ref[lane, group:, :],
            )
            for lane in range(lanes)
        ]
    )
    inverse = 1.0 / total
    final_ref[0] = top
    final_ref[1] = inverse
    final_ref[2] = slope * inverse
    partial_ref[...] = jnp.zeros(partial_ref.shape, jnp.float32)
    sum_ref[...] = jnp.zeros(sum_ref.shape, jnp.float32)
    factor = lane_scale()
    low_half = lax.broadcasted_iota(jnp.int32, (S, 2 * S), 1) < S

    def stage_copy(stage, cell):
        at = pl.ds(pl.multiple_of(cell * S, S), S)
        return pltpu.make_async_copy(stage_ref.at[stage], table_ref.at[at, :], stage_sems.at[stage])

    def step(t, carry):
        wait(t)
        found = []
        for u in range(UNROLL):
            pos = t * UNROLL + u
            slot = slot_ref[pos]
            live = slot < SLOTS * group
            row = pl.ds(lax.rem(slot, group), 1)
            item = pl.multiple_of(item_ref[pos] * S, S)
            pairs = fetch_ref[lax.rem(t, DEPTH) * UNROLL + u]
            corner = diagonal(qd_ref[pl.ds(item, S), :])
            both = dot_nt(pairs, corner) * factor
            prob = jnp.exp(both - final_ref[0, row, :]) * final_ref[1, row, :]
            dscore = prob * ((pltpu.roll(both, S, 1) - final_ref[2, row, :]) * SCALE)
            packed = jnp.where(low_half, dscore, pltpu.roll(prob, S, 1))
            packed = jnp.where(live, packed, 0.0).astype(jnp.bfloat16)
            found.append((pos, item, dot_nn(packed, corner), dot_tn(packed, pairs)))
        running = sum_ref[...]
        for pos, item, grads, crossed in found:
            fresh = order_ref[pos] != order_ref[jnp.maximum(pos - 1, 0)]
            running = grads + jnp.where(fresh, 0.0, running)

            @pl.when(last_ref[pos] > 0)
            def _():
                stage = lax.rem(order_ref[pos], STAGES)

                @pl.when(order_ref[pos] >= STAGES)
                def _():
                    stage_copy(stage, cell_ref[pos]).wait()

                stage_ref[stage] = running.astype(jnp.bfloat16)
                stage_copy(stage, cell_ref[pos]).start()

            at = pl.ds(item, S)
            partial_ref[at, :D] += crossed[S:, D:]
            partial_ref[at, D:] += crossed[:S, :D]
        sum_ref[...] = running
        start(t + DEPTH)
        return carry

    lax.fori_loop(0, meta_ref[0], step, 0)
    mixed_ref[...] = partial_ref[:tokens, :]
    for shift, sent_ref in enumerate(sent_refs):
        low = (shift + 1) * tokens
        sent_ref[...] = partial_ref[low : low + tokens, :].astype(jnp.bfloat16)
    for stage in range(STAGES):

        @pl.when(stage < meta_ref[2])
        def _():
            stage_copy(stage, 0).wait()


def own_grads_kernel(
    meta_ref,
    bias_ref,
    flag_ref,
    qd_ref,
    kv_ref,
    shared_ref,
    final_ref,
    rows_ref,
    edge_ref,
    pairs_ref,
    mixed_ref,
    shared_grad_ref,
):
    tokens = qd_ref.shape[0]
    blocks = tokens // S
    first = meta_ref[1] * blocks
    rows = rows_ref[...]
    row_top = jnp.max(rows[:, 0:1, :], axis=0)
    factors = jnp.exp(rows[:, 0:1, :] - row_top[None])
    sums = jnp.sum(rows * factors, axis=0)
    row_inverse = 1.0 / sums[1:2]
    row_slope = sums[2:3] * row_inverse
    q = shared_ref[:, :D]
    dout = shared_ref[:, D : 2 * D]
    mixed = jnp.zeros((G, D), jnp.float32)
    dq = jnp.zeros((G, D), jnp.float32)
    for low in range(0, tokens, G):
        key = kv_ref[low : low + G, :D]
        value = kv_ref[low : low + G, D:]
        scores = dot_nt(key, q) * SCALE
        slopes = dot_nt(value, dout)
        prob = jnp.exp(scores - row_top) * row_inverse
        dscore = (prob * ((slopes - row_slope) * SCALE)).astype(jnp.bfloat16)
        prob = prob.astype(jnp.bfloat16)
        pairs_ref[low : low + G, :D] = dot_nn(dscore, q)
        pairs_ref[low : low + G, D:] = dot_nn(prob, dout)
        mixed = mixed + dot_tn(prob, value)
        dq = dq + dot_tn(dscore, key)
    shared_grad_ref[G:, :D] = mixed
    shared_grad_ref[G:, D:] = dq
    global_dkey = jnp.zeros((G, D), jnp.float32)
    global_dvalue = jnp.zeros((G, D), jnp.float32)
    for i in range(blocks):
        low, high, q, dout, scores, slopes, global_scores, global_slopes = own_scores(
            i, blocks, qd_ref, kv_ref, shared_ref, bias_ref
        )
        top = final_ref[0, pl.ds(first + i, 1), :S]
        inverse = final_ref[1, pl.ds(first + i, 1), :S] * flag_ref[i]
        slope = final_ref[2, pl.ds(first + i, 1), :S]

        def both(scores, slopes):
            prob = jnp.exp(scores - top) * inverse
            dscore = (prob * ((slopes - slope) * SCALE)).astype(jnp.bfloat16)
            return prob.astype(jnp.bfloat16), dscore

        prob, dscore = both(scores, slopes)
        global_prob, global_dscore = both(global_scores, global_slopes)
        pairs_ref[low:high, :D] += dot_nn(dscore, q)
        pairs_ref[low:high, D:] += dot_nn(prob, dout)
        global_dkey = global_dkey + dot_nn(global_dscore, q)
        global_dvalue = global_dvalue + dot_nn(global_prob, dout)
        at = slice(i * S, (i + 1) * S)
        mixed_ref[at, :D] = (
            edge_ref[at, :D]
            + dot_tn(prob, kv_ref[low:high, D:])
            + dot_tn(global_prob, shared_ref[:, 3 * D :])
        )
        mixed_ref[at, D:] = (
            edge_ref[at, D:]
            + dot_tn(dscore, kv_ref[low:high, :D])
            + dot_tn(global_dscore, shared_ref[:, 2 * D : 3 * D])
        )
    shared_grad_ref[:G, :D] = global_dkey
    shared_grad_ref[:G, D:] = global_dvalue


def body(query, key_in, value_in, grad_out, random_blocks, universal_segment_indices):
    f32 = jnp.float32
    z_count = lax.axis_size(Z_AXIS)
    y_count = lax.axis_size(Y_AXIS)
    ctx_count = z_count * y_count
    z_place = lax.axis_index(Z_AXIS)
    y_place = lax.axis_index(Y_AXIS)
    ctx_place = z_place * y_count + y_place

    kv = by_head(key_in, value_in)
    query, grad_out, random_blocks, kv = lax.optimization_barrier(
        (query, grad_out, random_blocks, kv)
    )
    kv_all = lax.all_gather(kv, Z_AXIS, axis=0, tiled=True)
    qd = by_head(query, grad_out)
    random_blocks, universal_segment_indices, qd = lax.optimization_barrier(
        (random_blocks, universal_segment_indices, qd)
    )
    tokens = qd.shape[0]
    block_count = tokens // S
    group = block_count * y_count
    block_total = ctx_count * block_count
    cells = z_count * block_count

    owners = universal_segment_indices // block_count
    starts = universal_segment_indices % block_count * S
    pieces = []
    for g in range(WORLDWIDE_COUNT):
        pieces.append(
            jnp.concatenate(
                [lax.dynamic_slice_in_dim(part, starts[g], S, 0) for part in (qd, kv)], 1
            )
        )
    part = G // y_count
    owner = owners[(y_place * part) // S]
    sent = jnp.concatenate(pieces, 0).reshape(y_count, part, 4 * D)
    picked = lax.dynamic_index_in_dim(exchange(sent, Y_AXIS), owner % y_count, 0, False)
    sent = picked.reshape(z_count, part // z_count, 4 * D)
    picked = lax.dynamic_index_in_dim(exchange(sent, Z_AXIS), owner // y_count, 0, False)
    shared = to_all(picked, Z_AXIS).reshape(part, 4 * D)
    shared = to_all(shared, Y_AXIS).reshape(G, 4 * D)

    shifts = range(1, y_count)
    forward = [[(i, (i + shift) % y_count) for i in range(y_count)] for shift in shifts]
    backward = [[(i, (i - shift) % y_count) for i in range(y_count)] for shift in shifts]
    qd_group = jnp.concatenate([qd] + [lax.ppermute(qd, Y_AXIS, pairs) for pairs in forward], 0)
    random_group = to_all(random_blocks[:, 0, :], Y_AXIS).reshape(group, RANDOM)

    ids = z_place * group + jnp.arange(group, dtype=jnp.int32)
    local = jnp.arange(group, dtype=jnp.int32) % block_count
    globals_ = jnp.broadcast_to(universal_segment_indices[None], (group, WORLDWIDE_COUNT))
    listed = jnp.concatenate(
        [jnp.stack([ids - 1, ids, ids + 1], 1), random_group, globals_], 1
    )
    kept = list_masks(listed, block_total)
    is_global = jnp.any(ids[:, None] == universal_segment_indices[None], 1)
    border = jnp.where(local == 0, ids - 1, jnp.where(local == block_count - 1, ids + 1, -1))
    named = jnp.concatenate([border[:, None], random_group], 1)
    valid = jnp.concatenate(
        [((border >= 0) & (border < block_total))[:, None], kept[:, 3 : 3 + RANDOM]], 1
    )
    lane = named // block_count % y_count
    valid = valid & jnp.logical_not(is_global)[:, None] & (lane == y_place)
    cell = named // group * block_count + named % block_count
    valid = valid.T.reshape(-1)
    cell = cell.T.reshape(-1)
    entries = SLOTS * group
    order = jnp.arange(entries, dtype=jnp.int32)
    label = cell * entries + order
    rank = jnp.sum((valid[None, :] & (label[None, :] < label[:, None])).astype(jnp.int32), 1)
    edge_count = jnp.sum(valid.astype(jnp.int32))
    hit = (rank[None, :] == order[:, None]) & valid[None, :]
    slot_list = jnp.sum(jnp.where(hit, order[None, :], 0), 1)
    cell_list = jnp.sum(jnp.where(hit, cell[None, :], 0), 1)
    real = order < edge_count
    fresh = real & ((order == 0) | (cell_list != jnp.roll(cell_list, 1)))
    last_list = real & ((order == edge_count - 1) | (cell_list != jnp.roll(cell_list, -1)))
    order_list = jnp.sum((fresh[None, :] & (order[None, :] <= order[:, None])).astype(jnp.int32), 1) - 1
    slot_list = jnp.where(real, slot_list, entries + group)
    item_list = slot_list % group
    item_list = (y_place - item_list // block_count) % y_count * block_count + item_list % block_count
    last_list = last_list.astype(jnp.int32)
    meta = jnp.stack(
        [(edge_count + UNROLL - 1) // UNROLL, y_place, jnp.sum(fresh.astype(jnp.int32))]
    ).astype(jnp.int32)
    lists = (meta, slot_list, item_list, cell_list)

    own_first = y_place * block_count
    own_kept = lax.dynamic_slice_in_dim(kept, own_first, block_count, 0)
    bias = jnp.where(own_kept[:, 3 + RANDOM :], 0.0, NEG).astype(f32).reshape(-1)
    own_ids = ctx_place * block_count + jnp.arange(block_count, dtype=jnp.int32)
    hits = own_ids[:, None] == universal_segment_indices[None]
    flags = jnp.where(jnp.any(hits, 1), 0.0, 1.0).astype(f32)

    own, rows = pl.pallas_call(
        own_stats_kernel,
        out_shape=(
            jax.ShapeDtypeStruct((3, block_count, S), f32),
            jax.ShapeDtypeStruct((3, G), f32),
        ),
        in_specs=[SMEM, VMEM, VMEM, VMEM],
        out_specs=(VMEM, VMEM),
        compiler_params=PARAMS,
        name="own_stats",
    )(bias, qd, kv, shared)

    stat_rows = (SLOTS + 1) * group + 8
    fetch_scratch = [
        pltpu.VMEM((DEPTH * UNROLL, S, 2 * D), jnp.bfloat16),
        pltpu.SemaphoreType.DMA((DEPTH * UNROLL,)),
    ]
    stats, cleared = pl.pallas_call(
        edge_stats_kernel,
        out_shape=(
            jax.ShapeDtypeStruct((y_count, 2 * group, 2 * S), f32),
            jax.ShapeDtypeStruct((cells * S, 2 * D), jnp.bfloat16),
        ),
        in_specs=[SMEM] * 4 + [VMEM, ANY, VMEM],
        out_specs=(VMEM, ANY),
        scratch_shapes=[pltpu.VMEM((stat_rows, 2 * S), f32)] * 3
        + [pltpu.VMEM((tokens, 2 * D), jnp.bfloat16)]
        + fetch_scratch
        + [pltpu.SemaphoreType.DMA((z_count,))],
        compiler_params=PARAMS,
        name="edge_stats",
    )(*lists, qd_group, kv_all, own)
    parts = exchange(stats, Y_AXIS)

    table, final, edge_mixed, *halves = pl.pallas_call(
        edge_grads_kernel,
        out_shape=(
            jax.ShapeDtypeStruct((cells * S, 2 * D), jnp.bfloat16),
            jax.ShapeDtypeStruct((3, group, 2 * S), f32),
            jax.ShapeDtypeStruct((tokens, 2 * D), f32),
        )
        + (jax.ShapeDtypeStruct((tokens, 2 * D), jnp.bfloat16),) * (y_count - 1),
        in_specs=[SMEM] * 6 + [VMEM, ANY, VMEM, ANY],
        out_specs=(ANY,) + (VMEM,) * (y_count + 1),
        scratch_shapes=[
            pltpu.VMEM((group * S, 2 * D), f32),
            pltpu.VMEM((S, 2 * D), f32),
            pltpu.VMEM((STAGES, S, 2 * D), jnp.bfloat16),
        ]
        + fetch_scratch
        + [pltpu.SemaphoreType.DMA((STAGES,))],
        input_output_aliases={9: 0},
        compiler_params=PARAMS,
        name="edge_grads",
    )(*lists, order_list, last_list, qd_group, kv_all, parts, cleared)
    returned = lax.psum_scatter(table, Z_AXIS, scatter_dimension=0, tiled=True)
    halves = [lax.ppermute(half, Y_AXIS, pairs) for half, pairs in zip(halves, backward)]
    rows_all = to_all(to_all(rows, Z_AXIS), Y_AXIS).reshape(ctx_count, 3, G)

    pairs, mixed, shared_grads = pl.pallas_call(
        own_grads_kernel,
        out_shape=(
            jax.ShapeDtypeStruct((tokens, 2 * D), f32),
            jax.ShapeDtypeStruct((tokens, 2 * D), f32),
            jax.ShapeDtypeStruct((2 * G, 2 * D), f32),
        ),
        in_specs=[SMEM] * 3 + [VMEM] * 6,
        out_specs=(VMEM, VMEM, VMEM),
        compiler_params=PARAMS,
        name="own_grads",
    )(meta, bias, flags, qd, kv, shared, final, rows_all, edge_mixed)

    summed = shared_grads.astype(jnp.bfloat16)
    for axis in (Y_AXIS, Z_AXIS):
        count = lax.axis_size(axis)
        summed = exchange(summed.reshape(count, -1, 2 * D), axis)
        summed = jnp.sum(summed.astype(f32), 0).astype(jnp.bfloat16)
    for axis in (Z_AXIS, Y_AXIS):
        summed = to_all(summed, axis).reshape(-1, 2 * D)
    shared_sums = summed.reshape(2, WORLDWIDE_COUNT, 1, S, 2 * D).astype(f32)

    mixed = sum([half.astype(f32) for half in halves], mixed).reshape(block_count, S, 2 * D)
    pairs = (returned.astype(f32) + pairs).reshape(block_count, S, 2 * D)
    for g in range(WORLDWIDE_COUNT):
        mask = hits[:, g][:, None, None]
        mixed = jnp.where(mask, shared_sums[1, g], mixed)
        pairs = pairs + jnp.where(mask, shared_sums[0, g], 0.0)
    mixed = mixed.reshape(tokens, 2 * D).astype(jnp.bfloat16)
    pairs = pairs.reshape(tokens, 2 * D).astype(jnp.bfloat16)
    return mixed[:, :D], mixed[:, D:], pairs[:, :D], pairs[:, D:]


def solution(mesh):
    torus = Mesh(mesh.devices.reshape(16, 4, mesh.shape["head"]), ("ctx_0", "ctx_1", "head"))
    return on_torus(torus)


def on_torus(torus):
    placed = (
        P(CTX_HEAD, None),
        P(CTX_HEAD, None),
        P(CTX_HEAD, None),
        P(CTX_HEAD, None),
        P(CTX, "head", None),
        P(),
    )
    return jax.shard_map(
        body,
        mesh=torus,
        in_specs=placed,
        out_specs=(P(CTX, "head"), P(CTX, "head"), P(CTX, "head"), P(CTX, "head")),
        check_vma=False,
    )
```

```python
import functools

import jax
import jax.numpy as jnp
from jax import lax
from jax.experimental import pallas as pl
from jax.experimental.pallas import tpu as pltpu
from jax.sharding import Mesh
from jax.sharding import PartitionSpec as P

FEATURE_LENGTH = 128
SPAN_TOKENS = 64
RANDOM = 3
WORLDWIDE_COUNT = 2
Z_AXIS = "ctx_0"
Y_AXIS = "ctx_1"
CTX = (Z_AXIS, Y_AXIS)
CTX_HEAD = (Z_AXIS, Y_AXIS, "head")
NEG = -1e30
SCALE = FEATURE_LENGTH ** (-0.5)
UNROLL = 8
DEPTH = 4
STAGES = 32
CODE = 32
SLOTS = 1 + RANDOM
D = FEATURE_LENGTH
S = SPAN_TOKENS
G = WORLDWIDE_COUNT * SPAN_TOKENS
VMEM = pl.BlockSpec(memory_space=pltpu.VMEM)
SMEM = pl.BlockSpec(memory_space=pltpu.SMEM)
ANY = pl.BlockSpec(memory_space=pl.ANY)
PARAMS = pltpu.CompilerParams(vmem_limit_bytes=56 * 2**20)


def dot_nt(a, b):
    return lax.dot_general(a, b, (((1,), (1,)), ((), ())), preferred_element_type=jnp.float32)


def dot_nn(a, b):
    return lax.dot_general(a, b, (((1,), (0,)), ((), ())), preferred_element_type=jnp.float32)


def dot_tn(a, b):
    return lax.dot_general(a, b, (((0,), (0,)), ((), ())), preferred_element_type=jnp.float32)


def list_masks(listed, block_total):
    inside = (listed >= 0) & (listed < block_total)
    kept = []
    for slot_pos in range(listed.shape[-1]):
        seen = jnp.zeros(listed.shape[:-1], dtype=jnp.bool_)
        for prior_pos in range(slot_pos):
            seen = seen | inside[..., prior_pos] & (listed[..., prior_pos] == listed[..., slot_pos])
        kept.append(inside[..., slot_pos] & jnp.logical_not(seen))
    return jnp.stack(kept, -1)


def exchange(array, axes):
    return lax.all_to_all(array, axes, split_axis=0, concat_axis=0, tiled=True)


def to_all(array, axes):
    count = lax.axis_size(axes)
    return exchange(jnp.broadcast_to(array[None], (count,) + array.shape), axes)


def by_head(first, second):
    rows = first.shape[0]
    heads = first.shape[1] // D
    both = jnp.concatenate([first.reshape(rows, heads, D), second.reshape(rows, heads, D)], 2)
    return exchange(both.transpose(1, 0, 2), "head").reshape(heads * rows, 2 * D)


def merge(parts):
    top = functools.reduce(jnp.maximum, [part[0] for part in parts])
    factors = [jnp.exp(part[0] - top) for part in parts]
    total = sum(part[1] * factor for part, factor in zip(parts, factors))
    slope = sum(part[2] * factor for part, factor in zip(parts, factors))
    return top, total, slope


def column_stats(scores, slopes):
    top = jnp.max(scores, axis=0, keepdims=True)
    weights = jnp.exp(scores - top)
    return (
        top,
        jnp.sum(weights, axis=0, keepdims=True),
        jnp.sum(weights * slopes, axis=0, keepdims=True),
    )


def own_scores(i, blocks, qd_ref, kv_ref, shared_ref, bias_ref):
    low = max(i - 1, 0) * S
    high = min(i + 2, blocks) * S
    q = qd_ref[i * S : (i + 1) * S, :D]
    dout = qd_ref[i * S : (i + 1) * S, D:]
    scores = dot_nt(kv_ref[low:high, :D], q) * SCALE
    slopes = dot_nt(kv_ref[low:high, D:], dout)
    global_scores = dot_nt(shared_ref[:, 2 * D : 3 * D], q) * SCALE
    global_scores = jnp.concatenate(
        [
            global_scores[g * S : (g + 1) * S] + bias_ref[i * WORLDWIDE_COUNT + g]
            for g in range(WORLDWIDE_COUNT)
        ],
        0,
    )
    global_slopes = dot_nt(shared_ref[:, 3 * D :], dout)
    return low, high, q, dout, scores, slopes, global_scores, global_slopes


def pick_kernel(index_ref, qd_ref, kv_ref, code_ref, out_ref, rows_ref, sems):
    blocks = qd_ref.shape[0] // S
    lanes = out_ref.shape[0]
    part = S // lanes
    copies = []
    for g in range(WORLDWIDE_COUNT):
        first = pl.multiple_of(lax.rem(index_ref[g], blocks) * S, S)
        for pos, ref in enumerate((qd_ref, kv_ref)):
            copies.append(
                pltpu.make_async_copy(
                    ref.at[pl.ds(first, S), :],
                    rows_ref.at[pl.ds(g * S, S), pl.ds(pos * 2 * D, 2 * D)],
                    sems.at[2 * g + pos],
                )
            )
    for copy in copies:
        copy.start()
    for lane in range(lanes):
        out_ref[lane, WORLDWIDE_COUNT * part :, :] = code_ref[...]
    for copy in copies:
        copy.wait()
    for lane in range(lanes):
        for g in range(WORLDWIDE_COUNT):
            low = g * S + lane * part
            out_ref[lane, g * part : (g + 1) * part, :] = rows_ref[low : low + part, :]


def own_stats_kernel(bias_ref, qd_ref, kv_ref, shared_ref, own_ref, rows_ref):
    tokens = qd_ref.shape[0]
    blocks = tokens // S
    for i in range(blocks):
        _, _, _, _, scores, slopes, global_scores, global_slopes = own_scores(
            i, blocks, qd_ref, kv_ref, shared_ref, bias_ref
        )
        top, total, slope = merge(
            [column_stats(scores, slopes), column_stats(global_scores, global_slopes)]
        )
        own_ref[0, i : i + 1, :] = top
        own_ref[1, i : i + 1, :] = total
        own_ref[2, i : i + 1, :] = slope
    parts = []
    for low in range(0, tokens, G):
        scores = dot_nt(kv_ref[low : low + G, :D], shared_ref[:, :D]) * SCALE
        slopes = dot_nt(kv_ref[low : low + G, D:], shared_ref[:, D : 2 * D])
        parts.append(column_stats(scores, slopes))
    top, total, slope = merge(parts)
    rows_ref[0:1, :] = top
    rows_ref[1:2, :] = total
    rows_ref[2:3, :] = slope


def cell_fetcher(meta_ref, cell_ref, kv_ref, fetch_ref, fetch_sems):
    def copies(t):
        found = []
        for u in range(UNROLL):
            buffer = lax.rem(t, DEPTH) * UNROLL + u
            cell = pl.multiple_of(cell_ref[t * UNROLL + u] * S, S)
            found.append(
                pltpu.make_async_copy(
                    kv_ref.at[pl.ds(cell, S), :], fetch_ref.at[buffer], fetch_sems.at[buffer]
                )
            )
        return found

    def start(t):
        @pl.when(t < meta_ref[0])
        def _():
            for copy in copies(t):
                copy.start()

    def wait(t):
        for copy in copies(t):
            copy.wait()

    return start, wait


def diagonal(qd):
    zeros = jnp.zeros((S, D), jnp.bfloat16)
    return jnp.concatenate(
        [jnp.concatenate([qd[:, :D], zeros], 1), jnp.concatenate([zeros, qd[:, D:]], 1)], 0
    )


def lane_scale():
    return jnp.where(lax.broadcasted_iota(jnp.int32, (1, 2 * S), 1) < S, SCALE, 1.0)


def edge_stats_kernel(
    meta_ref,
    slot_ref,
    item_ref,
    cell_ref,
    qd_ref,
    kv_ref,
    own_ref,
    out_ref,
    table_ref,
    top_ref,
    total_ref,
    slope_ref,
    zero_ref,
    fetch_ref,
    fetch_sems,
    zero_sems,
):
    group = qd_ref.shape[0] // S
    blocks = own_ref.shape[1]
    start, wait = cell_fetcher(meta_ref, cell_ref, kv_ref, fetch_ref, fetch_sems)
    for t in range(DEPTH):
        start(t)
    rows = zero_ref.shape[0]
    zero_ref[...] = jnp.zeros(zero_ref.shape, jnp.bfloat16)
    clears = [
        pltpu.make_async_copy(zero_ref, table_ref.at[pl.ds(i * rows, rows), :], zero_sems.at[i])
        for i in range(table_ref.shape[0] // rows)
    ]
    for clear in clears:
        clear.start()
    top_ref[...] = jnp.full(top_ref.shape, NEG, jnp.float32)
    total_ref[...] = jnp.zeros(total_ref.shape, jnp.float32)
    slope_ref[...] = jnp.zeros(slope_ref.shape, jnp.float32)
    factor = lane_scale()

    def step(t, carry):
        wait(t)
        found = []
        for u in range(UNROLL):
            pos = t * UNROLL + u
            item = pl.multiple_of(item_ref[pos] * S, S)
            pairs = fetch_ref[lax.rem(t, DEPTH) * UNROLL + u]
            both = dot_nt(pairs, diagonal(qd_ref[pl.ds(item, S), :])) * factor
            top = jnp.max(both, axis=0, keepdims=True)
            weights = jnp.exp(both - top)
            total = jnp.sum(weights, axis=0, keepdims=True)
            slope = jnp.sum(weights * pltpu.roll(both, S, 1), axis=0, keepdims=True)
            found.append((slot_ref[pos], top, total, slope))
        for slot, top, total, slope in found:
            top_ref[pl.ds(slot, 1), :] = top
            total_ref[pl.ds(slot, 1), :] = total
            slope_ref[pl.ds(slot, 1), :] = slope
        start(t + DEPTH)
        return carry

    lax.fori_loop(0, meta_ref[0], step, 0)
    mine = pl.multiple_of(SLOTS * group + meta_ref[1] * blocks, 8)
    top_ref[pl.ds(mine, blocks), :S] = own_ref[0]
    total_ref[pl.ds(mine, blocks), :S] = own_ref[1]
    slope_ref[pl.ds(mine, blocks), :S] = own_ref[2]
    top, total, slope = merge(
        [
            (
                top_ref[s * group : (s + 1) * group, :S],
                total_ref[s * group : (s + 1) * group, :S],
                slope_ref[s * group : (s + 1) * group, :S],
            )
            for s in range(SLOTS + 1)
        ]
    )
    first = jnp.concatenate([top, total], 1)
    second = jnp.concatenate([slope, slope], 1)
    for lane in range(out_ref.shape[0]):
        out_ref[lane, :group, :] = first
        out_ref[lane, group:, :] = second
    for clear in clears:
        clear.wait()


def edge_grads_kernel(
    meta_ref,
    slot_ref,
    item_ref,
    cell_ref,
    order_ref,
    mark_ref,
    qd_ref,
    kv_ref,
    parts_ref,
    cleared_ref,
    table_ref,
    final_ref,
    mixed_ref,
    *rest,
):
    sent_refs = rest[:-6]
    partial_ref, sum_ref, stage_ref, fetch_ref, fetch_sems, stage_sems = rest[-6:]
    group = qd_ref.shape[0] // S
    tokens = mixed_ref.shape[0]
    lanes = parts_ref.shape[0]
    start, wait = cell_fetcher(meta_ref, cell_ref, kv_ref, fetch_ref, fetch_sems)
    for t in range(DEPTH):
        start(t)
    top, total, slope = merge(
        [
            (
                parts_ref[lane, :group, :],
                pltpu.roll(parts_ref[lane, :group, :], S, 1),
                parts_ref[lane, group:, :],
            )
            for lane in range(lanes)
        ]
    )
    inverse = 1.0 / total
    final_ref[0] = top
    final_ref[1] = inverse
    final_ref[2] = slope * inverse
    partial_ref[...] = jnp.zeros(partial_ref.shape, jnp.float32)
    sum_ref[...] = jnp.zeros(sum_ref.shape, jnp.float32)
    factor = lane_scale()
    low_half = lax.broadcasted_iota(jnp.int32, (S, 2 * S), 1) < S

    def stage_copy(stage, cell):
        at = pl.ds(pl.multiple_of(cell * S, S), S)
        return pltpu.make_async_copy(stage_ref.at[stage], table_ref.at[at, :], stage_sems.at[stage])

    def step(t, carry):
        wait(t)
        for u in range(UNROLL):
            pos = t * UNROLL + u

            @pl.when(mark_ref[pos] >= 2)
            def _():
                stage_copy(lax.rem(order_ref[pos], STAGES), cell_ref[pos]).wait()

        found = []
        for u in range(UNROLL):
            pos = t * UNROLL + u
            slot = slot_ref[pos]
            live = slot < SLOTS * group
            row = pl.ds(lax.rem(slot, group), 1)
            item = pl.multiple_of(item_ref[pos] * S, S)
            pairs = fetch_ref[lax.rem(t, DEPTH) * UNROLL + u]
            corner = diagonal(qd_ref[pl.ds(item, S), :])
            both = dot_nt(pairs, corner) * factor
            prob = jnp.exp(both - final_ref[0, row, :]) * final_ref[1, row, :]
            dscore = prob * ((pltpu.roll(both, S, 1) - final_ref[2, row, :]) * SCALE)
            packed = jnp.where(low_half, dscore, pltpu.roll(prob, S, 1))
            packed = jnp.where(live, packed, 0.0).astype(jnp.bfloat16)
            found.append((pos, item, dot_nn(packed, corner), dot_tn(packed, pairs)))
        running = sum_ref[...]
        for pos, item, grads, crossed in found:
            fresh = order_ref[pos] != order_ref[jnp.maximum(pos - 1, 0)]
            running = grads + jnp.where(fresh, 0.0, running)
            stage_ref[lax.rem(order_ref[pos], STAGES)] = running.astype(jnp.bfloat16)
            at = pl.ds(item, S)
            partial_ref[at, :D] += crossed[S:, D:]
            partial_ref[at, D:] += crossed[:S, :D]
        sum_ref[...] = running
        for u in range(UNROLL):
            pos = t * UNROLL + u

            @pl.when(lax.rem(mark_ref[pos], 2) > 0)
            def _():
                stage_copy(lax.rem(order_ref[pos], STAGES), cell_ref[pos]).start()

        start(t + DEPTH)
        return carry

    lax.fori_loop(0, meta_ref[0], step, 0)
    mixed_ref[...] = partial_ref[:tokens, :]
    for shift, sent_ref in enumerate(sent_refs):
        low = (shift + 1) * tokens
        sent_ref[...] = partial_ref[low : low + tokens, :].astype(jnp.bfloat16)
    for stage in range(STAGES):

        @pl.when(stage < meta_ref[2])
        def _():
            stage_copy(stage, 0).wait()


def own_grads_kernel(
    meta_ref,
    bias_ref,
    flag_ref,
    qd_ref,
    kv_ref,
    shared_ref,
    final_ref,
    rows_ref,
    edge_ref,
    pairs_ref,
    mixed_ref,
    shared_grad_ref,
):
    tokens = qd_ref.shape[0]
    blocks = tokens // S
    first = meta_ref[1] * blocks
    rows = rows_ref[...]
    row_top = jnp.max(rows[:, 0:1, :], axis=0)
    factors = jnp.exp(rows[:, 0:1, :] - row_top[None])
    sums = jnp.sum(rows * factors, axis=0)
    row_inverse = 1.0 / sums[1:2]
    row_slope = sums[2:3] * row_inverse
    q = shared_ref[:, :D]
    dout = shared_ref[:, D : 2 * D]
    mixed = jnp.zeros((G, D), jnp.float32)
    dq = jnp.zeros((G, D), jnp.float32)
    for low in range(0, tokens, G):
        key = kv_ref[low : low + G, :D]
        value = kv_ref[low : low + G, D:]
        scores = dot_nt(key, q) * SCALE
        slopes = dot_nt(value, dout)
        prob = jnp.exp(scores - row_top) * row_inverse
        dscore = (prob * ((slopes - row_slope) * SCALE)).astype(jnp.bfloat16)
        prob = prob.astype(jnp.bfloat16)
        pairs_ref[low : low + G, :D] = dot_nn(dscore, q)
        pairs_ref[low : low + G, D:] = dot_nn(prob, dout)
        mixed = mixed + dot_tn(prob, value)
        dq = dq + dot_tn(dscore, key)
    shared_grad_ref[G:, :D] = mixed
    shared_grad_ref[G:, D:] = dq
    global_dkey = jnp.zeros((G, D), jnp.float32)
    global_dvalue = jnp.zeros((G, D), jnp.float32)
    for i in range(blocks):
        low, high, q, dout, scores, slopes, global_scores, global_slopes = own_scores(
            i, blocks, qd_ref, kv_ref, shared_ref, bias_ref
        )
        top = final_ref[0, pl.ds(first + i, 1), :S]
        inverse = final_ref[1, pl.ds(first + i, 1), :S] * flag_ref[i]
        slope = final_ref[2, pl.ds(first + i, 1), :S]

        def both(scores, slopes):
            prob = jnp.exp(scores - top) * inverse
            dscore = (prob * ((slopes - slope) * SCALE)).astype(jnp.bfloat16)
            return prob.astype(jnp.bfloat16), dscore

        prob, dscore = both(scores, slopes)
        global_prob, global_dscore = both(global_scores, global_slopes)
        pairs_ref[low:high, :D] += dot_nn(dscore, q)
        pairs_ref[low:high, D:] += dot_nn(prob, dout)
        global_dkey = global_dkey + dot_nn(global_dscore, q)
        global_dvalue = global_dvalue + dot_nn(global_prob, dout)
        at = slice(i * S, (i + 1) * S)
        mixed_ref[at, :D] = (
            edge_ref[at, :D]
            + dot_tn(prob, kv_ref[low:high, D:])
            + dot_tn(global_prob, shared_ref[:, 3 * D :])
        )
        mixed_ref[at, D:] = (
            edge_ref[at, D:]
            + dot_tn(dscore, kv_ref[low:high, :D])
            + dot_tn(global_dscore, shared_ref[:, 2 * D : 3 * D])
        )
    shared_grad_ref[:G, :D] = global_dkey
    shared_grad_ref[:G, D:] = global_dvalue


def body(query, key_in, value_in, grad_out, random_blocks, universal_segment_indices):
    f32 = jnp.float32
    z_count = lax.axis_size(Z_AXIS)
    y_count = lax.axis_size(Y_AXIS)
    ctx_count = z_count * y_count
    z_place = lax.axis_index(Z_AXIS)
    y_place = lax.axis_index(Y_AXIS)
    ctx_place = z_place * y_count + y_place

    kv = by_head(key_in, value_in)
    query, grad_out, random_blocks, kv = lax.optimization_barrier(
        (query, grad_out, random_blocks, kv)
    )
    kv_all = lax.all_gather(kv, Z_AXIS, axis=0, tiled=True)
    qd = by_head(query, grad_out)
    tokens = qd.shape[0]
    block_count = tokens // S
    group = block_count * y_count
    block_total = ctx_count * block_count
    cells = z_count * block_count

    part = S // y_count
    codes = random_blocks.reshape(1, -1)
    codes = jnp.concatenate([codes // CODE, codes % CODE], 1).astype(jnp.bfloat16)
    codes = jnp.pad(codes, ((0, 15), (0, 4 * D - codes.shape[1])))
    sent = pl.pallas_call(
        pick_kernel,
        out_shape=jax.ShapeDtypeStruct((y_count, WORLDWIDE_COUNT * part + 16, 4 * D), jnp.bfloat16),
        in_specs=[SMEM, ANY, ANY, VMEM],
        out_specs=VMEM,
        scratch_shapes=[
            pltpu.VMEM((G, 4 * D), jnp.bfloat16),
            pltpu.SemaphoreType.DMA((2 * WORLDWIDE_COUNT,)),
        ],
        compiler_params=PARAMS,
        name="pick",
    )(universal_segment_indices, qd, kv, codes)
    owners = universal_segment_indices // block_count

    def chosen(arrived, place):
        count = arrived.shape[0]
        mask = jnp.arange(count, dtype=jnp.int32)[:, None] == place[None]
        return jnp.sum(jnp.where(mask[:, :, None, None], arrived, 0), 0)

    arrived = exchange(sent, Y_AXIS)
    codes = arrived[:, WORLDWIDE_COUNT * part, : 2 * block_count * RANDOM]
    codes = codes.astype(jnp.int32).reshape(y_count, 2, block_count * RANDOM)
    random_group = (codes[:, 0] * CODE + codes[:, 1]).reshape(group, RANDOM)
    arrived = arrived[:, : WORLDWIDE_COUNT * part].reshape(y_count, WORLDWIDE_COUNT, part, 4 * D)
    qd_sent, arrived = lax.optimization_barrier((qd, arrived))
    picked = chosen(arrived, owners % y_count)
    sent = picked.reshape(WORLDWIDE_COUNT, z_count, -1, 4 * D).transpose(1, 0, 2, 3)
    picked = chosen(exchange(sent, Z_AXIS), owners // y_count)
    shared = to_all(picked, Z_AXIS).transpose(1, 0, 2, 3).reshape(WORLDWIDE_COUNT, part, 4 * D)
    shared = to_all(shared, Y_AXIS).transpose(1, 0, 2, 3).reshape(G, 4 * D)

    shifts = range(1, y_count)
    forward = [[(i, (i + shift) % y_count) for i in range(y_count)] for shift in shifts]
    backward = [[(i, (i - shift) % y_count) for i in range(y_count)] for shift in shifts]
    qd_group = jnp.concatenate(
        [qd] + [lax.ppermute(qd_sent, Y_AXIS, pairs) for pairs in forward], 0
    )

    ids = z_place * group + jnp.arange(group, dtype=jnp.int32)
    local = jnp.arange(group, dtype=jnp.int32) % block_count
    globals_ = jnp.broadcast_to(universal_segment_indices[None], (group, WORLDWIDE_COUNT))
    listed = jnp.concatenate(
        [jnp.stack([ids - 1, ids, ids + 1], 1), random_group, globals_], 1
    )
    kept = list_masks(listed, block_total)
    is_global = jnp.any(ids[:, None] == universal_segment_indices[None], 1)
    border = jnp.where(local == 0, ids - 1, jnp.where(local == block_count - 1, ids + 1, -1))
    named = jnp.concatenate([border[:, None], random_group], 1)
    valid = jnp.concatenate(
        [((border >= 0) & (border < block_total))[:, None], kept[:, 3 : 3 + RANDOM]], 1
    )
    lane = named // block_count % y_count
    valid = valid & jnp.logical_not(is_global)[:, None] & (lane == y_place)
    cell = named // group * block_count + named % block_count
    valid = valid.T.reshape(-1)
    cell = cell.T.reshape(-1)
    entries = SLOTS * group
    order = jnp.arange(entries, dtype=jnp.int32)
    label = cell * entries + order
    rank = jnp.sum((valid[None, :] & (label[None, :] < label[:, None])).astype(jnp.int32), 1)
    edge_count = jnp.sum(valid.astype(jnp.int32))
    hit = (rank[None, :] == order[:, None]) & valid[None, :]
    slot_list = jnp.sum(jnp.where(hit, order[None, :], 0), 1)
    cell_list = jnp.sum(jnp.where(hit, cell[None, :], 0), 1)
    real = order < edge_count
    fresh = real & ((order == 0) | (cell_list != jnp.roll(cell_list, 1)))
    last_list = real & ((order == edge_count - 1) | (cell_list != jnp.roll(cell_list, -1)))
    order_list = jnp.sum((fresh[None, :] & (order[None, :] <= order[:, None])).astype(jnp.int32), 1) - 1
    slot_list = jnp.where(real, slot_list, entries + group)
    item_list = slot_list % group
    item_list = (y_place - item_list // block_count) % y_count * block_count + item_list % block_count
    mark_list = last_list.astype(jnp.int32) + 2 * (fresh & (order_list >= STAGES))
    meta = jnp.stack(
        [(edge_count + UNROLL - 1) // UNROLL, y_place, jnp.sum(fresh.astype(jnp.int32))]
    ).astype(jnp.int32)
    lists = (meta, slot_list, item_list, cell_list)

    own_first = y_place * block_count
    own_kept = lax.dynamic_slice_in_dim(kept, own_first, block_count, 0)
    bias = jnp.where(own_kept[:, 3 + RANDOM :], 0.0, NEG).astype(f32).reshape(-1)
    own_ids = ctx_place * block_count + jnp.arange(block_count, dtype=jnp.int32)
    hits = own_ids[:, None] == universal_segment_indices[None]
    flags = jnp.where(jnp.any(hits, 1), 0.0, 1.0).astype(f32)

    own, rows = pl.pallas_call(
        own_stats_kernel,
        out_shape=(
            jax.ShapeDtypeStruct((3, block_count, S), f32),
            jax.ShapeDtypeStruct((3, G), f32),
        ),
        in_specs=[SMEM, VMEM, VMEM, VMEM],
        out_specs=(VMEM, VMEM),
        compiler_params=PARAMS,
        name="own_stats",
    )(bias, qd, kv, shared)

    stat_rows = (SLOTS + 1) * group + 8
    fetch_scratch = [
        pltpu.VMEM((DEPTH * UNROLL, S, 2 * D), jnp.bfloat16),
        pltpu.SemaphoreType.DMA((DEPTH * UNROLL,)),
    ]
    stats, cleared = pl.pallas_call(
        edge_stats_kernel,
        out_shape=(
            jax.ShapeDtypeStruct((y_count, 2 * group, 2 * S), f32),
            jax.ShapeDtypeStruct((cells * S, 2 * D), jnp.bfloat16),
        ),
        in_specs=[SMEM] * 4 + [VMEM, ANY, VMEM],
        out_specs=(VMEM, ANY),
        scratch_shapes=[pltpu.VMEM((stat_rows, 2 * S), f32)] * 3
        + [pltpu.VMEM((tokens, 2 * D), jnp.bfloat16)]
        + fetch_scratch
        + [pltpu.SemaphoreType.DMA((z_count,))],
        compiler_params=PARAMS,
        name="edge_stats",
    )(*lists, qd_group, kv_all, own)
    parts = exchange(stats, Y_AXIS)

    table, final, edge_mixed, *halves = pl.pallas_call(
        edge_grads_kernel,
        out_shape=(
            jax.ShapeDtypeStruct((cells * S, 2 * D), jnp.bfloat16),
            jax.ShapeDtypeStruct((3, group, 2 * S), f32),
            jax.ShapeDtypeStruct((tokens, 2 * D), f32),
        )
        + (jax.ShapeDtypeStruct((tokens, 2 * D), jnp.bfloat16),) * (y_count - 1),
        in_specs=[SMEM] * 6 + [VMEM, ANY, VMEM, ANY],
        out_specs=(ANY,) + (VMEM,) * (y_count + 1),
        scratch_shapes=[
            pltpu.VMEM((group * S, 2 * D), f32),
            pltpu.VMEM((S, 2 * D), f32),
            pltpu.VMEM((STAGES, S, 2 * D), jnp.bfloat16),
        ]
        + fetch_scratch
        + [pltpu.SemaphoreType.DMA((STAGES,))],
        input_output_aliases={9: 0},
        compiler_params=PARAMS,
        name="edge_grads",
    )(*lists, order_list, mark_list, qd_group, kv_all, parts, cleared)
    returned = lax.psum_scatter(table, Z_AXIS, scatter_dimension=0, tiled=True)
    halves = [lax.ppermute(half, Y_AXIS, pairs) for half, pairs in zip(halves, backward)]
    rows_all = to_all(to_all(rows, Z_AXIS), Y_AXIS).reshape(ctx_count, 3, G)

    pairs, mixed, shared_grads = pl.pallas_call(
        own_grads_kernel,
        out_shape=(
            jax.ShapeDtypeStruct((tokens, 2 * D), f32),
            jax.ShapeDtypeStruct((tokens, 2 * D), f32),
            jax.ShapeDtypeStruct((2 * G, 2 * D), f32),
        ),
        in_specs=[SMEM] * 3 + [VMEM] * 6,
        out_specs=(VMEM, VMEM, VMEM),
        compiler_params=PARAMS,
        name="own_grads",
    )(meta, bias, flags, qd, kv, shared, final, rows_all, edge_mixed)

    summed = shared_grads.astype(jnp.bfloat16)
    for axis in (Y_AXIS, Z_AXIS):
        count = lax.axis_size(axis)
        summed = exchange(summed.reshape(count, -1, 2 * D), axis)
        summed = jnp.sum(summed.astype(f32), 0).astype(jnp.bfloat16)
    for axis in (Z_AXIS, Y_AXIS):
        summed = to_all(summed, axis).reshape(-1, 2 * D)
    shared_sums = summed.reshape(2, WORLDWIDE_COUNT, 1, S, 2 * D).astype(f32)

    mixed = sum([half.astype(f32) for half in halves], mixed).reshape(block_count, S, 2 * D)
    pairs = (returned.astype(f32) + pairs).reshape(block_count, S, 2 * D)
    for g in range(WORLDWIDE_COUNT):
        mask = hits[:, g][:, None, None]
        mixed = jnp.where(mask, shared_sums[1, g], mixed)
        pairs = pairs + jnp.where(mask, shared_sums[0, g], 0.0)
    mixed = mixed.reshape(tokens, 2 * D).astype(jnp.bfloat16)
    pairs = pairs.reshape(tokens, 2 * D).astype(jnp.bfloat16)
    return mixed[:, :D], mixed[:, D:], pairs[:, :D], pairs[:, D:]


def solution(mesh):
    torus = Mesh(mesh.devices.reshape(16, 4, mesh.shape["head"]), ("ctx_0", "ctx_1", "head"))
    return on_torus(torus)


def on_torus(torus):
    placed = (
        P(CTX_HEAD, None),
        P(CTX_HEAD, None),
        P(CTX_HEAD, None),
        P(CTX_HEAD, None),
        P(CTX, "head", None),
        P(),
    )
    return jax.shard_map(
        body,
        mesh=torus,
        in_specs=placed,
        out_specs=(P(CTX, "head"), P(CTX, "head"), P(CTX, "head"), P(CTX, "head")),
        check_vma=False,
    )
```

```python
import functools

import jax
import jax.numpy as jnp
from jax import lax
from jax.experimental import pallas as pl
from jax.experimental.pallas import tpu as pltpu
from jax.sharding import Mesh
from jax.sharding import PartitionSpec as P

FEATURE_LENGTH = 128
SPAN_TOKENS = 64
RANDOM = 3
WORLDWIDE_COUNT = 2
Z_AXIS = "ctx_0"
Y_AXIS = "ctx_1"
CTX = (Z_AXIS, Y_AXIS)
CTX_HEAD = (Z_AXIS, Y_AXIS, "head")
NEG = -1e30
SCALE = FEATURE_LENGTH ** (-0.5)
UNROLL = 8
DEPTH = 4
STAGES = 32
CODE = 32
LOG2E = 1.4426950408889634
SLOTS = 1 + RANDOM
D = FEATURE_LENGTH
S = SPAN_TOKENS
G = WORLDWIDE_COUNT * SPAN_TOKENS
VMEM = pl.BlockSpec(memory_space=pltpu.VMEM)
SMEM = pl.BlockSpec(memory_space=pltpu.SMEM)
ANY = pl.BlockSpec(memory_space=pl.ANY)
PARAMS = pltpu.CompilerParams(vmem_limit_bytes=56 * 2**20)


def dot_nt(a, b):
    return lax.dot_general(a, b, (((1,), (1,)), ((), ())), preferred_element_type=jnp.float32)


def dot_nn(a, b):
    return lax.dot_general(a, b, (((1,), (0,)), ((), ())), preferred_element_type=jnp.float32)


def dot_tn(a, b):
    return lax.dot_general(a, b, (((0,), (0,)), ((), ())), preferred_element_type=jnp.float32)


def list_masks(listed, block_total):
    inside = (listed >= 0) & (listed < block_total)
    kept = []
    for slot_pos in range(listed.shape[-1]):
        seen = jnp.zeros(listed.shape[:-1], dtype=jnp.bool_)
        for prior_pos in range(slot_pos):
            seen = seen | inside[..., prior_pos] & (listed[..., prior_pos] == listed[..., slot_pos])
        kept.append(inside[..., slot_pos] & jnp.logical_not(seen))
    return jnp.stack(kept, -1)


def exchange(array, axes):
    return lax.all_to_all(array, axes, split_axis=0, concat_axis=0, tiled=True)


def to_all(array, axes):
    count = lax.axis_size(axes)
    return exchange(jnp.broadcast_to(array[None], (count,) + array.shape), axes)


def by_head(first, second):
    rows = first.shape[0]
    heads = first.shape[1] // D
    both = jnp.concatenate([first.reshape(rows, heads, D), second.reshape(rows, heads, D)], 2)
    return exchange(both.transpose(1, 0, 2), "head").reshape(heads * rows, 2 * D)


def merge(parts):
    top = functools.reduce(jnp.maximum, [part[0] for part in parts])
    factors = [jnp.exp(part[0] - top) for part in parts]
    total = sum(part[1] * factor for part, factor in zip(parts, factors))
    slope = sum(part[2] * factor for part, factor in zip(parts, factors))
    return top, total, slope


def column_stats(scores, slopes):
    top = jnp.max(scores, axis=0, keepdims=True)
    weights = jnp.exp(scores - top)
    return (
        top,
        jnp.sum(weights, axis=0, keepdims=True),
        jnp.sum(weights * slopes, axis=0, keepdims=True),
    )


def own_scores(i, blocks, qd_ref, kv_ref, shared_ref, bias_ref):
    low = max(i - 1, 0) * S
    high = min(i + 2, blocks) * S
    q = qd_ref[i * S : (i + 1) * S, :D]
    dout = qd_ref[i * S : (i + 1) * S, D:]
    scores = dot_nt(kv_ref[low:high, :D], q) * SCALE
    slopes = dot_nt(kv_ref[low:high, D:], dout)
    global_scores = dot_nt(shared_ref[:, 2 * D : 3 * D], q) * SCALE
    global_scores = jnp.concatenate(
        [
            global_scores[g * S : (g + 1) * S] + bias_ref[i * WORLDWIDE_COUNT + g]
            for g in range(WORLDWIDE_COUNT)
        ],
        0,
    )
    global_slopes = dot_nt(shared_ref[:, 3 * D :], dout)
    return low, high, q, dout, scores, slopes, global_scores, global_slopes


def pick_kernel(index_ref, qd_ref, kv_ref, code_ref, out_ref, rows_ref, sems):
    blocks = qd_ref.shape[0] // S
    lanes = out_ref.shape[0]
    part = S // lanes
    copies = []
    for g in range(WORLDWIDE_COUNT):
        first = pl.multiple_of(lax.rem(index_ref[g], blocks) * S, S)
        for pos, ref in enumerate((qd_ref, kv_ref)):
            copies.append(
                pltpu.make_async_copy(
                    ref.at[pl.ds(first, S), :],
                    rows_ref.at[pl.ds(g * S, S), pl.ds(pos * 2 * D, 2 * D)],
                    sems.at[2 * g + pos],
                )
            )
    for copy in copies:
        copy.start()
    for lane in range(lanes):
        out_ref[lane, WORLDWIDE_COUNT * part :, :] = code_ref[...]
    for copy in copies:
        copy.wait()
    for lane in range(lanes):
        for g in range(WORLDWIDE_COUNT):
            low = g * S + lane * part
            out_ref[lane, g * part : (g + 1) * part, :] = rows_ref[low : low + part, :]


def own_stats_kernel(bias_ref, qd_ref, kv_ref, shared_ref, own_ref, rows_ref):
    tokens = qd_ref.shape[0]
    blocks = tokens // S
    for i in range(blocks):
        _, _, _, _, scores, slopes, global_scores, global_slopes = own_scores(
            i, blocks, qd_ref, kv_ref, shared_ref, bias_ref
        )
        top, total, slope = merge(
            [column_stats(scores, slopes), column_stats(global_scores, global_slopes)]
        )
        own_ref[0, i : i + 1, :] = top
        own_ref[1, i : i + 1, :] = total
        own_ref[2, i : i + 1, :] = slope
    parts = []
    for low in range(0, tokens, G):
        scores = dot_nt(kv_ref[low : low + G, :D], shared_ref[:, :D]) * SCALE
        slopes = dot_nt(kv_ref[low : low + G, D:], shared_ref[:, D : 2 * D])
        parts.append(column_stats(scores, slopes))
    top, total, slope = merge(parts)
    rows_ref[0:1, :] = top
    rows_ref[1:2, :] = total
    rows_ref[2:3, :] = slope


def cell_fetcher(meta_ref, cell_ref, kv_ref, fetch_ref, fetch_sems):
    def start(t):
        @pl.when(t < meta_ref[0])
        def _():
            bank = t & (DEPTH - 1)
            for u in range(UNROLL):
                cell = pl.multiple_of(cell_ref[t * UNROLL + u] * S, S)
                pltpu.make_async_copy(
                    kv_ref.at[pl.ds(cell, S), :],
                    fetch_ref.at[bank, pl.ds(u * S, S), :],
                    fetch_sems.at[bank],
                ).start()

    def wait(t):
        bank = t & (DEPTH - 1)
        pltpu.make_async_copy(
            kv_ref.at[pl.ds(0, UNROLL * S), :], fetch_ref.at[bank], fetch_sems.at[bank]
        ).wait()

    return start, wait


def diagonal(qd):
    zeros = jnp.zeros((S, D), jnp.bfloat16)
    return jnp.concatenate(
        [jnp.concatenate([qd[:, :D], zeros], 1), jnp.concatenate([zeros, qd[:, D:]], 1)], 0
    )


def lane_scale(low, high):
    return jnp.where(lax.broadcasted_iota(jnp.int32, (1, 2 * S), 1) < S, low, high)


def edge_stats_kernel(
    meta_ref,
    slot_ref,
    item_ref,
    cell_ref,
    qd_ref,
    kv_ref,
    own_ref,
    out_ref,
    table_ref,
    top_ref,
    total_ref,
    slope_ref,
    zero_ref,
    fetch_ref,
    fetch_sems,
    zero_sems,
):
    group = qd_ref.shape[0] // S
    blocks = own_ref.shape[1]
    start, wait = cell_fetcher(meta_ref, cell_ref, kv_ref, fetch_ref, fetch_sems)
    for t in range(DEPTH):
        start(t)
    rows = zero_ref.shape[0]
    zero_ref[...] = jnp.zeros(zero_ref.shape, jnp.bfloat16)
    clears = [
        pltpu.make_async_copy(zero_ref, table_ref.at[pl.ds(i * rows, rows), :], zero_sems.at[i])
        for i in range(table_ref.shape[0] // rows)
    ]
    for clear in clears:
        clear.start()
    top_ref[...] = jnp.full(top_ref.shape, NEG, jnp.float32)
    total_ref[...] = jnp.zeros(total_ref.shape, jnp.float32)
    slope_ref[...] = jnp.zeros(slope_ref.shape, jnp.float32)
    factor = lane_scale(SCALE, 1.0)

    def step(t, carry):
        wait(t)
        found = []
        for u in range(UNROLL):
            pos = t * UNROLL + u
            item = pl.multiple_of(item_ref[pos] * S, S)
            pairs = fetch_ref[t & (DEPTH - 1), u * S : (u + 1) * S, :]
            both = dot_nt(pairs, diagonal(qd_ref[pl.ds(item, S), :])) * factor
            top = jnp.max(both, axis=0, keepdims=True)
            weights = jnp.exp(both - top)
            total = jnp.sum(weights, axis=0, keepdims=True)
            slope = jnp.sum(weights * pltpu.roll(both, S, 1), axis=0, keepdims=True)
            found.append((slot_ref[pos], top, total, slope))
        for slot, top, total, slope in found:
            top_ref[pl.ds(slot, 1), :] = top
            total_ref[pl.ds(slot, 1), :] = total
            slope_ref[pl.ds(slot, 1), :] = slope
        start(t + DEPTH)
        return carry

    lax.fori_loop(0, meta_ref[0], step, 0)
    mine = pl.multiple_of(SLOTS * group + meta_ref[1] * blocks, 8)
    top_ref[pl.ds(mine, blocks), :S] = own_ref[0]
    total_ref[pl.ds(mine, blocks), :S] = own_ref[1]
    slope_ref[pl.ds(mine, blocks), :S] = own_ref[2]
    top, total, slope = merge(
        [
            (
                top_ref[s * group : (s + 1) * group, :S],
                total_ref[s * group : (s + 1) * group, :S],
                slope_ref[s * group : (s + 1) * group, :S],
            )
            for s in range(SLOTS + 1)
        ]
    )
    first = jnp.concatenate([top, total], 1)
    second = jnp.concatenate([slope, slope], 1)
    for lane in range(out_ref.shape[0]):
        out_ref[lane, :group, :] = first
        out_ref[lane, group:, :] = second
    for clear in clears:
        clear.wait()


def edge_grads_kernel(
    meta_ref,
    row_ref,
    item_ref,
    cell_ref,
    stage_pos_ref,
    fresh_ref,
    last_ref,
    reuse_ref,
    qd_ref,
    kv_ref,
    parts_ref,
    cleared_ref,
    table_ref,
    final_ref,
    mixed_ref,
    *rest,
):
    sent_refs = rest[:-6]
    partial_ref, sum_ref, stage_ref, fetch_ref, fetch_sems, stage_sems = rest[-6:]
    group = qd_ref.shape[0] // S
    tokens = mixed_ref.shape[0]
    lanes = parts_ref.shape[0]
    start, wait = cell_fetcher(meta_ref, cell_ref, kv_ref, fetch_ref, fetch_sems)
    for t in range(DEPTH):
        start(t)
    top, total, slope = merge(
        [
            (
                parts_ref[lane, :group, :],
                pltpu.roll(parts_ref[lane, :group, :], S, 1),
                parts_ref[lane, group:, :],
            )
            for lane in range(lanes)
        ]
    )
    inverse = 1.0 / total
    final_ref[0, :group, :] = top * LOG2E
    final_ref[1, :group, :] = inverse
    final_ref[2, :group, :] = slope * inverse * SCALE
    final_ref[0, group:, :] = jnp.full((8, 2 * S), -NEG, jnp.float32)
    final_ref[1:, group:, :] = jnp.zeros((2, 8, 2 * S), jnp.float32)
    partial_ref[...] = jnp.zeros(partial_ref.shape, jnp.float32)
    sum_ref[...] = jnp.zeros(sum_ref.shape, jnp.float32)
    factor = lane_scale(SCALE * LOG2E, SCALE)
    low_half = lax.broadcasted_iota(jnp.int32, (S, 2 * S), 1) < S

    def stage_copy(stage, cell):
        at = pl.ds(pl.multiple_of(cell * S, S), S)
        return pltpu.make_async_copy(stage_ref.at[stage], table_ref.at[at, :], stage_sems.at[stage])

    def step(t, carry):
        wait(t)
        for u in range(UNROLL):
            pos = t * UNROLL + u

            @pl.when(reuse_ref[pos] > 0)
            def _():
                stage_copy(stage_pos_ref[pos], 0).wait()

        found = []
        for u in range(UNROLL):
            pos = t * UNROLL + u
            row = pl.ds(row_ref[pos], 1)
            item = pl.multiple_of(item_ref[pos] * S, S)
            pairs = fetch_ref[t & (DEPTH - 1), u * S : (u + 1) * S, :]
            corner = diagonal(qd_ref[pl.ds(item, S), :])
            both = dot_nt(pairs, corner) * factor
            prob = jnp.exp2(both - final_ref[0, row, :]) * final_ref[1, row, :]
            dscore = prob * (pltpu.roll(both, S, 1) - final_ref[2, row, :])
            packed = jnp.where(low_half, dscore, pltpu.roll(prob, S, 1)).astype(jnp.bfloat16)
            found.append((pos, item, jnp.concatenate([dot_nn(packed[:, :S], corner[:S, :D]), dot_nn(packed[:, S:], corner[S:, D:])], 1), dot_tn(packed[:, S:], pairs[:, D:]), dot_tn(packed[:, :S], pairs[:, :D])))
        running = sum_ref[...]
        for pos, item, grads, mixed, dq in found:
            running = grads + jnp.where(fresh_ref[pos] > 0, 0.0, running)
            stage_ref[stage_pos_ref[pos]] = running.astype(jnp.bfloat16)
            at = pl.ds(item, S)
            partial_ref[at, :D] += mixed
            partial_ref[at, D:] += dq
        sum_ref[...] = running
        for u in range(UNROLL):
            pos = t * UNROLL + u

            @pl.when(last_ref[pos] > 0)
            def _():
                stage_copy(stage_pos_ref[pos], cell_ref[pos]).start()

        start(t + DEPTH)
        return carry

    lax.fori_loop(0, meta_ref[0], step, 0)
    mixed_ref[...] = partial_ref[:tokens, :]
    for shift, sent_ref in enumerate(sent_refs):
        low = (shift + 1) * tokens
        sent_ref[...] = partial_ref[low : low + tokens, :].astype(jnp.bfloat16)
    for stage in range(STAGES):

        @pl.when(stage < meta_ref[2])
        def _():
            stage_copy(stage, 0).wait()


def own_grads_kernel(
    meta_ref,
    bias_ref,
    flag_ref,
    qd_ref,
    kv_ref,
    shared_ref,
    final_ref,
    rows_ref,
    edge_ref,
    pairs_ref,
    mixed_ref,
    shared_grad_ref,
):
    tokens = qd_ref.shape[0]
    blocks = tokens // S
    first = meta_ref[1] * blocks
    rows = rows_ref[...]
    row_top = jnp.max(rows[:, 0:1, :], axis=0)
    factors = jnp.exp(rows[:, 0:1, :] - row_top[None])
    sums = jnp.sum(rows * factors, axis=0)
    row_inverse = 1.0 / sums[1:2]
    row_slope = sums[2:3] * row_inverse
    q = shared_ref[:, :D]
    dout = shared_ref[:, D : 2 * D]
    mixed = jnp.zeros((G, D), jnp.float32)
    dq = jnp.zeros((G, D), jnp.float32)
    for low in range(0, tokens, G):
        key = kv_ref[low : low + G, :D]
        value = kv_ref[low : low + G, D:]
        scores = dot_nt(key, q) * SCALE
        slopes = dot_nt(value, dout)
        prob = jnp.exp(scores - row_top) * row_inverse
        dscore = (prob * ((slopes - row_slope) * SCALE)).astype(jnp.bfloat16)
        prob = prob.astype(jnp.bfloat16)
        pairs_ref[low : low + G, :D] = dot_nn(dscore, q)
        pairs_ref[low : low + G, D:] = dot_nn(prob, dout)
        mixed = mixed + dot_tn(prob, value)
        dq = dq + dot_tn(dscore, key)
    shared_grad_ref[G:, :D] = mixed
    shared_grad_ref[G:, D:] = dq
    global_dkey = jnp.zeros((G, D), jnp.float32)
    global_dvalue = jnp.zeros((G, D), jnp.float32)
    for i in range(blocks):
        low, high, q, dout, scores, slopes, global_scores, global_slopes = own_scores(
            i, blocks, qd_ref, kv_ref, shared_ref, bias_ref
        )
        top = final_ref[0, pl.ds(first + i, 1), :S]
        inverse = final_ref[1, pl.ds(first + i, 1), :S] * flag_ref[i]
        slope = final_ref[2, pl.ds(first + i, 1), :S]

        def both(scores, slopes):
            prob = jnp.exp2(scores * LOG2E - top) * inverse
            dscore = (prob * (slopes * SCALE - slope)).astype(jnp.bfloat16)
            return prob.astype(jnp.bfloat16), dscore

        prob, dscore = both(scores, slopes)
        global_prob, global_dscore = both(global_scores, global_slopes)
        pairs_ref[low:high, :D] += dot_nn(dscore, q)
        pairs_ref[low:high, D:] += dot_nn(prob, dout)
        global_dkey = global_dkey + dot_nn(global_dscore, q)
        global_dvalue = global_dvalue + dot_nn(global_prob, dout)
        at = slice(i * S, (i + 1) * S)
        mixed_ref[at, :D] = (
            edge_ref[at, :D]
            + dot_tn(prob, kv_ref[low:high, D:])
            + dot_tn(global_prob, shared_ref[:, 3 * D :])
        )
        mixed_ref[at, D:] = (
            edge_ref[at, D:]
            + dot_tn(dscore, kv_ref[low:high, :D])
            + dot_tn(global_dscore, shared_ref[:, 2 * D : 3 * D])
        )
    shared_grad_ref[:G, :D] = global_dkey
    shared_grad_ref[:G, D:] = global_dvalue


def body(query, key_in, value_in, grad_out, random_blocks, universal_segment_indices):
    f32 = jnp.float32
    z_count = lax.axis_size(Z_AXIS)
    y_count = lax.axis_size(Y_AXIS)
    ctx_count = z_count * y_count
    z_place = lax.axis_index(Z_AXIS)
    y_place = lax.axis_index(Y_AXIS)
    ctx_place = z_place * y_count + y_place

    kv = by_head(key_in, value_in)
    query, grad_out, random_blocks, kv = lax.optimization_barrier(
        (query, grad_out, random_blocks, kv)
    )
    kv_all = lax.all_gather(kv, Z_AXIS, axis=0, tiled=True)
    qd = by_head(query, grad_out)
    tokens = qd.shape[0]
    block_count = tokens // S
    group = block_count * y_count
    block_total = ctx_count * block_count
    cells = z_count * block_count

    part = S // y_count
    codes = random_blocks.reshape(1, -1)
    codes = jnp.concatenate([codes // CODE, codes % CODE], 1).astype(jnp.bfloat16)
    codes = jnp.pad(codes, ((0, 15), (0, 4 * D - codes.shape[1])))
    sent = pl.pallas_call(
        pick_kernel,
        out_shape=jax.ShapeDtypeStruct((y_count, WORLDWIDE_COUNT * part + 16, 4 * D), jnp.bfloat16),
        in_specs=[SMEM, ANY, ANY, VMEM],
        out_specs=VMEM,
        scratch_shapes=[
            pltpu.VMEM((G, 4 * D), jnp.bfloat16),
            pltpu.SemaphoreType.DMA((2 * WORLDWIDE_COUNT,)),
        ],
        compiler_params=PARAMS,
        name="pick",
    )(universal_segment_indices, qd, kv, codes)
    owners = universal_segment_indices // block_count

    def chosen(arrived, place):
        count = arrived.shape[0]
        mask = jnp.arange(count, dtype=jnp.int32)[:, None] == place[None]
        return jnp.sum(jnp.where(mask[:, :, None, None], arrived, 0), 0)

    arrived = exchange(sent, Y_AXIS)
    codes = arrived[:, WORLDWIDE_COUNT * part, : 2 * block_count * RANDOM]
    codes = codes.astype(jnp.int32).reshape(y_count, 2, block_count * RANDOM)
    random_group = (codes[:, 0] * CODE + codes[:, 1]).reshape(group, RANDOM)
    arrived = arrived[:, : WORLDWIDE_COUNT * part].reshape(y_count, WORLDWIDE_COUNT, part, 4 * D)
    qd_sent, arrived = lax.optimization_barrier((qd, arrived))
    picked = chosen(arrived, owners % y_count)
    sent = picked.reshape(WORLDWIDE_COUNT, z_count, -1, 4 * D).transpose(1, 0, 2, 3)
    picked = chosen(exchange(sent, Z_AXIS), owners // y_count)
    shared = to_all(picked, Z_AXIS).transpose(1, 0, 2, 3).reshape(WORLDWIDE_COUNT, part, 4 * D)
    shared = to_all(shared, Y_AXIS).transpose(1, 0, 2, 3).reshape(G, 4 * D)

    shifts = range(1, y_count)
    forward = [[(i, (i + shift) % y_count) for i in range(y_count)] for shift in shifts]
    backward = [[(i, (i - shift) % y_count) for i in range(y_count)] for shift in shifts]
    qd_group = jnp.concatenate(
        [qd] + [lax.ppermute(qd_sent, Y_AXIS, pairs) for pairs in forward], 0
    )

    ids = z_place * group + jnp.arange(group, dtype=jnp.int32)
    local = jnp.arange(group, dtype=jnp.int32) % block_count
    globals_ = jnp.broadcast_to(universal_segment_indices[None], (group, WORLDWIDE_COUNT))
    listed = jnp.concatenate(
        [jnp.stack([ids - 1, ids, ids + 1], 1), random_group, globals_], 1
    )
    kept = list_masks(listed, block_total)
    is_global = jnp.any(ids[:, None] == universal_segment_indices[None], 1)
    border = jnp.where(local == 0, ids - 1, jnp.where(local == block_count - 1, ids + 1, -1))
    named = jnp.concatenate([border[:, None], random_group], 1)
    valid = jnp.concatenate(
        [((border >= 0) & (border < block_total))[:, None], kept[:, 3 : 3 + RANDOM]], 1
    )
    lane = named // block_count % y_count
    valid = valid & jnp.logical_not(is_global)[:, None] & (lane == y_place)
    cell = named // group * block_count + named % block_count
    valid = valid.T.reshape(-1)
    cell = cell.T.reshape(-1)
    entries = SLOTS * group
    order = jnp.arange(entries, dtype=jnp.int32)
    label = cell * entries + order
    rank = jnp.sum((valid[None, :] & (label[None, :] < label[:, None])).astype(jnp.int32), 1)
    edge_count = jnp.sum(valid.astype(jnp.int32))
    hit = (rank[None, :] == order[:, None]) & valid[None, :]
    slot_list = jnp.sum(jnp.where(hit, order[None, :], 0), 1)
    cell_list = jnp.sum(jnp.where(hit, cell[None, :], 0), 1)
    real = order < edge_count
    fresh = real & ((order == 0) | (cell_list != jnp.roll(cell_list, 1)))
    last_list = real & ((order == edge_count - 1) | (cell_list != jnp.roll(cell_list, -1)))
    order_list = jnp.sum((fresh[None, :] & (order[None, :] <= order[:, None])).astype(jnp.int32), 1) - 1
    slot_list = jnp.where(real, slot_list, entries + group)
    item_list = slot_list % group
    item_list = (y_place - item_list // block_count) % y_count * block_count + item_list % block_count
    row_list = jnp.where(real, slot_list % group, group)
    grad_lists = (
        row_list,
        order_list % STAGES,
        fresh.astype(jnp.int32),
        last_list.astype(jnp.int32),
        (fresh & (order_list >= STAGES)).astype(jnp.int32),
    )
    meta = jnp.stack(
        [(edge_count + UNROLL - 1) // UNROLL, y_place, jnp.sum(fresh.astype(jnp.int32))]
    ).astype(jnp.int32)
    lists = (meta, slot_list, item_list, cell_list)

    own_first = y_place * block_count
    own_kept = lax.dynamic_slice_in_dim(kept, own_first, block_count, 0)
    bias = jnp.where(own_kept[:, 3 + RANDOM :], 0.0, NEG).astype(f32).reshape(-1)
    own_ids = ctx_place * block_count + jnp.arange(block_count, dtype=jnp.int32)
    hits = own_ids[:, None] == universal_segment_indices[None]
    flags = jnp.where(jnp.any(hits, 1), 0.0, 1.0).astype(f32)

    own, rows = pl.pallas_call(
        own_stats_kernel,
        out_shape=(
            jax.ShapeDtypeStruct((3, block_count, S), f32),
            jax.ShapeDtypeStruct((3, G), f32),
        ),
        in_specs=[SMEM, VMEM, VMEM, VMEM],
        out_specs=(VMEM, VMEM),
        compiler_params=PARAMS,
        name="own_stats",
    )(bias, qd, kv, shared)

    stat_rows = (SLOTS + 1) * group + 8
    own, grad_lists = lax.optimization_barrier((own, grad_lists))
    fetch_scratch = [
        pltpu.VMEM((DEPTH, UNROLL * S, 2 * D), jnp.bfloat16),
        pltpu.SemaphoreType.DMA((DEPTH,)),
    ]
    stats, cleared = pl.pallas_call(
        edge_stats_kernel,
        out_shape=(
            jax.ShapeDtypeStruct((y_count, 2 * group, 2 * S), f32),
            jax.ShapeDtypeStruct((cells * S, 2 * D), jnp.bfloat16),
        ),
        in_specs=[SMEM] * 4 + [VMEM, ANY, VMEM],
        out_specs=(VMEM, ANY),
        scratch_shapes=[pltpu.VMEM((stat_rows, 2 * S), f32)] * 3
        + [pltpu.VMEM((tokens, 2 * D), jnp.bfloat16)]
        + fetch_scratch
        + [pltpu.SemaphoreType.DMA((z_count,))],
        compiler_params=PARAMS,
        name="edge_stats",
    )(*lists, qd_group, kv_all, own)
    parts = exchange(stats, Y_AXIS)

    table, final, edge_mixed, *halves = pl.pallas_call(
        edge_grads_kernel,
        out_shape=(
            jax.ShapeDtypeStruct((cells * S, 2 * D), jnp.bfloat16),
            jax.ShapeDtypeStruct((3, group + 8, 2 * S), f32),
            jax.ShapeDtypeStruct((tokens, 2 * D), f32),
        )
        + (jax.ShapeDtypeStruct((tokens, 2 * D), jnp.bfloat16),) * (y_count - 1),
        in_specs=[SMEM] * 8 + [VMEM, ANY, VMEM, ANY],
        out_specs=(ANY,) + (VMEM,) * (y_count + 1),
        scratch_shapes=[
            pltpu.VMEM((group * S, 2 * D), f32),
            pltpu.VMEM((S, 2 * D), f32),
            pltpu.VMEM((STAGES, S, 2 * D), jnp.bfloat16),
        ]
        + fetch_scratch
        + [pltpu.SemaphoreType.DMA((STAGES,))],
        input_output_aliases={11: 0},
        compiler_params=PARAMS,
        name="edge_grads",
    )(meta, grad_lists[0], item_list, cell_list, *grad_lists[1:], qd_group, kv_all, parts, cleared)
    returned = lax.psum_scatter(table, Z_AXIS, scatter_dimension=0, tiled=True)
    halves = [lax.ppermute(half, Y_AXIS, pairs) for half, pairs in zip(halves, backward)]
    rows_all = to_all(to_all(rows, Z_AXIS), Y_AXIS).reshape(ctx_count, 3, G)

    pairs, mixed, shared_grads = pl.pallas_call(
        own_grads_kernel,
        out_shape=(
            jax.ShapeDtypeStruct((tokens, 2 * D), f32),
            jax.ShapeDtypeStruct((tokens, 2 * D), f32),
            jax.ShapeDtypeStruct((2 * G, 2 * D), f32),
        ),
        in_specs=[SMEM] * 3 + [VMEM] * 6,
        out_specs=(VMEM, VMEM, VMEM),
        compiler_params=PARAMS,
        name="own_grads",
    )(meta, bias, flags, qd, kv, shared, final, rows_all, edge_mixed)

    summed = shared_grads.astype(jnp.bfloat16)
    for axis in (Y_AXIS, Z_AXIS):
        count = lax.axis_size(axis)
        summed = exchange(summed.reshape(count, -1, 2 * D), axis)
        summed = jnp.sum(summed.astype(f32), 0).astype(jnp.bfloat16)
    for axis in (Z_AXIS, Y_AXIS):
        summed = to_all(summed, axis).reshape(-1, 2 * D)
    shared_sums = summed.reshape(2, WORLDWIDE_COUNT, 1, S, 2 * D).astype(f32)

    mixed = sum([half.astype(f32) for half in halves], mixed).reshape(block_count, S, 2 * D)
    for g in range(WORLDWIDE_COUNT):
        mask = hits[:, g][:, None, None]
        mixed = jnp.where(mask, shared_sums[1, g], mixed)
    mixed = mixed.reshape(tokens, 2 * D).astype(jnp.bfloat16)
    pairs = pairs.reshape(block_count, S, 2 * D)
    for g in range(WORLDWIDE_COUNT):
        pairs = pairs + jnp.where(hits[:, g][:, None, None], shared_sums[0, g], 0.0)
    pairs = lax.optimization_barrier((pairs.reshape(tokens, 2 * D), mixed))[0]
    grads = [
        (returned[:, half].astype(f32) + pairs[:, half]).astype(jnp.bfloat16)
        for half in (slice(0, D), slice(D, 2 * D))
    ]
    return mixed[:, :D], mixed[:, D:], grads[0], grads[1]


def solution(mesh):
    torus = Mesh(mesh.devices.reshape(16, 4, mesh.shape["head"]), ("ctx_0", "ctx_1", "head"))
    return on_torus(torus)


def on_torus(torus):
    placed = (
        P(CTX_HEAD, None),
        P(CTX_HEAD, None),
        P(CTX_HEAD, None),
        P(CTX_HEAD, None),
        P(CTX, "head", None),
        P(),
    )
    return jax.shard_map(
        body,
        mesh=torus,
        in_specs=placed,
        out_specs=(P(CTX, "head"), P(CTX, "head"), P(CTX, "head"), P(CTX, "head")),
        check_vma=False,
    )
```

```python
import functools

import jax
import jax.numpy as jnp
from jax import lax
from jax.experimental import pallas as pl
from jax.experimental.pallas import tpu as pltpu
from jax.sharding import Mesh
from jax.sharding import PartitionSpec as P

FEATURE_LENGTH = 128
SPAN_TOKENS = 64
RANDOM = 3
WORLDWIDE_COUNT = 2
Z_AXIS = "ctx_0"
Y_AXIS = "ctx_1"
CTX = (Z_AXIS, Y_AXIS)
CTX_HEAD = (Z_AXIS, Y_AXIS, "head")
NEG = -1e30
SCALE = FEATURE_LENGTH ** (-0.5)
UNROLL = 8
DEPTH = 4
STAGES = 32
CODE = 32
LOG2E = 1.4426950408889634
SLOTS = 1 + RANDOM
D = FEATURE_LENGTH
S = SPAN_TOKENS
G = WORLDWIDE_COUNT * SPAN_TOKENS
VMEM = pl.BlockSpec(memory_space=pltpu.VMEM)
SMEM = pl.BlockSpec(memory_space=pltpu.SMEM)
ANY = pl.BlockSpec(memory_space=pl.ANY)
PARAMS = pltpu.CompilerParams(vmem_limit_bytes=56 * 2**20)


def dot_nt(a, b):
    return lax.dot_general(a, b, (((1,), (1,)), ((), ())), preferred_element_type=jnp.float32)


def dot_nn(a, b):
    return lax.dot_general(a, b, (((1,), (0,)), ((), ())), preferred_element_type=jnp.float32)


def dot_tn(a, b):
    return lax.dot_general(a, b, (((0,), (0,)), ((), ())), preferred_element_type=jnp.float32)


def list_masks(listed, block_total):
    inside = (listed >= 0) & (listed < block_total)
    kept = []
    for slot_pos in range(listed.shape[-1]):
        seen = jnp.zeros(listed.shape[:-1], dtype=jnp.bool_)
        for prior_pos in range(slot_pos):
            seen = seen | inside[..., prior_pos] & (listed[..., prior_pos] == listed[..., slot_pos])
        kept.append(inside[..., slot_pos] & jnp.logical_not(seen))
    return jnp.stack(kept, -1)


def exchange(array, axes):
    return lax.all_to_all(array, axes, split_axis=0, concat_axis=0, tiled=True)


def to_all(array, axes):
    count = lax.axis_size(axes)
    return exchange(jnp.broadcast_to(array[None], (count,) + array.shape), axes)


def by_head(first, second):
    rows = first.shape[0]
    heads = first.shape[1] // D
    both = jnp.concatenate([first.reshape(rows, heads, D), second.reshape(rows, heads, D)], 2)
    return exchange(both.transpose(1, 0, 2), "head").reshape(heads * rows, 2 * D)


def merge(parts):
    top = functools.reduce(jnp.maximum, [part[0] for part in parts])
    factors = [jnp.exp(part[0] - top) for part in parts]
    total = sum(part[1] * factor for part, factor in zip(parts, factors))
    slope = sum(part[2] * factor for part, factor in zip(parts, factors))
    return top, total, slope


def column_stats(scores, slopes):
    top = jnp.max(scores, axis=0, keepdims=True)
    weights = jnp.exp(scores - top)
    return (
        top,
        jnp.sum(weights, axis=0, keepdims=True),
        jnp.sum(weights * slopes, axis=0, keepdims=True),
    )


def own_scores(i, blocks, qd_ref, kv_ref, shared_ref, bias_ref):
    low = max(i - 1, 0) * S
    high = min(i + 2, blocks) * S
    q = qd_ref[i * S : (i + 1) * S, :D]
    dout = qd_ref[i * S : (i + 1) * S, D:]
    scores = dot_nt(kv_ref[low:high, :D], q) * SCALE
    slopes = dot_nt(kv_ref[low:high, D:], dout)
    global_scores = dot_nt(shared_ref[:, 2 * D : 3 * D], q) * SCALE
    global_scores = jnp.concatenate(
        [
            global_scores[g * S : (g + 1) * S] + bias_ref[i * WORLDWIDE_COUNT + g]
            for g in range(WORLDWIDE_COUNT)
        ],
        0,
    )
    global_slopes = dot_nt(shared_ref[:, 3 * D :], dout)
    return low, high, q, dout, scores, slopes, global_scores, global_slopes


def pick_kernel(index_ref, qd_ref, kv_ref, code_ref, out_ref, rows_ref, sems):
    blocks = qd_ref.shape[0] // S
    lanes = out_ref.shape[0]
    part = S // lanes
    copies = []
    for g in range(WORLDWIDE_COUNT):
        first = pl.multiple_of(lax.rem(index_ref[g], blocks) * S, S)
        for pos, ref in enumerate((qd_ref, kv_ref)):
            copies.append(
                pltpu.make_async_copy(
                    ref.at[pl.ds(first, S), :],
                    rows_ref.at[pl.ds(g * S, S), pl.ds(pos * 2 * D, 2 * D)],
                    sems.at[2 * g + pos],
                )
            )
    for copy in copies:
        copy.start()
    for lane in range(lanes):
        out_ref[lane, WORLDWIDE_COUNT * part :, :] = code_ref[...]
    for copy in copies:
        copy.wait()
    for lane in range(lanes):
        for g in range(WORLDWIDE_COUNT):
            low = g * S + lane * part
            out_ref[lane, g * part : (g + 1) * part, :] = rows_ref[low : low + part, :]


def own_stats_kernel(
    bias_ref, qd_ref, kv_ref, shared_ref, own_ref, rows_ref, table_ref, zero_ref, zero_sems
):
    size = zero_ref.shape[0]
    zero_ref[...] = jnp.zeros(zero_ref.shape, jnp.bfloat16)
    clears = [
        pltpu.make_async_copy(zero_ref, table_ref.at[pl.ds(i * size, size), :], zero_sems.at[i])
        for i in range(table_ref.shape[0] // size)
    ]
    for clear in clears:
        clear.start()
    tokens = qd_ref.shape[0]
    blocks = tokens // S
    for i in range(blocks):
        _, _, _, _, scores, slopes, global_scores, global_slopes = own_scores(
            i, blocks, qd_ref, kv_ref, shared_ref, bias_ref
        )
        top, total, slope = merge(
            [column_stats(scores, slopes), column_stats(global_scores, global_slopes)]
        )
        own_ref[0, i : i + 1, :] = top
        own_ref[1, i : i + 1, :] = total
        own_ref[2, i : i + 1, :] = slope
    parts = []
    for low in range(0, tokens, G):
        scores = dot_nt(kv_ref[low : low + G, :D], shared_ref[:, :D]) * SCALE
        slopes = dot_nt(kv_ref[low : low + G, D:], shared_ref[:, D : 2 * D])
        parts.append(column_stats(scores, slopes))
    top, total, slope = merge(parts)
    rows_ref[0:1, :] = top
    rows_ref[1:2, :] = total
    rows_ref[2:3, :] = slope
    for clear in clears:
        clear.wait()


def cell_fetcher(meta_ref, cell_ref, kv_ref, fetch_ref, fetch_sems):
    def start(t):
        @pl.when(t < meta_ref[0])
        def _():
            bank = t & (DEPTH - 1)
            for u in range(UNROLL):
                cell = pl.multiple_of(cell_ref[t * UNROLL + u] * S, S)
                pltpu.make_async_copy(
                    kv_ref.at[pl.ds(cell, S), :],
                    fetch_ref.at[bank, pl.ds(u * S, S), :],
                    fetch_sems.at[bank],
                ).start()

    def wait(t):
        bank = t & (DEPTH - 1)
        pltpu.make_async_copy(
            kv_ref.at[pl.ds(0, UNROLL * S), :], fetch_ref.at[bank], fetch_sems.at[bank]
        ).wait()

    return start, wait


def diagonal(qd):
    zeros = jnp.zeros((S, D), jnp.bfloat16)
    return jnp.concatenate(
        [jnp.concatenate([qd[:, :D], zeros], 1), jnp.concatenate([zeros, qd[:, D:]], 1)], 0
    )


def lane_scale(low, high):
    return jnp.where(lax.broadcasted_iota(jnp.int32, (1, 2 * S), 1) < S, low, high)


def edge_stats_kernel(
    meta_ref,
    slot_ref,
    item_ref,
    cell_ref,
    qd_ref,
    kv_ref,
    own_ref,
    out_ref,
    top_ref,
    total_ref,
    slope_ref,
    fetch_ref,
    fetch_sems,
):
    group = qd_ref.shape[0] // S
    blocks = own_ref.shape[1]
    start, wait = cell_fetcher(meta_ref, cell_ref, kv_ref, fetch_ref, fetch_sems)
    for t in range(DEPTH):
        start(t)
    top_ref[...] = jnp.full(top_ref.shape, NEG, jnp.float32)
    total_ref[...] = jnp.zeros(total_ref.shape, jnp.float32)
    slope_ref[...] = jnp.zeros(slope_ref.shape, jnp.float32)
    factor = lane_scale(SCALE, 1.0)

    def step(t, carry):
        wait(t)
        found = []
        for u in range(UNROLL):
            pos = t * UNROLL + u
            item = pl.multiple_of(item_ref[pos] * S, S)
            pairs = fetch_ref[t & (DEPTH - 1), u * S : (u + 1) * S, :]
            both = dot_nt(pairs, diagonal(qd_ref[pl.ds(item, S), :])) * factor
            top = jnp.max(both, axis=0, keepdims=True)
            weights = jnp.exp(both - top)
            total = jnp.sum(weights, axis=0, keepdims=True)
            slope = jnp.sum(weights * pltpu.roll(both, S, 1), axis=0, keepdims=True)
            found.append((slot_ref[pos], top, total, slope))
        for slot, top, total, slope in found:
            top_ref[pl.ds(slot, 1), :] = top
            total_ref[pl.ds(slot, 1), :] = total
            slope_ref[pl.ds(slot, 1), :] = slope
        start(t + DEPTH)
        return carry

    lax.fori_loop(0, meta_ref[0], step, 0)
    mine = pl.multiple_of(SLOTS * group + meta_ref[1] * blocks, 8)
    top_ref[pl.ds(mine, blocks), :S] = own_ref[0]
    total_ref[pl.ds(mine, blocks), :S] = own_ref[1]
    slope_ref[pl.ds(mine, blocks), :S] = own_ref[2]
    top, total, slope = merge(
        [
            (
                top_ref[s * group : (s + 1) * group, :S],
                total_ref[s * group : (s + 1) * group, :S],
                slope_ref[s * group : (s + 1) * group, :S],
            )
            for s in range(SLOTS + 1)
        ]
    )
    first = jnp.concatenate([top, total], 1)
    second = jnp.concatenate([slope, slope], 1)
    for lane in range(out_ref.shape[0]):
        out_ref[lane, :group, :] = first
        out_ref[lane, group:, :] = second


def edge_grads_kernel(
    meta_ref,
    row_ref,
    item_ref,
    cell_ref,
    stage_pos_ref,
    fresh_ref,
    last_ref,
    reuse_ref,
    qd_ref,
    kv_ref,
    parts_ref,
    cleared_ref,
    table_ref,
    final_ref,
    mixed_ref,
    *rest,
):
    sent_refs = rest[:-6]
    partial_ref, sum_ref, stage_ref, fetch_ref, fetch_sems, stage_sems = rest[-6:]
    group = qd_ref.shape[0] // S
    tokens = mixed_ref.shape[0]
    lanes = parts_ref.shape[0]
    start, wait = cell_fetcher(meta_ref, cell_ref, kv_ref, fetch_ref, fetch_sems)
    for t in range(DEPTH):
        start(t)
    top, total, slope = merge(
        [
            (
                parts_ref[lane, :group, :],
                pltpu.roll(parts_ref[lane, :group, :], S, 1),
                parts_ref[lane, group:, :],
            )
            for lane in range(lanes)
        ]
    )
    inverse = 1.0 / total
    final_ref[0, :group, :] = top * LOG2E
    final_ref[1, :group, :] = inverse
    final_ref[2, :group, :] = slope * inverse * SCALE
    final_ref[0, group:, :] = jnp.full((8, 2 * S), -NEG, jnp.float32)
    final_ref[1:, group:, :] = jnp.zeros((2, 8, 2 * S), jnp.float32)
    partial_ref[...] = jnp.zeros(partial_ref.shape, jnp.float32)
    sum_ref[...] = jnp.zeros(sum_ref.shape, jnp.float32)
    factor = lane_scale(SCALE * LOG2E, SCALE)
    low_half = lax.broadcasted_iota(jnp.int32, (S, 2 * S), 1) < S

    def stage_copy(stage, cell):
        at = pl.ds(pl.multiple_of(cell * S, S), S)
        return pltpu.make_async_copy(stage_ref.at[stage], table_ref.at[at, :], stage_sems.at[stage])

    def step(t, carry):
        wait(t)
        for u in range(UNROLL):
            pos = t * UNROLL + u

            @pl.when(reuse_ref[pos] > 0)
            def _():
                stage_copy(stage_pos_ref[pos], 0).wait()

        found = []
        for u in range(UNROLL):
            pos = t * UNROLL + u
            row = pl.ds(row_ref[pos], 1)
            item = pl.multiple_of(item_ref[pos] * S, S)
            pairs = fetch_ref[t & (DEPTH - 1), u * S : (u + 1) * S, :]
            corner = diagonal(qd_ref[pl.ds(item, S), :])
            both = dot_nt(pairs, corner) * factor
            prob = jnp.exp2(both - final_ref[0, row, :]) * final_ref[1, row, :]
            dscore = prob * (pltpu.roll(both, S, 1) - final_ref[2, row, :])
            packed = jnp.where(low_half, dscore, pltpu.roll(prob, S, 1)).astype(jnp.bfloat16)
            found.append((pos, item, jnp.concatenate([dot_nn(packed[:, :S], corner[:S, :D]), dot_nn(packed[:, S:], corner[S:, D:])], 1), dot_tn(packed[:, S:], pairs[:, D:]), dot_tn(packed[:, :S], pairs[:, :D])))
        running = sum_ref[...]
        for pos, item, grads, mixed, dq in found:
            running = grads + jnp.where(fresh_ref[pos] > 0, 0.0, running)
            stage_ref[stage_pos_ref[pos]] = running.astype(jnp.bfloat16)
            at = pl.ds(item, S)
            partial_ref[at, :D] += mixed
            partial_ref[at, D:] += dq
        sum_ref[...] = running
        for u in range(UNROLL):
            pos = t * UNROLL + u

            @pl.when(last_ref[pos] > 0)
            def _():
                stage_copy(stage_pos_ref[pos], cell_ref[pos]).start()

        start(t + DEPTH)
        return carry

    lax.fori_loop(0, meta_ref[0], step, 0)
    mixed_ref[...] = partial_ref[:tokens, :]
    for shift, sent_ref in enumerate(sent_refs):
        low = (shift + 1) * tokens
        sent_ref[...] = partial_ref[low : low + tokens, :].astype(jnp.bfloat16)
    for stage in range(STAGES):

        @pl.when(stage < meta_ref[2])
        def _():
            stage_copy(stage, 0).wait()


def own_grads_kernel(
    meta_ref,
    bias_ref,
    flag_ref,
    qd_ref,
    kv_ref,
    shared_ref,
    final_ref,
    rows_ref,
    edge_ref,
    pairs_ref,
    mixed_ref,
    shared_grad_ref,
):
    tokens = qd_ref.shape[0]
    blocks = tokens // S
    first = meta_ref[1] * blocks
    rows = rows_ref[...]
    row_top = jnp.max(rows[:, 0:1, :], axis=0)
    factors = jnp.exp(rows[:, 0:1, :] - row_top[None])
    sums = jnp.sum(rows * factors, axis=0)
    row_inverse = 1.0 / sums[1:2]
    row_slope = sums[2:3] * row_inverse
    q = shared_ref[:, :D]
    dout = shared_ref[:, D : 2 * D]
    mixed = jnp.zeros((G, D), jnp.float32)
    dq = jnp.zeros((G, D), jnp.float32)
    for low in range(0, tokens, G):
        key = kv_ref[low : low + G, :D]
        value = kv_ref[low : low + G, D:]
        scores = dot_nt(key, q) * SCALE
        slopes = dot_nt(value, dout)
        prob = jnp.exp(scores - row_top) * row_inverse
        dscore = (prob * ((slopes - row_slope) * SCALE)).astype(jnp.bfloat16)
        prob = prob.astype(jnp.bfloat16)
        pairs_ref[low : low + G, :D] = dot_nn(dscore, q)
        pairs_ref[low : low + G, D:] = dot_nn(prob, dout)
        mixed = mixed + dot_tn(prob, value)
        dq = dq + dot_tn(dscore, key)
    shared_grad_ref[G:, :D] = mixed
    shared_grad_ref[G:, D:] = dq
    global_dkey = jnp.zeros((G, D), jnp.float32)
    global_dvalue = jnp.zeros((G, D), jnp.float32)
    for i in range(blocks):
        low, high, q, dout, scores, slopes, global_scores, global_slopes = own_scores(
            i, blocks, qd_ref, kv_ref, shared_ref, bias_ref
        )
        top = final_ref[0, pl.ds(first + i, 1), :S]
        inverse = final_ref[1, pl.ds(first + i, 1), :S] * flag_ref[i]
        slope = final_ref[2, pl.ds(first + i, 1), :S]

        def both(scores, slopes):
            prob = jnp.exp2(scores * LOG2E - top) * inverse
            dscore = (prob * (slopes * SCALE - slope)).astype(jnp.bfloat16)
            return prob.astype(jnp.bfloat16), dscore

        prob, dscore = both(scores, slopes)
        global_prob, global_dscore = both(global_scores, global_slopes)
        pairs_ref[low:high, :D] += dot_nn(dscore, q)
        pairs_ref[low:high, D:] += dot_nn(prob, dout)
        global_dkey = global_dkey + dot_nn(global_dscore, q)
        global_dvalue = global_dvalue + dot_nn(global_prob, dout)
        at = slice(i * S, (i + 1) * S)
        mixed_ref[at, :D] = (
            edge_ref[at, :D]
            + dot_tn(prob, kv_ref[low:high, D:])
            + dot_tn(global_prob, shared_ref[:, 3 * D :])
        )
        mixed_ref[at, D:] = (
            edge_ref[at, D:]
            + dot_tn(dscore, kv_ref[low:high, :D])
            + dot_tn(global_dscore, shared_ref[:, 2 * D : 3 * D])
        )
    shared_grad_ref[:G, :D] = global_dkey
    shared_grad_ref[:G, D:] = global_dvalue


def body(query, key_in, value_in, grad_out, random_blocks, universal_segment_indices):
    f32 = jnp.float32
    z_count = lax.axis_size(Z_AXIS)
    y_count = lax.axis_size(Y_AXIS)
    ctx_count = z_count * y_count
    z_place = lax.axis_index(Z_AXIS)
    y_place = lax.axis_index(Y_AXIS)
    ctx_place = z_place * y_count + y_place

    kv = by_head(key_in, value_in)
    query, grad_out, random_blocks, kv = lax.optimization_barrier(
        (query, grad_out, random_blocks, kv)
    )
    kv_all = lax.all_gather(kv, Z_AXIS, axis=0, tiled=True)
    qd = by_head(query, grad_out)
    tokens = qd.shape[0]
    block_count = tokens // S
    group = block_count * y_count
    block_total = ctx_count * block_count
    cells = z_count * block_count

    part = S // y_count
    codes = random_blocks.reshape(1, -1)
    codes = jnp.concatenate([codes // CODE, codes % CODE], 1).astype(jnp.bfloat16)
    codes = jnp.pad(codes, ((0, 15), (0, 4 * D - codes.shape[1])))
    sent = pl.pallas_call(
        pick_kernel,
        out_shape=jax.ShapeDtypeStruct((y_count, WORLDWIDE_COUNT * part + 16, 4 * D), jnp.bfloat16),
        in_specs=[SMEM, ANY, ANY, VMEM],
        out_specs=VMEM,
        scratch_shapes=[
            pltpu.VMEM((G, 4 * D), jnp.bfloat16),
            pltpu.SemaphoreType.DMA((2 * WORLDWIDE_COUNT,)),
        ],
        compiler_params=PARAMS,
        name="pick",
    )(universal_segment_indices, qd, kv, codes)
    owners = universal_segment_indices // block_count

    def chosen(arrived, place):
        count = arrived.shape[0]
        mask = jnp.arange(count, dtype=jnp.int32)[:, None] == place[None]
        return jnp.sum(jnp.where(mask[:, :, None, None], arrived, 0), 0)

    arrived = exchange(sent, Y_AXIS)
    codes = arrived[:, WORLDWIDE_COUNT * part, : 2 * block_count * RANDOM]
    codes = codes.astype(jnp.int32).reshape(y_count, 2, block_count * RANDOM)
    random_group = (codes[:, 0] * CODE + codes[:, 1]).reshape(group, RANDOM)
    arrived = arrived[:, : WORLDWIDE_COUNT * part].reshape(y_count, WORLDWIDE_COUNT, part, 4 * D)
    qd_sent, arrived = lax.optimization_barrier((qd, arrived))
    picked = chosen(arrived, owners % y_count)
    sent = picked.reshape(WORLDWIDE_COUNT, z_count, -1, 4 * D).transpose(1, 0, 2, 3)
    picked = chosen(exchange(sent, Z_AXIS), owners // y_count)
    shifts = range(1, y_count)
    forward = [[(i, (i + shift) % y_count) for i in range(y_count)] for shift in shifts]
    backward = [[(i, (i - shift) % y_count) for i in range(y_count)] for shift in shifts]
    qd_group = jnp.concatenate(
        [qd] + [lax.ppermute(qd_sent, Y_AXIS, pairs) for pairs in forward], 0
    )
    gathered, qd_group = lax.optimization_barrier((to_all(picked, Z_AXIS), qd_group))
    shared = gathered.transpose(1, 0, 2, 3).reshape(WORLDWIDE_COUNT, part, 4 * D)
    shared = to_all(shared, Y_AXIS).transpose(1, 0, 2, 3).reshape(G, 4 * D)

    ids = z_place * group + jnp.arange(group, dtype=jnp.int32)
    local = jnp.arange(group, dtype=jnp.int32) % block_count
    globals_ = jnp.broadcast_to(universal_segment_indices[None], (group, WORLDWIDE_COUNT))
    listed = jnp.concatenate(
        [jnp.stack([ids - 1, ids, ids + 1], 1), random_group, globals_], 1
    )
    kept = list_masks(listed, block_total)
    is_global = jnp.any(ids[:, None] == universal_segment_indices[None], 1)
    border = jnp.where(local == 0, ids - 1, jnp.where(local == block_count - 1, ids + 1, -1))
    named = jnp.concatenate([border[:, None], random_group], 1)
    valid = jnp.concatenate(
        [((border >= 0) & (border < block_total))[:, None], kept[:, 3 : 3 + RANDOM]], 1
    )
    lane = named // block_count % y_count
    valid = valid & jnp.logical_not(is_global)[:, None] & (lane == y_place)
    cell = named // group * block_count + named % block_count
    valid = valid.T.reshape(-1)
    cell = cell.T.reshape(-1)
    entries = SLOTS * group
    order = jnp.arange(entries, dtype=jnp.int32)
    label = cell * entries + order
    rank = jnp.sum((valid[None, :] & (label[None, :] < label[:, None])).astype(jnp.int32), 1)
    edge_count = jnp.sum(valid.astype(jnp.int32))
    hit = (rank[None, :] == order[:, None]) & valid[None, :]
    slot_list = jnp.sum(jnp.where(hit, order[None, :], 0), 1)
    cell_list = jnp.sum(jnp.where(hit, cell[None, :], 0), 1)
    real = order < edge_count
    fresh = real & ((order == 0) | (cell_list != jnp.roll(cell_list, 1)))
    last_list = real & ((order == edge_count - 1) | (cell_list != jnp.roll(cell_list, -1)))
    order_list = jnp.sum((fresh[None, :] & (order[None, :] <= order[:, None])).astype(jnp.int32), 1) - 1
    slot_list = jnp.where(real, slot_list, entries + group)
    item_list = slot_list % group
    item_list = (y_place - item_list // block_count) % y_count * block_count + item_list % block_count
    row_list = jnp.where(real, slot_list % group, group)
    grad_lists = (
        row_list,
        order_list % STAGES,
        fresh.astype(jnp.int32),
        last_list.astype(jnp.int32),
        (fresh & (order_list >= STAGES)).astype(jnp.int32),
    )
    meta = jnp.stack(
        [(edge_count + UNROLL - 1) // UNROLL, y_place, jnp.sum(fresh.astype(jnp.int32))]
    ).astype(jnp.int32)
    lists = (meta, slot_list, item_list, cell_list)

    own_first = y_place * block_count
    own_kept = lax.dynamic_slice_in_dim(kept, own_first, block_count, 0)
    bias = jnp.where(own_kept[:, 3 + RANDOM :], 0.0, NEG).astype(f32).reshape(-1)
    own_ids = ctx_place * block_count + jnp.arange(block_count, dtype=jnp.int32)
    hits = own_ids[:, None] == universal_segment_indices[None]
    flags = jnp.where(jnp.any(hits, 1), 0.0, 1.0).astype(f32)

    own, rows, cleared = pl.pallas_call(
        own_stats_kernel,
        out_shape=(
            jax.ShapeDtypeStruct((3, block_count, S), f32),
            jax.ShapeDtypeStruct((3, G), f32),
            jax.ShapeDtypeStruct((cells * S, 2 * D), jnp.bfloat16),
        ),
        in_specs=[SMEM, VMEM, VMEM, VMEM],
        out_specs=(VMEM, VMEM, ANY),
        scratch_shapes=[
            pltpu.VMEM((tokens, 2 * D), jnp.bfloat16),
            pltpu.SemaphoreType.DMA((z_count,)),
        ],
        compiler_params=PARAMS,
        name="own_stats",
    )(bias, qd, kv, shared)

    stat_rows = (SLOTS + 1) * group + 8
    own, grad_lists = lax.optimization_barrier((own, grad_lists))
    fetch_scratch = [
        pltpu.VMEM((DEPTH, UNROLL * S, 2 * D), jnp.bfloat16),
        pltpu.SemaphoreType.DMA((DEPTH,)),
    ]
    stats = pl.pallas_call(
        edge_stats_kernel,
        out_shape=jax.ShapeDtypeStruct((y_count, 2 * group, 2 * S), f32),
        in_specs=[SMEM] * 4 + [VMEM, ANY, VMEM],
        out_specs=VMEM,
        scratch_shapes=[pltpu.VMEM((stat_rows, 2 * S), f32)] * 3 + fetch_scratch,
        compiler_params=PARAMS,
        name="edge_stats",
    )(*lists, qd_group, kv_all, own)
    parts = exchange(stats, Y_AXIS)

    table, final, edge_mixed, *halves = pl.pallas_call(
        edge_grads_kernel,
        out_shape=(
            jax.ShapeDtypeStruct((cells * S, 2 * D), jnp.bfloat16),
            jax.ShapeDtypeStruct((3, group + 8, 2 * S), f32),
            jax.ShapeDtypeStruct((tokens, 2 * D), f32),
        )
        + (jax.ShapeDtypeStruct((tokens, 2 * D), jnp.bfloat16),) * (y_count - 1),
        in_specs=[SMEM] * 8 + [VMEM, ANY, VMEM, ANY],
        out_specs=(ANY,) + (VMEM,) * (y_count + 1),
        scratch_shapes=[
            pltpu.VMEM((group * S, 2 * D), f32),
            pltpu.VMEM((S, 2 * D), f32),
            pltpu.VMEM((STAGES, S, 2 * D), jnp.bfloat16),
        ]
        + fetch_scratch
        + [pltpu.SemaphoreType.DMA((STAGES,))],
        input_output_aliases={11: 0},
        compiler_params=PARAMS,
        name="edge_grads",
    )(meta, grad_lists[0], item_list, cell_list, *grad_lists[1:], qd_group, kv_all, parts, cleared)
    returned = lax.psum_scatter(table, Z_AXIS, scatter_dimension=0, tiled=True)
    halves = [lax.ppermute(half, Y_AXIS, pairs) for half, pairs in zip(halves, backward)]
    rows_all = to_all(to_all(rows, Z_AXIS), Y_AXIS).reshape(ctx_count, 3, G)

    pairs, mixed, shared_grads = pl.pallas_call(
        own_grads_kernel,
        out_shape=(
            jax.ShapeDtypeStruct((tokens, 2 * D), f32),
            jax.ShapeDtypeStruct((tokens, 2 * D), f32),
            jax.ShapeDtypeStruct((2 * G, 2 * D), f32),
        ),
        in_specs=[SMEM] * 3 + [VMEM] * 6,
        out_specs=(VMEM, VMEM, VMEM),
        compiler_params=PARAMS,
        name="own_grads",
    )(meta, bias, flags, qd, kv, shared, final, rows_all, edge_mixed)

    summed = shared_grads.astype(jnp.bfloat16)
    for axis in (Y_AXIS, Z_AXIS):
        count = lax.axis_size(axis)
        summed = exchange(summed.reshape(count, -1, 2 * D), axis)
        summed = jnp.sum(summed.astype(f32), 0).astype(jnp.bfloat16)
    for axis in (Z_AXIS, Y_AXIS):
        summed = to_all(summed, axis).reshape(-1, 2 * D)
    shared_sums = summed.reshape(2, WORLDWIDE_COUNT, 1, S, 2 * D).astype(f32)

    mixed = sum([half.astype(f32) for half in halves], mixed).reshape(block_count, S, 2 * D)
    for g in range(WORLDWIDE_COUNT):
        mask = hits[:, g][:, None, None]
        mixed = jnp.where(mask, shared_sums[1, g], mixed)
    mixed = mixed.reshape(tokens, 2 * D).astype(jnp.bfloat16)
    pairs = pairs.reshape(block_count, S, 2 * D)
    for g in range(WORLDWIDE_COUNT):
        pairs = pairs + jnp.where(hits[:, g][:, None, None], shared_sums[0, g], 0.0)
    pairs = lax.optimization_barrier((pairs.reshape(tokens, 2 * D), mixed))[0]
    grads = [
        (returned[:, half].astype(f32) + pairs[:, half]).astype(jnp.bfloat16)
        for half in (slice(0, D), slice(D, 2 * D))
    ]
    return mixed[:, :D], mixed[:, D:], grads[0], grads[1]


def solution(mesh):
    torus = Mesh(mesh.devices.reshape(16, 4, mesh.shape["head"]), ("ctx_0", "ctx_1", "head"))
    return on_torus(torus)


def on_torus(torus):
    placed = (
        P(CTX_HEAD, None),
        P(CTX_HEAD, None),
        P(CTX_HEAD, None),
        P(CTX_HEAD, None),
        P(CTX, "head", None),
        P(),
    )
    return jax.shard_map(
        body,
        mesh=torus,
        in_specs=placed,
        out_specs=(P(CTX, "head"), P(CTX, "head"), P(CTX, "head"), P(CTX, "head")),
        check_vma=False,
    )
```

```python
import functools

import jax
import jax.numpy as jnp
from jax import lax
from jax.experimental import pallas as pl
from jax.experimental.pallas import tpu as pltpu
from jax.sharding import Mesh
from jax.sharding import PartitionSpec as P

FEATURE_LENGTH = 128
SPAN_TOKENS = 64
RANDOM = 3
WORLDWIDE_COUNT = 2
Z_AXIS = "ctx_0"
Y_AXIS = "ctx_1"
CTX = (Z_AXIS, Y_AXIS)
CTX_HEAD = (Z_AXIS, Y_AXIS, "head")
NEG = -1e30
SCALE = FEATURE_LENGTH ** (-0.5)
UNROLL = 8
DEPTH = 4
STAGES = 32
CODE = 32
LOG2E = 1.4426950408889634
SLOTS = 1 + RANDOM
D = FEATURE_LENGTH
S = SPAN_TOKENS
G = WORLDWIDE_COUNT * SPAN_TOKENS
VMEM = pl.BlockSpec(memory_space=pltpu.VMEM)
SMEM = pl.BlockSpec(memory_space=pltpu.SMEM)
ANY = pl.BlockSpec(memory_space=pl.ANY)
PARAMS = pltpu.CompilerParams(vmem_limit_bytes=56 * 2**20)


def dot_nt(a, b):
    return lax.dot_general(a, b, (((1,), (1,)), ((), ())), preferred_element_type=jnp.float32)


def dot_nn(a, b):
    return lax.dot_general(a, b, (((1,), (0,)), ((), ())), preferred_element_type=jnp.float32)


def dot_tn(a, b):
    return lax.dot_general(a, b, (((0,), (0,)), ((), ())), preferred_element_type=jnp.float32)


def list_masks(listed, block_total):
    inside = (listed >= 0) & (listed < block_total)
    kept = []
    for slot_pos in range(listed.shape[-1]):
        seen = jnp.zeros(listed.shape[:-1], dtype=jnp.bool_)
        for prior_pos in range(slot_pos):
            seen = seen | inside[..., prior_pos] & (listed[..., prior_pos] == listed[..., slot_pos])
        kept.append(inside[..., slot_pos] & jnp.logical_not(seen))
    return jnp.stack(kept, -1)


def exchange(array, axes):
    return lax.all_to_all(array, axes, split_axis=0, concat_axis=0, tiled=True)


def to_all(array, axes):
    count = lax.axis_size(axes)
    return exchange(jnp.broadcast_to(array[None], (count,) + array.shape), axes)


def by_head(first, second):
    rows = first.shape[0]
    heads = first.shape[1] // D
    both = jnp.concatenate([first.reshape(rows, heads, D), second.reshape(rows, heads, D)], 2)
    return exchange(both.transpose(1, 0, 2), "head").reshape(heads * rows, 2 * D)


def merge(parts):
    top = functools.reduce(jnp.maximum, [part[0] for part in parts])
    factors = [jnp.exp(part[0] - top) for part in parts]
    total = sum(part[1] * factor for part, factor in zip(parts, factors))
    slope = sum(part[2] * factor for part, factor in zip(parts, factors))
    return top, total, slope


def column_stats(scores, slopes):
    top = jnp.max(scores, axis=0, keepdims=True)
    weights = jnp.exp(scores - top)
    return (
        top,
        jnp.sum(weights, axis=0, keepdims=True),
        jnp.sum(weights * slopes, axis=0, keepdims=True),
    )


def own_scores(i, blocks, qd_ref, kv_ref, shared_ref, bias_ref):
    low = max(i - 1, 0) * S
    high = min(i + 2, blocks) * S
    q = qd_ref[i * S : (i + 1) * S, :D]
    dout = qd_ref[i * S : (i + 1) * S, D:]
    scores = dot_nt(kv_ref[low:high, :D], q) * SCALE
    slopes = dot_nt(kv_ref[low:high, D:], dout)
    global_scores = dot_nt(shared_ref[:, 2 * D : 3 * D], q) * SCALE
    global_scores = jnp.concatenate(
        [
            global_scores[g * S : (g + 1) * S] + bias_ref[i * WORLDWIDE_COUNT + g]
            for g in range(WORLDWIDE_COUNT)
        ],
        0,
    )
    global_slopes = dot_nt(shared_ref[:, 3 * D :], dout)
    return low, high, q, dout, scores, slopes, global_scores, global_slopes


def pick_kernel(index_ref, qd_ref, kv_ref, code_ref, out_ref, rows_ref, sems):
    blocks = qd_ref.shape[0] // S
    lanes = out_ref.shape[0]
    part = S // lanes
    copies = []
    for g in range(WORLDWIDE_COUNT):
        first = pl.multiple_of(lax.rem(index_ref[g], blocks) * S, S)
        for pos, ref in enumerate((qd_ref, kv_ref)):
            copies.append(
                pltpu.make_async_copy(
                    ref.at[pl.ds(first, S), :],
                    rows_ref.at[pl.ds(g * S, S), pl.ds(pos * 2 * D, 2 * D)],
                    sems.at[2 * g + pos],
                )
            )
    for copy in copies:
        copy.start()
    for lane in range(lanes):
        out_ref[lane, WORLDWIDE_COUNT * part :, :] = code_ref[...]
    for copy in copies:
        copy.wait()
    for lane in range(lanes):
        for g in range(WORLDWIDE_COUNT):
            low = g * S + lane * part
            out_ref[lane, g * part : (g + 1) * part, :] = rows_ref[low : low + part, :]


def clear_kernel(after_ref, table_ref, zero_ref, zero_sems):
    size = zero_ref.shape[0]
    zero_ref[...] = jnp.zeros(zero_ref.shape, jnp.bfloat16)
    clears = [
        pltpu.make_async_copy(zero_ref, table_ref.at[pl.ds(i * size, size), :], zero_sems.at[i])
        for i in range(table_ref.shape[0] // size)
    ]
    for clear in clears:
        clear.start()
    for clear in clears:
        clear.wait()


def own_stats_kernel(bias_ref, qd_ref, kv_ref, shared_ref, own_ref, rows_ref):
    tokens = qd_ref.shape[0]
    blocks = tokens // S
    for i in range(blocks):
        _, _, _, _, scores, slopes, global_scores, global_slopes = own_scores(
            i, blocks, qd_ref, kv_ref, shared_ref, bias_ref
        )
        top, total, slope = merge(
            [column_stats(scores, slopes), column_stats(global_scores, global_slopes)]
        )
        own_ref[0, i : i + 1, :] = top
        own_ref[1, i : i + 1, :] = total
        own_ref[2, i : i + 1, :] = slope
    parts = []
    for low in range(0, tokens, G):
        scores = dot_nt(kv_ref[low : low + G, :D], shared_ref[:, :D]) * SCALE
        slopes = dot_nt(kv_ref[low : low + G, D:], shared_ref[:, D : 2 * D])
        parts.append(column_stats(scores, slopes))
    top, total, slope = merge(parts)
    rows_ref[0:1, :] = top
    rows_ref[1:2, :] = total
    rows_ref[2:3, :] = slope


def cell_fetcher(meta_ref, cell_ref, kv_ref, fetch_ref, fetch_sems):
    def start(t):
        @pl.when(t < meta_ref[0])
        def _():
            bank = t & (DEPTH - 1)
            for u in range(UNROLL):
                cell = pl.multiple_of(cell_ref[t * UNROLL + u] * S, S)
                pltpu.make_async_copy(
                    kv_ref.at[pl.ds(cell, S), :],
                    fetch_ref.at[bank, pl.ds(u * S, S), :],
                    fetch_sems.at[bank],
                ).start()

    def wait(t):
        bank = t & (DEPTH - 1)
        pltpu.make_async_copy(
            kv_ref.at[pl.ds(0, UNROLL * S), :], fetch_ref.at[bank], fetch_sems.at[bank]
        ).wait()

    return start, wait


def diagonal(qd):
    zeros = jnp.zeros((S, D), jnp.bfloat16)
    return jnp.concatenate(
        [jnp.concatenate([qd[:, :D], zeros], 1), jnp.concatenate([zeros, qd[:, D:]], 1)], 0
    )


def lane_scale(low, high):
    return jnp.where(lax.broadcasted_iota(jnp.int32, (1, 2 * S), 1) < S, low, high)


def edge_stats_kernel(
    meta_ref,
    slot_ref,
    item_ref,
    cell_ref,
    qd_ref,
    kv_ref,
    own_ref,
    out_ref,
    top_ref,
    total_ref,
    slope_ref,
    fetch_ref,
    fetch_sems,
):
    group = qd_ref.shape[0] // S
    blocks = own_ref.shape[1]
    start, wait = cell_fetcher(meta_ref, cell_ref, kv_ref, fetch_ref, fetch_sems)
    for t in range(DEPTH):
        start(t)
    top_ref[...] = jnp.full(top_ref.shape, NEG, jnp.float32)
    total_ref[...] = jnp.zeros(total_ref.shape, jnp.float32)
    slope_ref[...] = jnp.zeros(slope_ref.shape, jnp.float32)
    factor = lane_scale(SCALE, 1.0)

    def step(t, carry):
        wait(t)
        found = []
        for u in range(UNROLL):
            pos = t * UNROLL + u
            item = pl.multiple_of(item_ref[pos] * S, S)
            pairs = fetch_ref[t & (DEPTH - 1), u * S : (u + 1) * S, :]
            both = dot_nt(pairs, diagonal(qd_ref[pl.ds(item, S), :])) * factor
            top = jnp.max(both, axis=0, keepdims=True)
            weights = jnp.exp(both - top)
            total = jnp.sum(weights, axis=0, keepdims=True)
            slope = jnp.sum(weights * pltpu.roll(both, S, 1), axis=0, keepdims=True)
            found.append((slot_ref[pos], top, total, slope))
        for slot, top, total, slope in found:
            top_ref[pl.ds(slot, 1), :] = top
            total_ref[pl.ds(slot, 1), :] = total
            slope_ref[pl.ds(slot, 1), :] = slope
        start(t + DEPTH)
        return carry

    lax.fori_loop(0, meta_ref[0], step, 0)
    mine = pl.multiple_of(SLOTS * group + meta_ref[1] * blocks, 8)
    top_ref[pl.ds(mine, blocks), :S] = own_ref[0]
    total_ref[pl.ds(mine, blocks), :S] = own_ref[1]
    slope_ref[pl.ds(mine, blocks), :S] = own_ref[2]
    top, total, slope = merge(
        [
            (
                top_ref[s * group : (s + 1) * group, :S],
                total_ref[s * group : (s + 1) * group, :S],
                slope_ref[s * group : (s + 1) * group, :S],
            )
            for s in range(SLOTS + 1)
        ]
    )
    first = jnp.concatenate([top, total], 1)
    second = jnp.concatenate([slope, slope], 1)
    for lane in range(out_ref.shape[0]):
        out_ref[lane, :group, :] = first
        out_ref[lane, group:, :] = second


def edge_grads_kernel(
    meta_ref,
    row_ref,
    item_ref,
    cell_ref,
    stage_pos_ref,
    fresh_ref,
    last_ref,
    reuse_ref,
    qd_ref,
    kv_ref,
    parts_ref,
    cleared_ref,
    table_ref,
    final_ref,
    mixed_ref,
    *rest,
):
    sent_refs = rest[:-6]
    partial_ref, sum_ref, stage_ref, fetch_ref, fetch_sems, stage_sems = rest[-6:]
    group = qd_ref.shape[0] // S
    tokens = mixed_ref.shape[0]
    lanes = parts_ref.shape[0]
    start, wait = cell_fetcher(meta_ref, cell_ref, kv_ref, fetch_ref, fetch_sems)
    for t in range(DEPTH):
        start(t)
    top, total, slope = merge(
        [
            (
                parts_ref[lane, :group, :],
                pltpu.roll(parts_ref[lane, :group, :], S, 1),
                parts_ref[lane, group:, :],
            )
            for lane in range(lanes)
        ]
    )
    inverse = 1.0 / total
    final_ref[0, :group, :] = top * LOG2E
    final_ref[1, :group, :] = inverse
    final_ref[2, :group, :] = slope * inverse * SCALE
    final_ref[0, group:, :] = jnp.full((8, 2 * S), -NEG, jnp.float32)
    final_ref[1:, group:, :] = jnp.zeros((2, 8, 2 * S), jnp.float32)
    partial_ref[...] = jnp.zeros(partial_ref.shape, jnp.float32)
    sum_ref[...] = jnp.zeros(sum_ref.shape, jnp.float32)
    factor = lane_scale(SCALE * LOG2E, SCALE)
    low_half = lax.broadcasted_iota(jnp.int32, (S, 2 * S), 1) < S

    def stage_copy(stage, cell):
        at = pl.ds(pl.multiple_of(cell * S, S), S)
        return pltpu.make_async_copy(stage_ref.at[stage], table_ref.at[at, :], stage_sems.at[stage])

    def step(t, carry):
        wait(t)
        for u in range(UNROLL):
            pos = t * UNROLL + u

            @pl.when(reuse_ref[pos] > 0)
            def _():
                stage_copy(stage_pos_ref[pos], 0).wait()

        found = []
        for u in range(UNROLL):
            pos = t * UNROLL + u
            row = pl.ds(row_ref[pos], 1)
            item = pl.multiple_of(item_ref[pos] * S, S)
            pairs = fetch_ref[t & (DEPTH - 1), u * S : (u + 1) * S, :]
            corner = diagonal(qd_ref[pl.ds(item, S), :])
            both = dot_nt(pairs, corner) * factor
            prob = jnp.exp2(both - final_ref[0, row, :]) * final_ref[1, row, :]
            dscore = prob * (pltpu.roll(both, S, 1) - final_ref[2, row, :])
            packed = jnp.where(low_half, dscore, pltpu.roll(prob, S, 1)).astype(jnp.bfloat16)
            found.append((pos, item, jnp.concatenate([dot_nn(packed[:, :S], corner[:S, :D]), dot_nn(packed[:, S:], corner[S:, D:])], 1), dot_tn(packed[:, S:], pairs[:, D:]), dot_tn(packed[:, :S], pairs[:, :D])))
        running = sum_ref[...]
        for pos, item, grads, mixed, dq in found:
            running = grads + jnp.where(fresh_ref[pos] > 0, 0.0, running)
            stage_ref[stage_pos_ref[pos]] = running.astype(jnp.bfloat16)
            at = pl.ds(item, S)
            partial_ref[at, :D] += mixed
            partial_ref[at, D:] += dq
        sum_ref[...] = running
        for u in range(UNROLL):
            pos = t * UNROLL + u

            @pl.when(last_ref[pos] > 0)
            def _():
                stage_copy(stage_pos_ref[pos], cell_ref[pos]).start()

        start(t + DEPTH)
        return carry

    lax.fori_loop(0, meta_ref[0], step, 0)
    mixed_ref[...] = partial_ref[:tokens, :]
    for shift, sent_ref in enumerate(sent_refs):
        low = (shift + 1) * tokens
        sent_ref[...] = partial_ref[low : low + tokens, :].astype(jnp.bfloat16)
    for stage in range(STAGES):

        @pl.when(stage < meta_ref[2])
        def _():
            stage_copy(stage, 0).wait()


def own_grads_kernel(
    meta_ref,
    bias_ref,
    flag_ref,
    qd_ref,
    kv_ref,
    shared_ref,
    final_ref,
    rows_ref,
    edge_ref,
    pairs_ref,
    mixed_ref,
    shared_grad_ref,
):
    tokens = qd_ref.shape[0]
    blocks = tokens // S
    first = meta_ref[1] * blocks
    rows = rows_ref[...]
    row_top = jnp.max(rows[:, 0:1, :], axis=0)
    factors = jnp.exp(rows[:, 0:1, :] - row_top[None])
    sums = jnp.sum(rows * factors, axis=0)
    row_inverse = 1.0 / sums[1:2]
    row_slope = sums[2:3] * row_inverse
    q = shared_ref[:, :D]
    dout = shared_ref[:, D : 2 * D]
    mixed = jnp.zeros((G, D), jnp.float32)
    dq = jnp.zeros((G, D), jnp.float32)
    for low in range(0, tokens, G):
        key = kv_ref[low : low + G, :D]
        value = kv_ref[low : low + G, D:]
        scores = dot_nt(key, q) * SCALE
        slopes = dot_nt(value, dout)
        prob = jnp.exp(scores - row_top) * row_inverse
        dscore = (prob * ((slopes - row_slope) * SCALE)).astype(jnp.bfloat16)
        prob = prob.astype(jnp.bfloat16)
        pairs_ref[low : low + G, :D] = dot_nn(dscore, q)
        pairs_ref[low : low + G, D:] = dot_nn(prob, dout)
        mixed = mixed + dot_tn(prob, value)
        dq = dq + dot_tn(dscore, key)
    shared_grad_ref[G:, :D] = mixed
    shared_grad_ref[G:, D:] = dq
    global_dkey = jnp.zeros((G, D), jnp.float32)
    global_dvalue = jnp.zeros((G, D), jnp.float32)
    for i in range(blocks):
        low, high, q, dout, scores, slopes, global_scores, global_slopes = own_scores(
            i, blocks, qd_ref, kv_ref, shared_ref, bias_ref
        )
        top = final_ref[0, pl.ds(first + i, 1), :S]
        inverse = final_ref[1, pl.ds(first + i, 1), :S] * flag_ref[i]
        slope = final_ref[2, pl.ds(first + i, 1), :S]

        def both(scores, slopes):
            prob = jnp.exp2(scores * LOG2E - top) * inverse
            dscore = (prob * (slopes * SCALE - slope)).astype(jnp.bfloat16)
            return prob.astype(jnp.bfloat16), dscore

        prob, dscore = both(scores, slopes)
        global_prob, global_dscore = both(global_scores, global_slopes)
        pairs_ref[low:high, :D] += dot_nn(dscore, q)
        pairs_ref[low:high, D:] += dot_nn(prob, dout)
        global_dkey = global_dkey + dot_nn(global_dscore, q)
        global_dvalue = global_dvalue + dot_nn(global_prob, dout)
        at = slice(i * S, (i + 1) * S)
        mixed_ref[at, :D] = (
            edge_ref[at, :D]
            + dot_tn(prob, kv_ref[low:high, D:])
            + dot_tn(global_prob, shared_ref[:, 3 * D :])
        )
        mixed_ref[at, D:] = (
            edge_ref[at, D:]
            + dot_tn(dscore, kv_ref[low:high, :D])
            + dot_tn(global_dscore, shared_ref[:, 2 * D : 3 * D])
        )
    shared_grad_ref[:G, :D] = global_dkey
    shared_grad_ref[:G, D:] = global_dvalue


def body(query, key_in, value_in, grad_out, random_blocks, universal_segment_indices):
    f32 = jnp.float32
    z_count = lax.axis_size(Z_AXIS)
    y_count = lax.axis_size(Y_AXIS)
    ctx_count = z_count * y_count
    z_place = lax.axis_index(Z_AXIS)
    y_place = lax.axis_index(Y_AXIS)
    ctx_place = z_place * y_count + y_place

    kv = by_head(key_in, value_in)
    query, grad_out, random_blocks, kv = lax.optimization_barrier(
        (query, grad_out, random_blocks, kv)
    )
    kv_all = lax.all_gather(kv, Z_AXIS, axis=0, tiled=True)
    qd = by_head(query, grad_out)
    tokens = qd.shape[0]
    block_count = tokens // S
    group = block_count * y_count
    block_total = ctx_count * block_count
    cells = z_count * block_count

    part = S // y_count
    codes = random_blocks.reshape(1, -1)
    codes = jnp.concatenate([codes // CODE, codes % CODE], 1).astype(jnp.bfloat16)
    codes = jnp.pad(codes, ((0, 15), (0, 4 * D - codes.shape[1])))
    sent = pl.pallas_call(
        pick_kernel,
        out_shape=jax.ShapeDtypeStruct((y_count, WORLDWIDE_COUNT * part + 16, 4 * D), jnp.bfloat16),
        in_specs=[SMEM, ANY, ANY, VMEM],
        out_specs=VMEM,
        scratch_shapes=[
            pltpu.VMEM((G, 4 * D), jnp.bfloat16),
            pltpu.SemaphoreType.DMA((2 * WORLDWIDE_COUNT,)),
        ],
        compiler_params=PARAMS,
        name="pick",
    )(universal_segment_indices, qd, kv, codes)
    owners = universal_segment_indices // block_count

    def chosen(arrived, place):
        count = arrived.shape[0]
        mask = jnp.arange(count, dtype=jnp.int32)[:, None] == place[None]
        return jnp.sum(jnp.where(mask[:, :, None, None], arrived, 0), 0)

    arrived = exchange(sent, Y_AXIS)
    codes = arrived[:, WORLDWIDE_COUNT * part, : 2 * block_count * RANDOM]
    codes = codes.astype(jnp.int32).reshape(y_count, 2, block_count * RANDOM)
    random_group = (codes[:, 0] * CODE + codes[:, 1]).reshape(group, RANDOM)
    arrived = arrived[:, : WORLDWIDE_COUNT * part].reshape(y_count, WORLDWIDE_COUNT, part, 4 * D)
    qd_sent, arrived = lax.optimization_barrier((qd, arrived))
    picked = chosen(arrived, owners % y_count)
    sent = picked.reshape(WORLDWIDE_COUNT, z_count, -1, 4 * D).transpose(1, 0, 2, 3)
    picked = chosen(exchange(sent, Z_AXIS), owners // y_count)
    shifts = range(1, y_count)
    forward = [[(i, (i + shift) % y_count) for i in range(y_count)] for shift in shifts]
    backward = [[(i, (i - shift) % y_count) for i in range(y_count)] for shift in shifts]
    qd_group = jnp.concatenate(
        [qd] + [lax.ppermute(qd_sent, Y_AXIS, pairs) for pairs in forward], 0
    )
    cleared = pl.pallas_call(
        clear_kernel,
        out_shape=jax.ShapeDtypeStruct((cells * S, 2 * D), jnp.bfloat16),
        in_specs=[ANY],
        out_specs=ANY,
        scratch_shapes=[
            pltpu.VMEM((tokens, 2 * D), jnp.bfloat16),
            pltpu.SemaphoreType.DMA((z_count,)),
        ],
        compiler_params=PARAMS,
        name="clear",
    )(qd_group)
    gathered, qd_group, cleared = lax.optimization_barrier(
        (to_all(picked, Z_AXIS), qd_group, cleared)
    )
    shared = gathered.transpose(1, 0, 2, 3).reshape(WORLDWIDE_COUNT, part, 4 * D)
    shared = to_all(shared, Y_AXIS).transpose(1, 0, 2, 3).reshape(G, 4 * D)

    ids = z_place * group + jnp.arange(group, dtype=jnp.int32)
    local = jnp.arange(group, dtype=jnp.int32) % block_count
    globals_ = jnp.broadcast_to(universal_segment_indices[None], (group, WORLDWIDE_COUNT))
    listed = jnp.concatenate(
        [jnp.stack([ids - 1, ids, ids + 1], 1), random_group, globals_], 1
    )
    kept = list_masks(listed, block_total)
    is_global = jnp.any(ids[:, None] == universal_segment_indices[None], 1)
    border = jnp.where(local == 0, ids - 1, jnp.where(local == block_count - 1, ids + 1, -1))
    named = jnp.concatenate([border[:, None], random_group], 1)
    valid = jnp.concatenate(
        [((border >= 0) & (border < block_total))[:, None], kept[:, 3 : 3 + RANDOM]], 1
    )
    lane = named // block_count % y_count
    valid = valid & jnp.logical_not(is_global)[:, None] & (lane == y_place)
    cell = named // group * block_count + named % block_count
    valid = valid.T.reshape(-1)
    cell = cell.T.reshape(-1)
    entries = SLOTS * group
    order = jnp.arange(entries, dtype=jnp.int32)
    label = cell * entries + order
    rank = jnp.sum((valid[None, :] & (label[None, :] < label[:, None])).astype(jnp.int32), 1)
    edge_count = jnp.sum(valid.astype(jnp.int32))
    hit = (rank[None, :] == order[:, None]) & valid[None, :]
    slot_list = jnp.sum(jnp.where(hit, order[None, :], 0), 1)
    cell_list = jnp.sum(jnp.where(hit, cell[None, :], 0), 1)
    real = order < edge_count
    fresh = real & ((order == 0) | (cell_list != jnp.roll(cell_list, 1)))
    last_list = real & ((order == edge_count - 1) | (cell_list != jnp.roll(cell_list, -1)))
    order_list = jnp.sum((fresh[None, :] & (order[None, :] <= order[:, None])).astype(jnp.int32), 1) - 1
    slot_list = jnp.where(real, slot_list, entries + group)
    item_list = slot_list % group
    item_list = (y_place - item_list // block_count) % y_count * block_count + item_list % block_count
    row_list = jnp.where(real, slot_list % group, group)
    grad_lists = (
        row_list,
        order_list % STAGES,
        fresh.astype(jnp.int32),
        last_list.astype(jnp.int32),
        (fresh & (order_list >= STAGES)).astype(jnp.int32),
    )
    meta = jnp.stack(
        [(edge_count + UNROLL - 1) // UNROLL, y_place, jnp.sum(fresh.astype(jnp.int32))]
    ).astype(jnp.int32)
    lists = (meta, slot_list, item_list, cell_list)

    own_first = y_place * block_count
    own_kept = lax.dynamic_slice_in_dim(kept, own_first, block_count, 0)
    bias = jnp.where(own_kept[:, 3 + RANDOM :], 0.0, NEG).astype(f32).reshape(-1)
    own_ids = ctx_place * block_count + jnp.arange(block_count, dtype=jnp.int32)
    hits = own_ids[:, None] == universal_segment_indices[None]
    flags = jnp.where(jnp.any(hits, 1), 0.0, 1.0).astype(f32)

    own, rows = pl.pallas_call(
        own_stats_kernel,
        out_shape=(
            jax.ShapeDtypeStruct((3, block_count, S), f32),
            jax.ShapeDtypeStruct((3, G), f32),
        ),
        in_specs=[SMEM, VMEM, VMEM, VMEM],
        out_specs=(VMEM, VMEM),
        compiler_params=PARAMS,
        name="own_stats",
    )(bias, qd, kv, shared)

    stat_rows = (SLOTS + 1) * group + 8
    own, grad_lists = lax.optimization_barrier((own, grad_lists))
    fetch_scratch = [
        pltpu.VMEM((DEPTH, UNROLL * S, 2 * D), jnp.bfloat16),
        pltpu.SemaphoreType.DMA((DEPTH,)),
    ]
    stats = pl.pallas_call(
        edge_stats_kernel,
        out_shape=jax.ShapeDtypeStruct((y_count, 2 * group, 2 * S), f32),
        in_specs=[SMEM] * 4 + [VMEM, ANY, VMEM],
        out_specs=VMEM,
        scratch_shapes=[pltpu.VMEM((stat_rows, 2 * S), f32)] * 3 + fetch_scratch,
        compiler_params=PARAMS,
        name="edge_stats",
    )(*lists, qd_group, kv_all, own)
    parts = exchange(stats, Y_AXIS)

    table, final, edge_mixed, *halves = pl.pallas_call(
        edge_grads_kernel,
        out_shape=(
            jax.ShapeDtypeStruct((cells * S, 2 * D), jnp.bfloat16),
            jax.ShapeDtypeStruct((3, group + 8, 2 * S), f32),
            jax.ShapeDtypeStruct((tokens, 2 * D), f32),
        )
        + (jax.ShapeDtypeStruct((tokens, 2 * D), jnp.bfloat16),) * (y_count - 1),
        in_specs=[SMEM] * 8 + [VMEM, ANY, VMEM, ANY],
        out_specs=(ANY,) + (VMEM,) * (y_count + 1),
        scratch_shapes=[
            pltpu.VMEM((group * S, 2 * D), f32),
            pltpu.VMEM((S, 2 * D), f32),
            pltpu.VMEM((STAGES, S, 2 * D), jnp.bfloat16),
        ]
        + fetch_scratch
        + [pltpu.SemaphoreType.DMA((STAGES,))],
        input_output_aliases={11: 0},
        compiler_params=PARAMS,
        name="edge_grads",
    )(meta, grad_lists[0], item_list, cell_list, *grad_lists[1:], qd_group, kv_all, parts, cleared)
    returned = lax.psum_scatter(table, Z_AXIS, scatter_dimension=0, tiled=True)
    halves = [lax.ppermute(half, Y_AXIS, pairs) for half, pairs in zip(halves, backward)]
    rows_all = to_all(to_all(rows, Z_AXIS), Y_AXIS).reshape(ctx_count, 3, G)

    pairs, mixed, shared_grads = pl.pallas_call(
        own_grads_kernel,
        out_shape=(
            jax.ShapeDtypeStruct((tokens, 2 * D), f32),
            jax.ShapeDtypeStruct((tokens, 2 * D), f32),
            jax.ShapeDtypeStruct((2 * G, 2 * D), f32),
        ),
        in_specs=[SMEM] * 3 + [VMEM] * 6,
        out_specs=(VMEM, VMEM, VMEM),
        compiler_params=PARAMS,
        name="own_grads",
    )(meta, bias, flags, qd, kv, shared, final, rows_all, edge_mixed)

    summed = shared_grads.astype(jnp.bfloat16)
    for axis in (Y_AXIS, Z_AXIS):
        count = lax.axis_size(axis)
        summed = exchange(summed.reshape(count, -1, 2 * D), axis)
        summed = jnp.sum(summed.astype(f32), 0).astype(jnp.bfloat16)
    for axis in (Z_AXIS, Y_AXIS):
        summed = to_all(summed, axis).reshape(-1, 2 * D)
    shared_sums = summed.reshape(2, WORLDWIDE_COUNT, 1, S, 2 * D).astype(f32)

    mixed = sum([half.astype(f32) for half in halves], mixed).reshape(block_count, S, 2 * D)
    for g in range(WORLDWIDE_COUNT):
        mask = hits[:, g][:, None, None]
        mixed = jnp.where(mask, shared_sums[1, g], mixed)
    mixed = mixed.reshape(tokens, 2 * D).astype(jnp.bfloat16)
    pairs = pairs.reshape(block_count, S, 2 * D)
    for g in range(WORLDWIDE_COUNT):
        pairs = pairs + jnp.where(hits[:, g][:, None, None], shared_sums[0, g], 0.0)
    pairs = lax.optimization_barrier((pairs.reshape(tokens, 2 * D), mixed))[0]
    grads = [
        (returned[:, half].astype(f32) + pairs[:, half]).astype(jnp.bfloat16)
        for half in (slice(0, D), slice(D, 2 * D))
    ]
    return mixed[:, :D], mixed[:, D:], grads[0], grads[1]


def solution(mesh):
    torus = Mesh(mesh.devices.reshape(16, 4, mesh.shape["head"]), ("ctx_0", "ctx_1", "head"))
    return on_torus(torus)


def on_torus(torus):
    placed = (
        P(CTX_HEAD, None),
        P(CTX_HEAD, None),
        P(CTX_HEAD, None),
        P(CTX_HEAD, None),
        P(CTX, "head", None),
        P(),
    )
    return jax.shard_map(
        body,
        mesh=torus,
        in_specs=placed,
        out_specs=(P(CTX, "head"), P(CTX, "head"), P(CTX, "head"), P(CTX, "head")),
        check_vma=False,
    )
```
